128 devices in a mesh: seq: 32 (over z, y, core), head: 4 (over x).
Axes of the slice: x: 4, y: 4, z: 4, core: 2. Of those that a mesh axis runs over, the one named last changes fastest.
Arguments:
- tokens: bfloat16 [65536, 1024], P(('seq', 'head')), may hold values from -6 to 6
- w_gate_x: bfloat16 [1024, 4096], replicated, may hold values from -0.1875 to 0.1875
- w_bc_dt: bfloat16 [1024, 160], replicated, may hold values from -0.1875 to 0.1875
- conv_x_weight: float32 [4, 2048], P(None, 'head'), may hold values from -0.5 to 0.5
- conv_x_bias: float32 [2048], P('head'), may hold values from -0.5 to 0.5
- conv_bc_weight: float32 [4, 128], replicated, may hold values from -0.5 to 0.5
- conv_bc_bias: float32 [128], replicated, may hold values from -0.5 to 0.5
- dt_bias: float32 [32], P('head'), may hold values from -9 to -1
- a_log: float32 [32], P('head'), may hold values from -4 to 1
- skip_d: float32 [32], P('head'), may hold values from 0.5 to 1.5
- norm_gain: float32 [2048], replicated, may hold values from 0.1 to 1.9
- w_out: bfloat16 [2048, 1024], replicated, may hold values from -0.125 to 0.125
Outputs:
- mixed: bfloat16 [65536, 1024], P(('seq', 'head'))
The draws below stay inside these ranges and needn't reach their ends.
All inputs are finite; a program needn't handle non-finite values.
Results may differ from the reference program's by a relative error of at most 0.009.
Values may be sent and summed in bfloat16 or wider, within the bound.
No kernel may reach another device: no remote copies, remote signals or barrier semaphores. Data moves between devices by JAX's collectives and lax.ppermute only.
A program may use at most 128 MiB of HBM per device.

```python
import jax
import jax.numpy as jnp
from jax import lax

D = 1024
HEADS = 32
HEAD_DIM = 64
STATE = 64
GROUP = 256
CONV = 4
DINNER = 2048
TOKENS = 65536


def level_of(stream_key, extent, cuts, low, largest):
    gain = 1.0
    for position, shards_of in cuts:
        steps = jax.random.uniform(jax.random.fold_in(jax.random.fold_in(stream_key, 6), position), (shards_of,), jnp.float32, low / len(cuts), largest / len(cuts))
        gain = gain * jnp.repeat(jnp.exp(steps), extent[position] // shards_of).reshape((-1,) + (1,) * (len(extent) - 1 - position))
    return gain


def normal_values(own_key, shape, width, bound, pieces=(), dtype=jnp.bfloat16):
    level = level_of(own_key, shape, pieces, -0.22, 0.18) if pieces else 1.0
    result = jax.random.normal(own_key, shape, jnp.float32) * width * level
    return jnp.minimum(jnp.maximum(result, -bound), bound).astype(dtype)


def setup_inputs(seed: int = 0) -> dict:
    key_of = jax.random.split(jax.random.key(seed), 13)
    tokens = normal_values(key_of[0], (TOKENS, D), 1.0, 6.0, ((0, 128),))
    w_gate_x = normal_values(key_of[1], (D, 2 * DINNER), D ** -0.5, 0.1875)
    w_bc_dt = normal_values(key_of[2], (D, 2 * STATE + HEADS), D ** -0.5, 0.1875)
    conv_x_weight = jnp.clip(jax.random.uniform(key_of[3], (CONV, DINNER), jnp.float32, -0.5, 0.5) * level_of(key_of[3], (CONV, DINNER), ((1, 4),), -0.4, 0.0), -0.5, 0.5)
    conv_x_bias = jnp.clip(jax.random.uniform(key_of[4], (DINNER,), jnp.float32, -0.5, 0.5) * level_of(key_of[4], (DINNER,), ((0, 4),), -0.4, 0.0), -0.5, 0.5)
    conv_bc_weight = jnp.clip(jax.random.uniform(key_of[5], (CONV, 2 * STATE), jnp.float32, -0.5, 0.5), -0.5, 0.5)
    conv_bc_bias = jnp.clip(jax.random.uniform(key_of[6], (2 * STATE,), jnp.float32, -0.5, 0.5), -0.5, 0.5)
    dt_bias = jnp.clip(-9.0 + 8.0 * jax.random.uniform(key_of[7], (HEADS,), jnp.float32) ** level_of(key_of[7], (HEADS,), ((0, 4),), -0.2, 0.2), -9.0, -1.0)
    a_log = jnp.clip(-4.0 + 5.0 * jax.random.uniform(key_of[8], (HEADS,), jnp.float32) ** level_of(key_of[8], (HEADS,), ((0, 4),), -0.2, 0.2), -4.0, 1.0)
    skip_d = jnp.clip(0.5 + 1.0 * jax.random.uniform(key_of[9], (HEADS,), jnp.float32) ** level_of(key_of[9], (HEADS,), ((0, 4),), -0.2, 0.2), 0.5, 1.5)
    norm_gain = jnp.clip(1.0 + 0.18 * jax.random.normal(key_of[10], (DINNER,), jnp.float32), 0.1, 1.9)
    w_out = normal_values(key_of[11], (DINNER, D), DINNER ** -0.5, 0.125)
    return dict(tokens=tokens, w_gate_x=w_gate_x, w_bc_dt=w_bc_dt, conv_x_weight=conv_x_weight, conv_x_bias=conv_x_bias, conv_bc_weight=conv_bc_weight, conv_bc_bias=conv_bc_bias, dt_bias=dt_bias, a_log=a_log, skip_d=skip_d, norm_gain=norm_gain, w_out=w_out)


epsilon = 1e-05

def causal_taps(source, weights, biases):
    count = source.shape[0]
    padded = jnp.pad(source.astype(jnp.float32), ((CONV - 1, 0), (0, 0)))
    summed = biases + weights[0] * padded[0:count]
    for tap_index in range(1, CONV):
        summed = summed + weights[tap_index] * padded[tap_index:tap_index + count]
    return jax.nn.silu(summed).astype(jnp.bfloat16)

def reference(tokens, w_gate_x, w_bc_dt, conv_x_weight, conv_x_bias, conv_bc_weight, conv_bc_bias, dt_bias, a_log, skip_d, norm_gain, w_out):
    highest = lax.Precision.HIGHEST
    gate_x = jnp.dot(tokens, w_gate_x, preferred_element_type=jnp.float32).astype(jnp.bfloat16)
    gate_x = gate_x.reshape(TOKENS, HEADS, 2 * HEAD_DIM)
    bc_dt = jnp.dot(tokens, w_bc_dt, preferred_element_type=jnp.float32).astype(jnp.bfloat16)
    gate_z = gate_x[:, :, :HEAD_DIM]
    x_chan = gate_x[:, :, HEAD_DIM:].reshape(TOKENS, DINNER)
    conved_x = causal_taps(x_chan, conv_x_weight, conv_x_bias)
    conved_bc = causal_taps(bc_dt[:, :2 * STATE], conv_bc_weight, conv_bc_bias)
    dt_step = jax.nn.softplus(bc_dt[:, 2 * STATE:].astype(jnp.float32) + dt_bias)
    log_decay = dt_step * -jnp.exp(a_log)
    x_heads = conved_x.astype(jnp.float32).reshape(TOKENS, HEADS, HEAD_DIM)
    x_dt = x_heads * dt_step[:, :, None]
    b_mat = conved_bc[:, :STATE].astype(jnp.float32)
    c_mat = conved_bc[:, STATE:].astype(jnp.float32)
    blocks = TOKENS // GROUP
    causal = jnp.arange(GROUP)[:, None] >= jnp.arange(GROUP)[None, :]

    def group_step(carried, inputs):
        decay_c, xdt_c, b_c, c_c = inputs
        cumlog = jnp.cumsum(decay_c, axis=0)
        scores = jnp.dot(c_c, b_c.T, precision=highest)
        by_head = cumlog.T
        gaps = by_head[:, :, None] - by_head[:, None, :]
        decays = jnp.where(causal[None], jnp.exp(jnp.minimum(gaps, 0.0)), 0.0)
        mixed = scores[None] * decays
        outputs = jnp.einsum('hts,shp->thp', mixed, xdt_c, precision=highest)
        outputs = outputs + jnp.exp(cumlog)[:, :, None] * jnp.einsum('tn,hpn->thp', c_c, carried, precision=highest)
        to_end = jnp.exp(cumlog[-1][None, :] - cumlog)
        weighted = to_end[:, :, None] * xdt_c
        fresh = jnp.einsum('shp,sn->hpn', weighted, b_c, precision=highest)
        updated = jnp.exp(cumlog[-1])[:, None, None] * carried + fresh
        return (updated, outputs)
    initial = jnp.zeros((HEADS, HEAD_DIM, STATE), jnp.float32)
    inputs = (log_decay.reshape(blocks, GROUP, HEADS), x_dt.reshape(blocks, GROUP, HEADS, HEAD_DIM), b_mat.reshape(blocks, GROUP, STATE), c_mat.reshape(blocks, GROUP, STATE))
    final_state, outputs = lax.scan(group_step, initial, inputs)
    y_heads = outputs.reshape(TOKENS, HEADS, HEAD_DIM) + skip_d[None, :, None] * x_heads
    gated = (y_heads * jax.nn.silu(gate_z.astype(jnp.float32))).astype(jnp.bfloat16).reshape(TOKENS, DINNER)
    gated_f = gated.astype(jnp.float32)
    mean_sq = lax.optimization_barrier(jnp.mean(gated_f * gated_f, axis=1, keepdims=True))
    normed = (gated_f * lax.rsqrt(mean_sq + epsilon) * norm_gain).astype(jnp.bfloat16)
    return jnp.dot(normed, w_out, preferred_element_type=jnp.float32).astype(jnp.bfloat16)
```

```python
import functools

import jax
import jax.numpy as jnp
from jax import lax
from jax.experimental import pallas as pl
from jax.experimental.pallas import tpu as pltpu
from jax.sharding import PartitionSpec as P

HEADS = 32
HEAD_DIM = 64
STATE = 64
CONV = 4
DINNER = HEADS * HEAD_DIM
BC = 2 * STATE
SUB = 128
EPSILON = 1e-05
BOTH = ("seq", "head")
F32 = jnp.float32
BF16 = jnp.bfloat16
LIMIT = 56 * 1024 * 1024


def params(steps=1):
    return pltpu.CompilerParams(
        dimension_semantics=("arbitrary",) * steps, vmem_limit_bytes=LIMIT
    )


def silu(v):
    half = 0.5 * v
    return half + half * jnp.tanh(half)


def hi_lo(v, axis):
    hi = v.astype(BF16)
    lo = (v - hi.astype(F32)).astype(BF16)
    return jnp.concatenate([hi, lo], axis=axis)


def dot(a, b):
    return jnp.dot(a, b, preferred_element_type=F32)


def one_hot(first_channel, width):
    row = lax.broadcasted_iota(jnp.int32, (2 * HEADS, width), 0)
    chan = lax.broadcasted_iota(jnp.int32, (2 * HEADS, width), 1) + first_channel
    return ((row % HEADS) == (chan // HEAD_DIM)).astype(F32).astype(BF16)


def project_kernel(tok_ref, w_ref, wbc_ref, x_ref, z_ref, tail_ref, bc_ref, dt_ref):
    j = pl.program_id(0)
    width = x_ref.shape[1]
    rows = tok_ref.shape[0]

    @pl.when(j == 0)
    def _():
        small = dot(tok_ref[...], wbc_ref[...])
        bc = small[:, :BC]
        bc_ref[...] = bc.astype(BF16)
        dt_ref[...] = small[:, BC:].astype(BF16).astype(F32)
        tail_ref[:, DINNER:] = bc[rows - 8 :].astype(BF16)

    full = dot(tok_ref[...], w_ref[...])
    lane = lax.broadcasted_iota(jnp.int32, (1, 128), 1) < HEAD_DIM
    for pair in range(width // 128):
        a = full[:, pair * 256 : pair * 256 + 128]
        b = full[:, pair * 256 + 128 : pair * 256 + 256]
        cols = slice(pair * 128, pair * 128 + 128)
        z_ref[:, cols] = jnp.where(lane, a, pltpu.roll(b, HEAD_DIM, 1)).astype(BF16)
        x = jnp.where(lane, pltpu.roll(a, HEAD_DIM, 1), b).astype(BF16)
        x_ref[:, cols] = x
        start = pl.multiple_of(j * width + pair * 128, 128)
        tail_ref[:, pl.ds(start, 128)] = x[rows - 8 :]


def project(tokens, w_gate_x, w_bc_dt):
    rows, depth = tokens.shape
    width = 256
    return pl.pallas_call(
        project_kernel,
        grid=(DINNER // width,),
        in_specs=[
            pl.BlockSpec((rows, depth), lambda j: (0, 0)),
            pl.BlockSpec((depth, 2 * width), lambda j: (0, j)),
            pl.BlockSpec(w_bc_dt.shape, lambda j: (0, 0)),
        ],
        out_specs=[
            pl.BlockSpec((rows, width), lambda j: (0, j)),
            pl.BlockSpec((rows, width), lambda j: (0, j)),
            pl.BlockSpec((8, DINNER + BC), lambda j: (0, 0)),
            pl.BlockSpec((rows, BC), lambda j: (0, 0)),
            pl.BlockSpec((rows, HEADS), lambda j: (0, 0)),
        ],
        out_shape=[
            jax.ShapeDtypeStruct((rows, DINNER), BF16),
            jax.ShapeDtypeStruct((rows, DINNER), BF16),
            jax.ShapeDtypeStruct((8, DINNER + BC), BF16),
            jax.ShapeDtypeStruct((rows, BC), BF16),
            jax.ShapeDtypeStruct((rows, HEADS), F32),
        ],
        compiler_params=params(),
        name="project",
    )(tokens, w_gate_x, w_bc_dt)


def taps(buf_ref, start, count, weights, bias):
    summed = bias
    for k in range(CONV):
        summed = summed + weights[k : k + 1] * buf_ref[pl.ds(start + 5 + k, count), :]
    return silu(summed)


def state_kernel(
    x_ref, halo_ref, bc_ref, dtraw_ref, par_ref, parall_ref, wbc_ref, bbc_ref,
    xc_ref, bcout_ref, dt_ref, cum_ref, slab_ref,
    buf, bcbuf, wgt, bt,
):
    g = pl.program_id(0)
    rows, width = x_ref.shape

    @pl.when(g == 0)
    def _():
        dt_bias = jnp.sum(parall_ref[:, 6, :HEADS], axis=0, keepdims=True)
        a_log = jnp.sum(parall_ref[:, 7, :HEADS], axis=0, keepdims=True)
        raw = dtraw_ref[...] + dt_bias
        step = jnp.maximum(raw, 0.0) + jnp.log1p(jnp.exp(-jnp.abs(raw)))
        decay = step * -jnp.exp(a_log)
        r = lax.broadcasted_iota(jnp.int32, (SUB, SUB), 0)
        c = lax.broadcasted_iota(jnp.int32, (SUB, SUB), 1)
        ones = (r >= c).astype(F32)
        before = jnp.zeros((1, HEADS), F32)
        parts = []
        for k in range(rows // SUB):
            part = before + jnp.dot(
                ones, decay[k * SUB : (k + 1) * SUB],
                precision=lax.Precision.HIGHEST, preferred_element_type=F32,
            )
            before = part[SUB - 1 : SUB]
            parts.append(part)
        cum = jnp.concatenate(parts, axis=0)
        dt_ref[...] = step
        cum_ref[...] = cum
        wgt[0:rows] = hi_lo(step * jnp.exp(before - cum), 1)
        total = hi_lo(jnp.exp(before), 1)
        zero = jnp.zeros((1, HEADS), BF16)
        wgt[rows : rows + 8] = jnp.concatenate(
            [
                jnp.concatenate([total[:, :HEADS], zero], axis=1),
                jnp.concatenate([zero, total[:, HEADS:]], axis=1),
                jnp.zeros((6, 2 * HEADS), BF16),
            ],
            axis=0,
        )
        bcbuf[0:8] = halo_ref[:, DINNER:].astype(F32)
        bcbuf[8 : 8 + rows] = bc_ref[...].astype(F32)
        conved = taps(bcbuf, 0, rows, wbc_ref[...], bbc_ref[...])
        bcout_ref[...] = conved.astype(BF16)
        bt[...] = conved.T[:STATE].astype(BF16)

    start = pl.multiple_of(g * width, width)
    buf[0:8] = halo_ref[:, pl.ds(start, width)].astype(F32)
    buf[8 : 8 + rows] = x_ref[...].astype(F32)
    spread = dot(wgt[...], one_hot(g * width, width))
    state = jnp.zeros((STATE, width), F32)
    for k in range(rows // SUB):
        here = slice(k * SUB, (k + 1) * SUB)
        xc = taps(buf, k * SUB, SUB, par_ref[0, 0:4], par_ref[0, 4:5]).astype(BF16)
        xc_ref[here] = xc
        weighted = (xc.astype(F32) * spread[here]).astype(BF16)
        state = state + dot(bt[:, here], weighted)
    extra = spread[rows : rows + 8]
    for c in range(width // 128):
        cols = slice(c * 128, c * 128 + 128)
        for r in range(STATE // 8):
            slab_ref[r, c, 0:8] = state[r * 8 : r * 8 + 8, cols].astype(BF16)
            slab_ref[r, c, 8:16] = extra[:, cols].astype(BF16)


def local_state(x, halo, bc, dt_raw, packed, conv_bc_weight, conv_bc_bias):
    rows = x.shape[0]
    width = 256
    per = packed.shape[2] // width

    def whole(a):
        return pl.BlockSpec(a.shape, lambda g: (0,) * a.ndim)

    return pl.pallas_call(
        state_kernel,
        grid=(DINNER // width,),
        in_specs=[
            pl.BlockSpec((rows, width), lambda g: (0, g)),
            whole(halo),
            whole(bc),
            whole(dt_raw),
            pl.BlockSpec((1, 8, width), lambda g: (g // per, 0, g % per)),
            whole(packed),
            whole(conv_bc_weight),
            whole(conv_bc_bias),
        ],
        out_specs=[
            pl.BlockSpec((rows, width), lambda g: (0, g)),
            pl.BlockSpec((rows, BC), lambda g: (0, 0)),
            pl.BlockSpec((rows, HEADS), lambda g: (0, 0)),
            pl.BlockSpec((rows, HEADS), lambda g: (0, 0)),
            pl.BlockSpec((STATE // 8, width // 128, 16, 128), lambda g: (0, g, 0, 0)),
        ],
        out_shape=[
            jax.ShapeDtypeStruct((rows, DINNER), BF16),
            jax.ShapeDtypeStruct((rows, BC), BF16),
            jax.ShapeDtypeStruct((rows, HEADS), F32),
            jax.ShapeDtypeStruct((rows, HEADS), F32),
            jax.ShapeDtypeStruct((STATE // 8, DINNER // 128, 16, 128), BF16),
        ],
        scratch_shapes=[
            pltpu.VMEM((rows + 8, width), F32),
            pltpu.VMEM((rows + 8, BC), F32),
            pltpu.VMEM((rows + 8, 2 * HEADS), BF16),
            pltpu.VMEM((STATE, rows), BF16),
        ],
        compiler_params=params(),
        name="local_state",
    )(x, halo, bc, dt_raw, packed, packed, conv_bc_weight, conv_bc_bias)


def intra_kernel(
    base, xc_ref, z_ref, bc_ref, dt_ref, cum_ref, par_ref,
    own_ref, scale_ref,
    scores, rowlog, bt, wgt,
):
    g = pl.program_id(0)
    rows, width = xc_ref.shape
    blocks = rows // SUB
    heads = width // HEAD_DIM

    @pl.when(g == 0)
    def _():
        bt[...] = bc_ref[...].astype(F32).T[:STATE].astype(BF16)
        for k in range(blocks):
            here = slice(k * SUB, (k + 1) * SUB)
            scores[here] = dot(bc_ref[here, STATE:], bt[:, here])
        cum = cum_ref[...]
        step = dt_ref[...]
        by_row = (cum - jnp.log(step)).T
        for group in range(HEADS // heads):
            rowlog[group, 0:heads] = by_row[group * heads : (group + 1) * heads]
        starts, ends = [], []
        before = jnp.zeros((1, HEADS), F32)
        for k in range(blocks):
            here = slice(k * SUB, (k + 1) * SUB)
            starts.append(jnp.broadcast_to(before, (SUB, HEADS)))
            before = cum[(k + 1) * SUB - 1 : (k + 1) * SUB]
            ends.append(jnp.broadcast_to(before, (SUB, HEADS)))
        starts = jnp.concatenate(starts, axis=0)
        ends = jnp.concatenate(ends, axis=0)
        wgt[0:rows] = hi_lo(step * jnp.exp(ends - cum), 1)
        wgt[rows : 2 * rows] = hi_lo(jnp.exp(cum - starts), 1)
        wgt[2 * rows : 3 * rows] = hi_lo(jnp.exp(cum), 1)

    first = base + g * width
    spread = one_hot(first, width)
    first_head = (base // width + g) * heads
    r = lax.broadcasted_iota(jnp.int32, (SUB, SUB), 0)
    c = lax.broadcasted_iota(jnp.int32, (SUB, SUB), 1)
    causal = r >= c
    lane = lax.broadcasted_iota(jnp.int32, (1, HEADS), 1)
    skip = par_ref[0, 5:6]
    state = jnp.zeros((STATE, width), F32)
    for k in range(blocks):
        here = slice(k * SUB, (k + 1) * SUB)
        xc = xc_ref[here]
        pieces = []
        for h in range(heads):
            head = first_head + h
            col = jnp.sum(
                jnp.where(lane == head, cum_ref[here], 0.0), axis=1, keepdims=True
            )
            row = rowlog[base // width + g, h : h + 1, here]
            decay = jnp.exp(jnp.where(causal, col - row, -jnp.inf))
            mixed = (scores[here] * decay).astype(BF16)
            pieces.append(dot(mixed, xc[:, h * HEAD_DIM : (h + 1) * HEAD_DIM]))
        y = jnp.concatenate(pieces, axis=1)
        xf = xc.astype(F32)
        grow = dot(wgt[rows + k * SUB : rows + (k + 1) * SUB], spread)
        if k > 0:
            y = y + grow * dot(bc_ref[here, STATE:], state.astype(BF16))
        if k + 1 < blocks:
            shrink = dot(wgt[here], spread)
            fresh = dot(bt[:, here], (xf * shrink).astype(BF16))
            state = state * grow[SUB - 1 : SUB] + fresh
        gate = silu(z_ref[here].astype(F32))
        own_ref[here] = (y + skip * xf) * gate
        full = dot(wgt[2 * rows + k * SUB : 2 * rows + (k + 1) * SUB], spread)
        scale_ref[here] = (full * gate).astype(BF16)


def intra(half, halves, xc, z, bc, dt, cum, packed):
    rows = xc.shape[0]
    width = 256
    span = DINNER // halves
    steps = span // width
    per = packed.shape[2] // width

    def whole(a):
        return pl.BlockSpec(a.shape, lambda g: (0,) * a.ndim)

    return pl.pallas_call(
        functools.partial(intra_kernel, half * span),
        grid=(steps,),
        in_specs=[
            pl.BlockSpec((rows, width), lambda g: (0, g + half * steps)),
            pl.BlockSpec((rows, width), lambda g: (0, g + half * steps)),
            whole(bc),
            whole(dt),
            whole(cum),
            pl.BlockSpec(
                (1, 8, width),
                lambda g: ((g + half * steps) // per, 0, (g + half * steps) % per),
            ),
        ],
        out_specs=[
            pl.BlockSpec((rows, width), lambda g: (0, g)),
            pl.BlockSpec((rows, width), lambda g: (0, g)),
        ],
        out_shape=[
            jax.ShapeDtypeStruct((rows, span), F32),
            jax.ShapeDtypeStruct((rows, span), BF16),
        ],
        scratch_shapes=[
            pltpu.VMEM((rows, SUB), F32),
            pltpu.VMEM((DINNER // width, 8, rows), F32),
            pltpu.VMEM((STATE, rows), BF16),
            pltpu.VMEM((3 * rows, 2 * HEADS), BF16),
        ],
        compiler_params=params(),
        name="intra",
    )(xc, z, bc, dt, cum, packed)


def scan_kernel(in_ref, out_ref):
    count = in_ref.shape[0]
    state = jnp.zeros((8, 128), F32)
    for q in range(count):
        out_ref[q] = state.astype(BF16)
        slab = in_ref[q].astype(F32)
        state = state * (slab[8:9] + slab[9:10]) + slab[0:8]


def scan_devices(slabs):
    count = slabs.shape[0]
    return pl.pallas_call(
        scan_kernel,
        out_shape=jax.ShapeDtypeStruct((count, 8, 128), BF16),
        compiler_params=params(0),
        name="scan_devices",
    )(slabs)


def finish_kernel(c_ref, slab_ref, own0, own1, scale0, scale1, gain_ref, w_ref,
                  out_ref, acc, squares):
    g = pl.program_id(0)
    last = pl.num_programs(0) - 1
    half = pl.num_programs(0) // 2
    columns = slab_ref.shape[1]
    slabs = [
        slab_ref[:, c].astype(F32).reshape(STATE, 128).astype(BF16)
        for c in range(columns)
    ]
    carried = dot(c_ref[:, STATE:], jnp.concatenate(slabs, axis=1))

    def step(own_ref, scale_ref):
        gated = (own_ref[...] + scale_ref[...].astype(F32) * carried).astype(BF16)
        gated = gated.astype(F32)
        part = jnp.sum(gated * gated, axis=1, keepdims=True)
        product = dot((gated * gain_ref[...]).astype(BF16), w_ref[...])

        @pl.when(g == 0)
        def _():
            acc[...] = product
            squares[...] = part

        @pl.when(g > 0)
        def _():
            acc[...] += product
            squares[...] += part

    @pl.when(g < half)
    def _():
        step(own0, scale0)

    @pl.when(g >= half)
    def _():
        step(own1, scale1)

    @pl.when(g == last)
    def _():
        scale = lax.rsqrt(squares[...] * (1.0 / DINNER) + EPSILON)
        out_ref[...] = (acc[...] * scale).astype(BF16)


def finish(bc, slabs, owns, scales, norm_gain, w_out):
    rows = bc.shape[0]
    width = 512
    steps = DINNER // width
    half = steps // 2
    columns = w_out.shape[1]

    def first(g):
        return (0, jnp.minimum(g, half - 1))

    def second(g):
        return (0, jnp.maximum(g - half, 0))

    return pl.pallas_call(
        finish_kernel,
        grid=(steps,),
        in_specs=[
            pl.BlockSpec(bc.shape, lambda g: (0, 0)),
            pl.BlockSpec((STATE // 8, width // 128, 8, 128), lambda g: (0, g, 0, 0)),
            pl.BlockSpec((rows, width), first),
            pl.BlockSpec((rows, width), second),
            pl.BlockSpec((rows, width), first),
            pl.BlockSpec((rows, width), second),
            pl.BlockSpec((1, width), lambda g: (0, g)),
            pl.BlockSpec((width, columns), lambda g: (g, 0)),
        ],
        out_specs=pl.BlockSpec((rows, columns), lambda g: (0, 0)),
        out_shape=jax.ShapeDtypeStruct((rows, columns), BF16),
        scratch_shapes=[pltpu.VMEM((rows, columns), F32), pltpu.VMEM((rows, 1), F32)],
        compiler_params=params(),
        name="finish",
    )(bc, slabs, owns[0], owns[1], scales[0], scales[1], norm_gain, w_out)


def gather_params(conv_x_weight, conv_x_bias, dt_bias, a_log, skip_d):
    n = lax.axis_size("head")
    me = lax.axis_index("head")
    wide = conv_x_bias.shape[0]
    here = dt_bias.shape[0]
    mine = (jnp.arange(wide) // here) == me
    packed = jnp.concatenate(
        [
            conv_x_weight,
            conv_x_bias[None],
            jnp.repeat(skip_d, HEAD_DIM)[None],
            jnp.where(mine, jnp.tile(dt_bias, wide // here), 0.0)[None],
            jnp.where(mine, jnp.tile(a_log, wide // here), 0.0)[None],
        ],
        axis=0,
    )
    ring = [packed]
    for k in range(1, n):
        pairs = [(i, (i - k) % n) for i in range(n)]
        ring.append(lax.ppermute(packed, "head", pairs))
    twice = jnp.stack(ring + ring[: n - 1])
    return lax.dynamic_slice_in_dim(twice, (n - me) % n, n, axis=0)


def on_device(
    tokens, w_gate_x, w_bc_dt, conv_x_weight, conv_x_bias, conv_bc_weight,
    conv_bc_bias, dt_bias, a_log, skip_d, norm_gain, w_out,
):
    devices = lax.axis_size("seq") * lax.axis_size("head")
    packed = gather_params(conv_x_weight, conv_x_bias, dt_bias, a_log, skip_d)
    x, z, tail, bc_raw, dt_raw = project(tokens, w_gate_x, w_bc_dt)
    halo = lax.ppermute(tail, BOTH, [(i, i + 1) for i in range(devices - 1)])
    xc, bc, dt, cum, slabs = local_state(
        x, halo, bc_raw, dt_raw, packed, conv_bc_weight, conv_bc_bias[None]
    )
    slabs = slabs.reshape(devices, 16, 128)
    by_owner = lax.all_to_all(slabs, BOTH, 0, 0, tiled=True)
    own0, scale0 = intra(0, 2, xc, z, bc, dt, cum, packed)
    incoming = scan_devices(by_owner)
    back = lax.all_to_all(incoming, BOTH, 0, 0, tiled=True)
    xc, incoming = lax.optimization_barrier((xc, incoming))
    own1, scale1 = intra(1, 2, xc, z, bc, dt, cum, packed)
    back = back.reshape(STATE // 8, DINNER // 128, 8, 128)
    return finish(bc, back, (own0, own1), (scale0, scale1), norm_gain[None], w_out)


def solution(mesh):
    return jax.shard_map(
        on_device,
        mesh=mesh,
        in_specs=(
            P(BOTH, None),
            P(),
            P(),
            P(None, "head"),
            P("head"),
            P(),
            P(),
            P("head"),
            P("head"),
            P("head"),
            P(),
            P(),
        ),
        out_specs=P(BOTH, None),
        check_vma=False,
    )
```

```python
import functools

import jax
import jax.numpy as jnp
from jax import lax
from jax.experimental import pallas as pl
from jax.experimental.pallas import tpu as pltpu
from jax.sharding import PartitionSpec as P

HEADS = 32
HEAD_DIM = 64
STATE = 64
CONV = 4
DINNER = HEADS * HEAD_DIM
BC = 2 * STATE
SUB = 128
PAD = 16
EPSILON = 1e-05
BOTH = ("seq", "head")
F32 = jnp.float32
BF16 = jnp.bfloat16
LIMIT = 56 * 1024 * 1024


def params(steps=1):
    return pltpu.CompilerParams(
        dimension_semantics=("arbitrary",) * steps, vmem_limit_bytes=LIMIT
    )


def silu(v):
    half = 0.5 * v
    return half + half * jnp.tanh(half)


def hi_lo(v, axis):
    hi = v.astype(BF16)
    lo = (v - hi.astype(F32)).astype(BF16)
    return jnp.concatenate([hi, lo], axis=axis)


def dot(a, b):
    return jnp.dot(a, b, preferred_element_type=F32)


def one_hot(first_channel, width):
    row = lax.broadcasted_iota(jnp.int32, (2 * HEADS, width), 0)
    chan = lax.broadcasted_iota(jnp.int32, (2 * HEADS, width), 1) + first_channel
    return ((row % HEADS) == (chan // HEAD_DIM)).astype(F32).astype(BF16)


def pack_kernel(w_ref, b_ref, dt_ref, a_ref, skip_ref, tok_ref, out_ref, tail_ref):
    out_ref[...] = jnp.zeros_like(out_ref)
    out_ref[0:CONV] = w_ref[...]
    out_ref[CONV : CONV + 1] = b_ref[...]
    here = dt_ref.shape[1]
    for row, ref in ((5, dt_ref), (6, a_ref), (7, skip_ref)):
        out_ref[row : row + 1, 0:here] = ref[...]
    tail_ref[...] = tok_ref[...]


def pack(weight, bias, dt_bias, a_log, skip_d, tokens):
    rows, depth = tokens.shape
    small = (weight, bias[None], dt_bias[None], a_log[None], skip_d[None])

    def whole(a):
        return pl.BlockSpec(a.shape, lambda g: (0, 0))

    return pl.pallas_call(
        pack_kernel,
        grid=(1,),
        in_specs=[whole(a) for a in small]
        + [pl.BlockSpec((8, depth), lambda g: (rows // 8 - 1, 0))],
        out_specs=[
            pl.BlockSpec((8, weight.shape[1]), lambda g: (0, 0)),
            pl.BlockSpec((8, depth), lambda g: (0, 0)),
        ],
        out_shape=[
            jax.ShapeDtypeStruct((8, weight.shape[1]), F32),
            jax.ShapeDtypeStruct((8, depth), BF16),
        ],
        compiler_params=params(),
        name="pack",
    )(*small, tokens)


def half_lanes(w, which):
    parts = []
    for pair in range(w.shape[1] // 256):
        for k in range(2):
            at = pair * 256 + k * 128 + which * HEAD_DIM
            parts.append(w[:, at : at + HEAD_DIM])
    return jnp.concatenate(parts, axis=1)


def taps(buf_ref, start, count, weights, bias):
    summed = bias
    for k in range(CONV):
        at = start + PAD - CONV + 1 + k
        summed = summed + weights[k : k + 1] * buf_ref[pl.ds(at, count), :]
    return silu(summed)


def state_kernel(
    me_ref, tok_ref, halo_ref, w_ref, wsmall_ref, p0, p1, p2, p3, wbc_ref, bbc_ref,
    xc_ref, bcout_ref, dt_ref, cum_ref, skip_ref, slab_ref,
    tok, buf, bcbuf, wgt, bt, par,
):
    g = pl.program_id(0)
    rows = tok_ref.shape[0]
    width = xc_ref.shape[1]
    wide = p0.shape[1]
    blocks = par.shape[0]
    each = HEADS // blocks

    @pl.when(g == 0)
    def _():
        tok[0 : PAD - 8] = jnp.zeros((PAD - 8, tok.shape[1]), BF16)
        tok[PAD - 8 : PAD] = halo_ref[...]
        tok[PAD:] = tok_ref[...]
        for k, piece in enumerate((p0, p1, p2, p3)):
            owner = lax.rem(me_ref[0] + k, blocks)
            par[owner] = piece[...]
        lane = lax.broadcasted_iota(jnp.int32, (8, 128), 1)
        heads = jnp.zeros((8, 128), F32)
        for k in range(blocks):
            block = par[k, :, 0:128]
            moved = block if k == 0 else pltpu.roll(block, each * k, 1)
            heads = jnp.where(lane // each == k, moved, heads)
        heads = heads[:, :HEADS]
        small = lax.dot_general(
            tok[...], wsmall_ref[...], (((1,), (1,)), ((), ())),
            preferred_element_type=F32,
        )
        small = small.astype(BF16).astype(F32)
        raw = small[PAD:, BC:] + heads[5:6]
        step = jnp.maximum(raw, 0.0) + jnp.log1p(jnp.exp(-jnp.abs(raw)))
        decay = step * -jnp.exp(heads[6:7])
        r = lax.broadcasted_iota(jnp.int32, (SUB, SUB), 0)
        c = lax.broadcasted_iota(jnp.int32, (SUB, SUB), 1)
        ones = (r >= c).astype(F32)
        before = jnp.zeros((1, HEADS), F32)
        parts = []
        for k in range(rows // SUB):
            part = before + jnp.dot(
                ones, decay[k * SUB : (k + 1) * SUB],
                precision=lax.Precision.HIGHEST, preferred_element_type=F32,
            )
            before = part[SUB - 1 : SUB]
            parts.append(part)
        cum = jnp.concatenate(parts, axis=0)
        dt_ref[...] = step
        cum_ref[...] = cum
        wgt[0:rows] = hi_lo(step * jnp.exp(before - cum), 1)
        total = hi_lo(jnp.exp(before), 1)
        skips = hi_lo(heads[7:8], 1)
        zero = jnp.zeros((1, HEADS), BF16)
        wgt[rows : rows + 8] = jnp.concatenate(
            [
                jnp.concatenate([total[:, :HEADS], zero], axis=1),
                jnp.concatenate([zero, total[:, HEADS:]], axis=1),
                skips,
                jnp.zeros((5, 2 * HEADS), BF16),
            ],
            axis=0,
        )
        bcbuf[...] = small[:, :BC]
        conved = taps(bcbuf, 0, rows, wbc_ref[...], bbc_ref[...])
        bcout_ref[...] = conved.astype(BF16)
        bt[...] = conved.T[:STATE].astype(BF16)

    buf[...] = dot(tok[...], half_lanes(w_ref[...], 1)).astype(BF16).astype(F32)
    spread = dot(wgt[...], one_hot(g * width, width))
    per = wide // width
    at = pl.multiple_of(lax.rem(g, per) * width, width)
    mine = par[g // per, :, pl.ds(at, width)]
    state = jnp.zeros((STATE, width), F32)
    for k in range(rows // SUB):
        here = slice(k * SUB, (k + 1) * SUB)
        xc = taps(buf, k * SUB, SUB, mine[0:CONV], mine[CONV : CONV + 1]).astype(BF16)
        xc_ref[here] = xc
        weighted = (xc.astype(F32) * spread[here]).astype(BF16)
        state = state + dot(bt[:, here], weighted)
    extra = spread[rows : rows + 8]
    skip_ref[...] = extra
    for c in range(width // 128):
        cols = slice(c * 128, c * 128 + 128)
        for r in range(STATE // 8):
            slab_ref[r, c, 0:8] = state[r * 8 : r * 8 + 8, cols].astype(BF16)
            slab_ref[r, c, 8:16] = extra[:, cols].astype(BF16)


def local_state(me, tokens, halo, w_gate_x, w_small, pieces, conv_w, conv_b):
    rows, depth = tokens.shape
    width = 256

    def whole(a):
        return pl.BlockSpec(a.shape, lambda g: (0,) * a.ndim)

    return pl.pallas_call(
        state_kernel,
        grid=(DINNER // width,),
        in_specs=[
            pl.BlockSpec(memory_space=pltpu.SMEM),
            whole(tokens),
            whole(halo),
            pl.BlockSpec((depth, 2 * width), lambda g: (0, g)),
            whole(w_small),
            *(whole(p) for p in pieces),
            whole(conv_w),
            whole(conv_b),
        ],
        out_specs=[
            pl.BlockSpec((rows, width), lambda g: (0, g)),
            pl.BlockSpec((rows, BC), lambda g: (0, 0)),
            pl.BlockSpec((rows, HEADS), lambda g: (0, 0)),
            pl.BlockSpec((rows, HEADS), lambda g: (0, 0)),
            pl.BlockSpec((8, width), lambda g: (0, g)),
            pl.BlockSpec((STATE // 8, width // 128, 16, 128), lambda g: (0, g, 0, 0)),
        ],
        out_shape=[
            jax.ShapeDtypeStruct((rows, DINNER), BF16),
            jax.ShapeDtypeStruct((rows, BC), BF16),
            jax.ShapeDtypeStruct((rows, HEADS), F32),
            jax.ShapeDtypeStruct((rows, HEADS), F32),
            jax.ShapeDtypeStruct((8, DINNER), F32),
            jax.ShapeDtypeStruct((STATE // 8, DINNER // 128, 16, 128), BF16),
        ],
        scratch_shapes=[
            pltpu.VMEM((PAD + rows, depth), BF16),
            pltpu.VMEM((PAD + rows, width), F32),
            pltpu.VMEM((PAD + rows, BC), F32),
            pltpu.VMEM((rows + 8, 2 * HEADS), BF16),
            pltpu.VMEM((STATE, rows), BF16),
            pltpu.VMEM((len(pieces), 8, DINNER // len(pieces)), F32),
        ],
        compiler_params=params(),
        name="local_state",
    )(me, tokens, halo, w_gate_x, w_small, *pieces, conv_w, conv_b)


def intra_kernel(
    base, xc_ref, tok_ref, w_ref, bc_ref, dt_ref, cum_ref, par_ref,
    own_ref, scale_ref,
    scores, rowlog, bt, wgt,
):
    g = pl.program_id(0)
    rows, width = xc_ref.shape
    blocks = rows // SUB
    heads = width // HEAD_DIM

    @pl.when(g == 0)
    def _():
        bt[...] = bc_ref[...].astype(F32).T[:STATE].astype(BF16)
        for k in range(blocks):
            here = slice(k * SUB, (k + 1) * SUB)
            scores[here] = dot(bc_ref[here, STATE:], bt[:, here])
        cum = cum_ref[...]
        step = dt_ref[...]
        by_row = (cum - jnp.log(step)).T
        for group in range(HEADS // heads):
            rowlog[group, 0:heads] = by_row[group * heads : (group + 1) * heads]
        starts, ends = [], []
        before = jnp.zeros((1, HEADS), F32)
        for k in range(blocks):
            here = slice(k * SUB, (k + 1) * SUB)
            starts.append(jnp.broadcast_to(before, (SUB, HEADS)))
            before = cum[(k + 1) * SUB - 1 : (k + 1) * SUB]
            ends.append(jnp.broadcast_to(before, (SUB, HEADS)))
        starts = jnp.concatenate(starts, axis=0)
        ends = jnp.concatenate(ends, axis=0)
        wgt[0:rows] = hi_lo(step * jnp.exp(ends - cum), 1)
        wgt[rows : 2 * rows] = hi_lo(jnp.exp(cum - starts), 1)
        wgt[2 * rows : 3 * rows] = hi_lo(jnp.exp(cum), 1)

    first = base + g * width
    spread = one_hot(first, width)
    first_head = (base // width + g) * heads
    r = lax.broadcasted_iota(jnp.int32, (SUB, SUB), 0)
    c = lax.broadcasted_iota(jnp.int32, (SUB, SUB), 1)
    causal = r >= c
    lane = lax.broadcasted_iota(jnp.int32, (1, HEADS), 1)
    skip = par_ref[2:3]
    z = dot(tok_ref[...], half_lanes(w_ref[...], 0)).astype(BF16).astype(F32)
    state = jnp.zeros((STATE, width), F32)
    for k in range(blocks):
        here = slice(k * SUB, (k + 1) * SUB)
        xc = xc_ref[here]
        pieces = []
        for h in range(heads):
            head = first_head + h
            col = jnp.sum(
                jnp.where(lane == head, cum_ref[here], 0.0), axis=1, keepdims=True
            )
            row = rowlog[base // width + g, h : h + 1, here]
            decay = jnp.exp(jnp.where(causal, col - row, -jnp.inf))
            mixed = (scores[here] * decay).astype(BF16)
            pieces.append(dot(mixed, xc[:, h * HEAD_DIM : (h + 1) * HEAD_DIM]))
        y = jnp.concatenate(pieces, axis=1)
        xf = xc.astype(F32)
        grow = dot(wgt[rows + k * SUB : rows + (k + 1) * SUB], spread)
        if k > 0:
            y = y + grow * dot(bc_ref[here, STATE:], state.astype(BF16))
        if k + 1 < blocks:
            shrink = dot(wgt[here], spread)
            fresh = dot(bt[:, here], (xf * shrink).astype(BF16))
            state = state * grow[SUB - 1 : SUB] + fresh
        gate = silu(z[here])
        own_ref[here] = (y + skip * xf) * gate
        full = dot(wgt[2 * rows + k * SUB : 2 * rows + (k + 1) * SUB], spread)
        scale_ref[here] = (full * gate).astype(BF16)


def intra(half, halves, xc, tokens, w_gate_x, bc, dt, cum, skips):
    rows = xc.shape[0]
    depth = tokens.shape[1]
    width = 256
    span = DINNER // halves
    steps = span // width
    def whole(a):
        return pl.BlockSpec(a.shape, lambda g: (0,) * a.ndim)

    return pl.pallas_call(
        functools.partial(intra_kernel, half * span),
        grid=(steps,),
        in_specs=[
            pl.BlockSpec((rows, width), lambda g: (0, g + half * steps)),
            whole(tokens),
            pl.BlockSpec((depth, 2 * width), lambda g: (0, g + half * steps)),
            whole(bc),
            whole(dt),
            whole(cum),
            pl.BlockSpec((8, width), lambda g: (0, g + half * steps)),
        ],
        out_specs=[
            pl.BlockSpec((rows, width), lambda g: (0, g)),
            pl.BlockSpec((rows, width), lambda g: (0, g)),
        ],
        out_shape=[
            jax.ShapeDtypeStruct((rows, span), F32),
            jax.ShapeDtypeStruct((rows, span), BF16),
        ],
        scratch_shapes=[
            pltpu.VMEM((rows, SUB), F32),
            pltpu.VMEM((DINNER // width, 8, rows), F32),
            pltpu.VMEM((STATE, rows), BF16),
            pltpu.VMEM((3 * rows, 2 * HEADS), BF16),
        ],
        compiler_params=params(),
        name="intra",
    )(xc, tokens, w_gate_x, bc, dt, cum, skips)


def scan_kernel(in_ref, out_ref):
    count = in_ref.shape[0]
    state = jnp.zeros((8, 128), F32)
    for q in range(count):
        out_ref[q] = state.astype(BF16)
        slab = in_ref[q].astype(F32)
        state = state * (slab[8:9] + slab[9:10]) + slab[0:8]


def scan_devices(slabs):
    count = slabs.shape[0]
    return pl.pallas_call(
        scan_kernel,
        out_shape=jax.ShapeDtypeStruct((count, 8, 128), BF16),
        compiler_params=params(0),
        name="scan_devices",
    )(slabs)


def finish_kernel(c_ref, slab_ref, own0, own1, scale0, scale1, gain_ref, w_ref,
                  out_ref, acc, squares):
    g = pl.program_id(0)
    last = pl.num_programs(0) - 1
    half = pl.num_programs(0) // 2
    columns = slab_ref.shape[1]
    slabs = [
        slab_ref[:, c].astype(F32).reshape(STATE, 128).astype(BF16)
        for c in range(columns)
    ]
    carried = dot(c_ref[:, STATE:], jnp.concatenate(slabs, axis=1))

    def step(own_ref, scale_ref):
        gated = (own_ref[...] + scale_ref[...].astype(F32) * carried).astype(BF16)
        gated = gated.astype(F32)
        part = jnp.sum(gated * gated, axis=1, keepdims=True)
        product = dot((gated * gain_ref[...]).astype(BF16), w_ref[...])

        @pl.when(g == 0)
        def _():
            acc[...] = product
            squares[...] = part

        @pl.when(g > 0)
        def _():
            acc[...] += product
            squares[...] += part

    @pl.when(g < half)
    def _():
        step(own0, scale0)

    @pl.when(g >= half)
    def _():
        step(own1, scale1)

    @pl.when(g == last)
    def _():
        scale = lax.rsqrt(squares[...] * (1.0 / DINNER) + EPSILON)
        out_ref[...] = (acc[...] * scale).astype(BF16)


def finish(bc, slabs, owns, scales, norm_gain, w_out):
    rows = bc.shape[0]
    width = 512
    steps = DINNER // width
    half = steps // 2
    columns = w_out.shape[1]

    def first(g):
        return (0, jnp.minimum(g, half - 1))

    def second(g):
        return (0, jnp.maximum(g - half, 0))

    return pl.pallas_call(
        finish_kernel,
        grid=(steps,),
        in_specs=[
            pl.BlockSpec(bc.shape, lambda g: (0, 0)),
            pl.BlockSpec((STATE // 8, width // 128, 8, 128), lambda g: (0, g, 0, 0)),
            pl.BlockSpec((rows, width), first),
            pl.BlockSpec((rows, width), second),
            pl.BlockSpec((rows, width), first),
            pl.BlockSpec((rows, width), second),
            pl.BlockSpec((1, width), lambda g: (0, g)),
            pl.BlockSpec((width, columns), lambda g: (g, 0)),
        ],
        out_specs=pl.BlockSpec((rows, columns), lambda g: (0, 0)),
        out_shape=jax.ShapeDtypeStruct((rows, columns), BF16),
        scratch_shapes=[pltpu.VMEM((rows, columns), F32), pltpu.VMEM((rows, 1), F32)],
        compiler_params=params(),
        name="finish",
    )(bc, slabs, owns[0], owns[1], scales[0], scales[1], norm_gain, w_out)


def on_device(
    tokens, w_gate_x, w_bc_dt, conv_x_weight, conv_x_bias, conv_bc_weight,
    conv_bc_bias, dt_bias, a_log, skip_d, norm_gain, w_out,
):
    n = lax.axis_size("head")
    devices = lax.axis_size("seq") * n
    me = lax.axis_index("head")[None]
    packed, tail = pack(conv_x_weight, conv_x_bias, dt_bias, a_log, skip_d, tokens)
    halo = lax.ppermute(tail, BOTH, [(i, i + 1) for i in range(devices - 1)])
    pieces = [packed]
    for k in range(1, n):
        pairs = [(i, (i - k) % n) for i in range(n)]
        pieces.append(lax.ppermute(packed, "head", pairs))
    xc, bc, dt, cum, skips, slabs = local_state(
        me, tokens, halo, w_gate_x, w_bc_dt.T, pieces,
        conv_bc_weight, conv_bc_bias[None],
    )
    slabs = slabs.reshape(devices, 16, 128)
    by_owner = lax.all_to_all(slabs, BOTH, 0, 0, tiled=True)
    rest = (tokens, w_gate_x, bc, dt, cum, skips)
    own0, scale0 = intra(0, 2, xc, *rest)
    by_owner, own0 = lax.optimization_barrier((by_owner, own0))
    incoming = scan_devices(by_owner)
    back = lax.all_to_all(incoming, BOTH, 0, 0, tiled=True)
    xc, incoming = lax.optimization_barrier((xc, incoming))
    own1, scale1 = intra(1, 2, xc, *rest)
    back = back.reshape(STATE // 8, DINNER // 128, 8, 128)
    return finish(bc, back, (own0, own1), (scale0, scale1), norm_gain[None], w_out)


def solution(mesh):
    return jax.shard_map(
        on_device,
        mesh=mesh,
        in_specs=(
            P(BOTH, None),
            P(),
            P(),
            P(None, "head"),
            P("head"),
            P(),
            P(),
            P("head"),
            P("head"),
            P("head"),
            P(),
            P(),
        ),
        out_specs=P(BOTH, None),
        check_vma=False,
    )
```

```python
import functools

import jax
import jax.numpy as jnp
from jax import lax
from jax.experimental import pallas as pl
from jax.experimental.pallas import tpu as pltpu
from jax.sharding import Mesh
from jax.sharding import PartitionSpec as P

HEADS = 32
HEAD_DIM = 64
STATE = 64
CONV = 4
DINNER = HEADS * HEAD_DIM
BC = 2 * STATE
SUB = 128
PAD = 16
EPSILON = 1e-05
FAR = "chips"
NEAR = ("row", "core", "head")
BOTH = (FAR, *NEAR)
WIDTH = 256
OWNED = 128
TOGETHER = 1
SPLIT = (2, 4, 2)
F32 = jnp.float32
BF16 = jnp.bfloat16
OWN = jnp.float32
LIMIT = 60 * 1024 * 1024
LOG2E = 1.4426950408889634
FAR_AWAY = pl.BlockSpec(memory_space=pltpu.HBM)


def params(steps=1):
    return pltpu.CompilerParams(
        dimension_semantics=("arbitrary",) * steps, vmem_limit_bytes=LIMIT
    )


def silu(v):
    half = 0.5 * v
    return half + half * jnp.tanh(half)


def hi_lo(v, axis):
    hi = v.astype(BF16)
    lo = (v - hi.astype(F32)).astype(BF16)
    return jnp.concatenate([hi, lo], axis=axis)


def dot(a, b):
    return jnp.dot(a, b, preferred_element_type=F32)


def split3(v):
    hi = v.astype(BF16)
    rest = v - hi.astype(F32)
    mid = rest.astype(BF16)
    return [hi, mid, (rest - mid.astype(F32)).astype(BF16)]


def call(kernel, args, outs, scratch, name, far=(), far_out=(), scalars=()):
    specs = [pl.BlockSpec(memory_space=pltpu.SMEM)] * len(scalars)
    specs += [FAR_AWAY if i in far else pl.BlockSpec() for i in range(len(args))]
    return pl.pallas_call(
        kernel,
        in_specs=specs,
        out_specs=[FAR_AWAY if i in far_out else pl.BlockSpec() for i in range(len(outs))],
        out_shape=[jax.ShapeDtypeStruct(shape, dtype) for shape, dtype in outs],
        scratch_shapes=scratch,
        compiler_params=params(0),
        name=name,
    )(*scalars, *args)


def start(source, target, sem):
    copy = pltpu.make_async_copy(source, target, sem)
    copy.start()
    return copy


def on_chip(array):
    return pltpu.with_memory_space_constraint(array, pltpu.VMEM)


def place(r):
    return r // 8 + SUB // 8 * (r % 8)


def reorder(back=False):
    r = lax.broadcasted_iota(jnp.int32, (SUB, SUB), 1 if back else 0)
    c = lax.broadcasted_iota(jnp.int32, (SUB, SUB), 0 if back else 1)
    return (place(r) == c).astype(F32).astype(BF16)


def one_hot(first_channel, width):
    row = lax.broadcasted_iota(jnp.int32, (2 * HEADS, width), 0)
    chan = lax.broadcasted_iota(jnp.int32, (2 * HEADS, width), 1) + first_channel
    return ((row % HEADS) == (chan // HEAD_DIM)).astype(F32).astype(BF16)


def pack_kernel(w_ref, b_ref, dt_ref, a_ref, skip_ref, tok_ref, out_ref, tail_ref):
    out_ref[...] = jnp.zeros_like(out_ref)
    here = dt_ref.shape[1]
    for k in range(out_ref.shape[0]):
        out_ref[k, 0:CONV] = w_ref[...]
        out_ref[k, CONV : CONV + 1] = b_ref[...]
        for row, ref in ((5, dt_ref), (6, a_ref), (7, skip_ref)):
            out_ref[k, row : row + 1, 0:here] = ref[...]
    tail_ref[...] = tok_ref[...]


def pack(weight, bias, dt_bias, a_log, skip_d, tokens, copies):
    rows, depth = tokens.shape
    small = (weight, bias[None], dt_bias[None], a_log[None], skip_d[None])

    def whole(a):
        return pl.BlockSpec(a.shape, lambda g: (0, 0))

    return pl.pallas_call(
        pack_kernel,
        grid=(1,),
        in_specs=[whole(a) for a in small]
        + [pl.BlockSpec((8, depth), lambda g: (rows // 8 - 1, 0))],
        out_specs=[
            pl.BlockSpec((copies, 8, weight.shape[1]), lambda g: (0, 0, 0)),
            pl.BlockSpec((8, depth), lambda g: (0, 0)),
        ],
        out_shape=[
            jax.ShapeDtypeStruct((copies, 8, weight.shape[1]), F32),
            jax.ShapeDtypeStruct((8, depth), BF16),
        ],
        compiler_params=params(),
        name="pack",
    )(*small, tokens)


def half_lanes(w, which):
    parts = []
    for k in range(w.shape[1] // 128):
        at = k * 128 + which * HEAD_DIM
        parts.append(w[:, at : at + HEAD_DIM])
    return jnp.concatenate(parts, axis=1)


def convolve(x, weights, bias):
    first = lax.broadcasted_iota(jnp.int32, (8, 1), 0) == 0
    results = []
    for k in range((x.shape[0] - PAD) // SUB):
        at = PAD + k * SUB
        rows = x[at : at + SUB]
        edge = []
        for m in range(1, CONV):
            own = x[at + SUB - 8 * m : at + SUB - 8 * m + 8]
            last = PAD - m if k == 0 else at - 8 * m + 7
            edge.insert(0, jnp.where(first, x[last : last + 1], pltpu.roll(own, 1, 0)))
        summed = bias + weights[CONV - 1 : CONV] * rows
        for m in range(1, CONV):
            moved = jnp.concatenate(edge[CONV - 1 - m :] + [rows[: SUB - 8 * m]], axis=0)
            summed = summed + weights[CONV - 1 - m : CONV - m] * moved
        results.append(silu(summed))
    return results


def state_kernel(
    tok_hbm, halo_ref, w_hbm, wsmall_hbm, par, wbc_ref, bbc_ref,
    xc_hbm, z_hbm, bc_hbm, dt_hbm, cum_hbm, skip_hbm, slab_ref,
    raw, tok, w_ref, wsmall, xc_ref, z_ref, bc_ref, dt_ref, cum_ref, skip_ref,
    wgt, bt, in_sem, out_sem,
):
    rows = tok_hbm.shape[0]
    groups = DINNER // WIDTH
    half = DINNER
    fetch_tok = start(tok_hbm, raw, in_sem.at[0])
    fetch_small = start(wsmall_hbm, wsmall, in_sem.at[1])
    fetch_w = [
        start(w_hbm.at[:, i * half : (i + 1) * half], w_ref.at[i], in_sem.at[2 + i])
        for i in range(2)
    ]
    tok[0 : PAD - 8] = jnp.zeros((PAD - 8, tok.shape[1]), BF16)
    tok[PAD - 8 : PAD] = halo_ref[...]
    fetch_tok.wait()
    order = reorder()
    for k in range(rows // SUB):
        here = slice(k * SUB, (k + 1) * SUB)
        tok[PAD + k * SUB : PAD + (k + 1) * SUB] = dot(order, raw[here]).astype(BF16)
    fetch_small.wait()
    begin(tok, wsmall, par, wbc_ref, bbc_ref, bc_ref, dt_ref, cum_ref, wgt, bt)
    sends = [
        start(bc_ref, bc_hbm, out_sem.at[0]),
        start(dt_ref, dt_hbm, out_sem.at[1]),
        start(cum_ref, cum_hbm, out_sem.at[2]),
    ]

    def project(g):
        at = 2 * g * WIDTH % half
        both = dot(tok[...], w_ref[2 * g * WIDTH // half, :, at : at + 2 * WIDTH])
        both = both.astype(BF16)
        z_ref[:, g * WIDTH : (g + 1) * WIDTH] = half_lanes(both[PAD:], 0)
        return half_lanes(both, 1).astype(F32)

    wide = par.shape[2]
    for part in range(2):
        fetch_w[part].wait()
        mine_groups = range(part * groups // 2, (part + 1) * groups // 2)
        ahead = project(mine_groups[0])
        for g in mine_groups:
            x = ahead
            if g + 1 in mine_groups:
                ahead = project(g + 1)
            cols = slice(g * WIDTH, (g + 1) * WIDTH)
            spread = dot(wgt[...], one_hot(g * WIDTH, WIDTH))
            at = g * WIDTH % wide
            mine = par[g * WIDTH // wide, :, at : at + WIDTH]
            blocks = convolve(x, mine[0:CONV], mine[CONV : CONV + 1])
            xc = jnp.concatenate([block.astype(BF16) for block in blocks], axis=0)
            xc_ref[:, cols] = xc
            weighted = (xc.astype(F32) * spread[:rows]).astype(BF16)
            state = dot(bt[...], weighted)
            extra = spread[rows : rows + 8]
            skip_ref[:, cols] = extra
            for i in range(WIDTH // OWNED):
                own = slice(i * OWNED, (i + 1) * OWNED)
                owner = g * WIDTH // OWNED + i
                slab_ref[owner, 0:STATE] = state[:, own].astype(BF16)
                slab_ref[owner, STATE : STATE + 8] = extra[:, own].astype(BF16)
        cols = slice(part * DINNER // 2, (part + 1) * DINNER // 2)
        for k, (ref, hbm) in enumerate(((xc_ref, xc_hbm), (z_ref, z_hbm))):
            sends.append(
                start(ref.at[:, cols], hbm.at[:, cols], out_sem.at[3 + 2 * part + k])
            )
    sends.append(start(skip_ref, skip_hbm, out_sem.at[7]))
    for copy in sends:
        copy.wait()


def begin(tok, wsmall_ref, par, wbc_ref, bbc_ref, bc_ref, dt_ref, cum_ref, wgt, bt):
    rows = dt_ref.shape[0]
    blocks = par.shape[0]
    each = HEADS // blocks
    lane = lax.broadcasted_iota(jnp.int32, (8, 128), 1)
    heads = jnp.zeros((8, 128), F32)
    for k in range(blocks):
        block = par[k, :, 0:128]
        moved = block if k == 0 else pltpu.roll(block, each * k, 1)
        heads = jnp.where(lane // each == k, moved, heads)
    heads = heads[:, :HEADS]
    small = lax.dot_general(
        tok[...], wsmall_ref[...], (((1,), (1,)), ((), ())),
        preferred_element_type=F32,
    )
    small = small.astype(BF16).astype(F32)
    raw = small[PAD:, BC:] + heads[5:6]
    step = jnp.maximum(raw, 0.0) + jnp.log1p(jnp.exp(-jnp.abs(raw)))
    decay = step * -jnp.exp(heads[6:7])
    r = lax.broadcasted_iota(jnp.int32, (SUB, SUB), 0)
    c = lax.broadcasted_iota(jnp.int32, (SUB, SUB), 1)
    ones = (place(r) >= place(c)).astype(F32).astype(BF16)
    before = jnp.zeros((1, HEADS), F32)
    parts = []
    for k in range(rows // SUB):
        three = jnp.concatenate(split3(decay[k * SUB : (k + 1) * SUB]), axis=1)
        sums = dot(ones, three)
        part = before + (
            sums[:, :HEADS] + sums[:, HEADS : 2 * HEADS] + sums[:, 2 * HEADS :]
        )
        before = part[SUB - 1 : SUB]
        parts.append(part)
    cum = jnp.concatenate(parts, axis=0)
    dt_ref[...] = step
    cum_ref[...] = cum
    wgt[0:rows] = hi_lo(step * jnp.exp(before - cum), 1)
    total = hi_lo(jnp.exp(before), 1)
    zero = jnp.zeros((1, HEADS), BF16)
    wgt[rows : rows + 8] = jnp.concatenate(
        [
            jnp.concatenate([total[:, :HEADS], zero], axis=1),
            jnp.concatenate([zero, total[:, HEADS:]], axis=1),
            hi_lo(heads[7:8], 1),
            jnp.zeros((5, 2 * HEADS), BF16),
        ],
        axis=0,
    )
    conved = jnp.concatenate(
        convolve(small[:, :BC], wbc_ref[...], bbc_ref[...]), axis=0
    )
    bc_ref[...] = conved.astype(BF16)
    bt[...] = conved.T[:STATE].astype(BF16)


def local_state(tokens, halo, w_gate_x, w_small, packed, conv_w, conv_b):
    rows, depth = tokens.shape
    outs = [
        ((rows, DINNER), BF16),
        ((rows, DINNER), BF16),
        ((rows, BC), BF16),
        ((rows, HEADS), F32),
        ((rows, HEADS), F32),
        ((8, DINNER), F32),
    ]
    return call(
        state_kernel,
        [tokens, on_chip(halo), w_gate_x, w_small, on_chip(packed), conv_w, conv_b],
        outs + [((DINNER // OWNED, STATE + 8, OWNED), BF16)],
        [
            pltpu.VMEM((rows, depth), BF16),
            pltpu.VMEM((PAD + rows, depth), BF16),
            pltpu.VMEM((2, depth, DINNER), BF16),
            pltpu.VMEM(w_small.shape, BF16),
            *(pltpu.VMEM(shape, dtype) for shape, dtype in outs),
            pltpu.VMEM((rows + 8, 2 * HEADS), BF16),
            pltpu.VMEM((STATE, rows), BF16),
            pltpu.SemaphoreType.DMA((4,)),
            pltpu.SemaphoreType.DMA((8,)),
        ],
        "local_state",
        far=(0, 2, 3),
        far_out=range(6),
    )


def prepare(bc_ref, dt_ref, cum_ref, scores, left, rowlog, bt, wgt):
    rows = bc_ref.shape[0]
    heads = WIDTH // HEAD_DIM
    bt[...] = bc_ref[...].astype(F32).T[:STATE].astype(BF16)
    for k in range(rows // SUB):
        here = slice(k * SUB, (k + 1) * SUB)
        scores[here] = dot(bc_ref[here, STATE:], bt[:, here])
    cum = cum_ref[...]
    step = dt_ref[...]
    ones = jnp.ones((rows, HEADS), BF16)
    left[...] = jnp.concatenate(split3(cum * LOG2E) + [ones], axis=1)
    by_row = (jnp.log(jnp.maximum(step, 1e-37)) - cum) * LOG2E
    by_row = jnp.concatenate([p.astype(F32) for p in split3(by_row)] + [cum], axis=1).T
    for g in range(HEADS // heads):
        for p in range(3):
            first = p * HEADS + g * heads
            rowlog[g, p, 0:heads] = by_row[first : first + heads]
    starts, ends = [], []
    before = jnp.zeros((1, HEADS), F32)
    for k in range(rows // SUB):
        starts.append(jnp.broadcast_to(before, (SUB, HEADS)))
        before = cum[(k + 1) * SUB - 1 : (k + 1) * SUB]
        ends.append(jnp.broadcast_to(before, (SUB, HEADS)))
    starts = jnp.concatenate(starts, axis=0)
    ends = jnp.concatenate(ends, axis=0)
    wgt[0:rows] = hi_lo(step * jnp.exp(ends - cum), 1)
    wgt[rows : 2 * rows] = hi_lo(jnp.exp(cum - starts), 1)
    wgt[2 * rows : 3 * rows] = hi_lo(jnp.exp(cum), 1)


def intra_kernel(
    first_group, xc_ref, z_ref, bc_ref, dt_ref, cum_ref, skip_ref,
    own_ref, scale_ref, scores, left, rowlog, bt, wgt,
):
    rows = xc_ref.shape[0]
    blocks = rows // SUB
    heads = WIDTH // HEAD_DIM
    together = xc_ref.shape[1] // WIDTH

    @pl.when(pl.program_id(0) == 0)
    def _():
        prepare(bc_ref, dt_ref, cum_ref, scores, left, rowlog, bt, wgt)

    r = lax.broadcasted_iota(jnp.int32, (SUB, heads * SUB), 0)
    c = lax.broadcasted_iota(jnp.int32, (SUB, heads * SUB), 1)
    causal = place(r) >= place(c % SUB)
    low = lax.broadcasted_iota(jnp.int32, (1, 128), 1) < HEAD_DIM
    pr = lax.broadcasted_iota(jnp.int32, (3 * HEADS, heads * SUB), 0)
    pc = lax.broadcasted_iota(jnp.int32, (3 * HEADS, heads * SUB), 1)
    for i in range(together):
        g = first_group + pl.program_id(0) * together + i
        mine = slice(i * WIDTH, (i + 1) * WIDTH)
        spread = one_hot(g * WIDTH, WIDTH)
        pick = (pr % HEADS == g * heads + pc // SUB).astype(F32).astype(BF16)
        skip = skip_ref[2:3, mine]
        state = jnp.zeros((STATE, WIDTH), F32)
        for k in range(blocks):
            here = slice(k * SUB, (k + 1) * SUB)
            xc = xc_ref[here, mine]
            late = jnp.concatenate(
                [
                    jnp.concatenate(
                        [rowlog[g, p, h : h + 1, here] for h in range(heads)], axis=1
                    )
                    for p in range(3)
                ]
                + [jnp.zeros((HEADS - 3, heads * SUB), F32)],
                axis=0,
            ).astype(BF16)
            gaps = dot(left[here], jnp.concatenate([pick, late], axis=0))
            decay = jnp.exp2(jnp.where(causal, gaps, -jnp.inf))
            score = scores[here]
            pieces = []
            for pair in range(heads // 2):
                both = [
                    (score * decay[:, h * SUB : (h + 1) * SUB]).astype(BF16)
                    for h in (2 * pair, 2 * pair + 1)
                ]
                x = xc[:, pair * 128 : pair * 128 + 128]
                none = jnp.zeros_like(x)
                right = jnp.concatenate(
                    [jnp.where(low, x, none), jnp.where(low, none, x)], axis=0
                )
                pieces.append(dot(jnp.concatenate(both, axis=1), right))
            y = jnp.concatenate(pieces, axis=1)
            xf = xc.astype(F32)
            grow = dot(wgt[rows + k * SUB : rows + (k + 1) * SUB], spread)
            if k > 0:
                y = y + grow * dot(bc_ref[here, STATE:], state.astype(BF16))
            if k + 1 < blocks:
                shrink = dot(wgt[here], spread)
                fresh = dot(bt[:, here], (xf * shrink).astype(BF16))
                state = state * grow[SUB - 1 : SUB] + fresh
            gate = silu(z_ref[here, mine].astype(F32))
            own_ref[here, mine] = ((y + skip * xf) * gate).astype(own_ref.dtype)
            full = dot(wgt[2 * rows + k * SUB : 2 * rows + (k + 1) * SUB], spread)
            scale_ref[here, mine] = (full * gate).astype(BF16)


def intra(first_group, groups, xc, z, bc, dt, cum, skips):
    rows = xc.shape[0]
    together = TOGETHER
    group = first_group // together
    wide = together * WIDTH

    def whole(a):
        return pl.BlockSpec(a.shape, lambda i: (0,) * a.ndim)

    return pl.pallas_call(
        functools.partial(intra_kernel, first_group),
        grid=(groups // together,),
        in_specs=[
            pl.BlockSpec((rows, wide), lambda i: (0, i + group)),
            pl.BlockSpec((rows, wide), lambda i: (0, i + group)),
            whole(bc),
            whole(dt),
            whole(cum),
            pl.BlockSpec((8, wide), lambda i: (0, i + group)),
        ],
        out_specs=[
            pl.BlockSpec((rows, wide), lambda i: (0, i)),
            pl.BlockSpec((rows, wide), lambda i: (0, i)),
        ],
        out_shape=[
            jax.ShapeDtypeStruct((rows, groups * WIDTH), OWN),
            jax.ShapeDtypeStruct((rows, groups * WIDTH), BF16),
        ],
        scratch_shapes=[
            pltpu.VMEM((rows, SUB), F32),
            pltpu.VMEM((rows, 4 * HEADS), BF16),
            pltpu.VMEM((DINNER // WIDTH, 3, 8, rows), F32),
            pltpu.VMEM((STATE, rows), BF16),
            pltpu.VMEM((3 * rows, 2 * HEADS), BF16),
        ],
        compiler_params=params(),
        name="intra",
    )(xc, z, bc, dt, cum, skips)


def through(state, slab):
    slab = slab.astype(F32)
    total = slab[STATE : STATE + 1] + slab[STATE + 1 : STATE + 2]
    return state * total + slab[0:STATE], total


def fold_kernel(in_ref, out_ref):
    state = jnp.zeros((STATE, OWNED), F32)
    whole = jnp.ones((1, OWNED), F32)
    for q in range(in_ref.shape[0]):
        state, total = through(state, in_ref[q])
        whole = whole * total
    hi = whole.astype(BF16).astype(F32)
    row = lax.broadcasted_iota(jnp.int32, (8, OWNED), 0)
    tail = jnp.where(row == 0, hi, jnp.where(row == 1, whole - hi, 0.0))
    state = state.astype(BF16)
    tail = tail.astype(BF16)
    for b in range(out_ref.shape[0]):
        out_ref[b, 0:STATE] = state
        out_ref[b, STATE:] = tail


def fold(near, blocks):
    out = ((blocks, *near.shape[1:]), BF16)
    return call(fold_kernel, [on_chip(near)], [out], [], "fold")[0]


def unfold_kernel(me_ref, near_ref, far_ref, out_ref):
    def earlier(b, state):
        return through(state, far_ref[b])[0]

    state = jnp.zeros((STATE, OWNED), F32)
    state = lax.fori_loop(0, me_ref[0], earlier, state)
    for q in range(near_ref.shape[0]):
        out_ref[q] = state.astype(BF16)
        state, _ = through(state, near_ref[q])


def unfold(me, near, far):
    count = near.shape[0]
    out = ((count, STATE, OWNED), BF16)
    operands = [on_chip(near), on_chip(far)]
    return call(unfold_kernel, operands, [out], [], "unfold", scalars=(me,))[0]


def finish_kernel(parts, c_ref, in_ref, gain_ref, w_hbm, *refs):
    own_hbm, scale_hbm = refs[:parts], refs[parts : 2 * parts]
    out_ref, w_ref, own_all, scale_all, acc, in_sem, w_sem = refs[2 * parts :]
    rows = c_ref.shape[0]
    halves = 2
    span = DINNER // halves
    fetches = []
    fetch_w = []
    for k in range(halves):
        fetches.append([])
        at = 0
        for p in range(parts):
            low, high = max(at, k * span), min(at + own_hbm[p].shape[1], (k + 1) * span)
            if low < high:
                there, here = slice(low - at, high - at), slice(low, high)
                for i, (hbm, ref) in enumerate(
                    ((own_hbm[p], own_all), (scale_hbm[p], scale_all))
                ):
                    source, target = hbm.at[:, there], ref.at[:, here]
                    fetches[k].append(start(source, target, in_sem.at[k, p, i]))
            at += own_hbm[p].shape[1]
        part = slice(k * span, (k + 1) * span)
        fetch_w.append(start(w_hbm.at[part], w_ref.at[part], w_sem.at[k]))
    total = jnp.zeros((rows, 128), F32)

    def gate(k, total):
        sides = []
        for g in range(k * span // WIDTH, (k + 1) * span // WIDTH):
            cols = slice(g * WIDTH, (g + 1) * WIDTH)
            slabs = [in_ref[2 * g], in_ref[2 * g + 1]]
            carried = dot(c_ref[:, STATE:], jnp.concatenate(slabs, axis=1))
            gated = own_all[:, cols] + scale_all[:, cols].astype(F32) * carried
            gated = gated.astype(BF16).astype(F32)
            square = gated * gated
            total = total + square[:, :128] + square[:, 128:]
            sides.append((gated * gain_ref[:, cols]).astype(BF16))
        return jnp.concatenate(sides, axis=1), total

    for copy in fetches[0]:
        copy.wait()
    left, total = gate(0, total)
    for copy in fetches[1] + fetch_w[:1]:
        copy.wait()
    acc[...] = dot(left, w_ref[:span])
    right, total = gate(1, total)
    fetch_w[1].wait()
    mean = jnp.sum(total, axis=1, keepdims=True) * (1.0 / DINNER)
    product = (acc[...] + dot(right, w_ref[span:])) * lax.rsqrt(mean + EPSILON)
    product = product.astype(BF16)
    order = reorder(back=True)
    for k in range(rows // SUB):
        here = slice(k * SUB, (k + 1) * SUB)
        out_ref[here] = dot(order, product[here]).astype(BF16)


def finish(bc, incoming, owns, scales, norm_gain, w_out):
    rows = bc.shape[0]
    columns = w_out.shape[1]
    parts = len(owns)
    return call(
        functools.partial(finish_kernel, parts),
        [bc, on_chip(incoming), norm_gain, w_out, *owns, *scales],
        [((rows, columns), BF16)],
        [
            pltpu.VMEM(w_out.shape, BF16),
            pltpu.VMEM((rows, DINNER), F32),
            pltpu.VMEM((rows, DINNER), BF16),
            pltpu.VMEM((rows, columns), F32),
            pltpu.SemaphoreType.DMA((2, parts, 2)),
            pltpu.SemaphoreType.DMA((2,)),
        ],
        "finish",
        far=range(3, 4 + 2 * parts),
    )[0]


def on_device(
    tokens, w_gate_x, w_bc_dt, conv_x_weight, conv_x_bias, conv_bc_weight,
    conv_bc_bias, dt_bias, a_log, skip_d, norm_gain, w_out,
):
    n = lax.axis_size("head")
    blocks = lax.axis_size(FAR)
    devices = blocks * lax.axis_size(NEAR)
    my_block = lax.axis_index(FAR)[None]
    packed, tail = pack(conv_x_weight, conv_x_bias, dt_bias, a_log, skip_d, tokens, n)
    packed = lax.all_to_all(packed, "head", 0, 0, tiled=True)
    halo = lax.ppermute(tail, BOTH, [(i, i + 1) for i in range(devices - 1)])
    xc, z, bc, dt, cum, skips, slabs = local_state(
        tokens, halo, w_gate_x, w_bc_dt.T, packed, conv_bc_weight, conv_bc_bias[None]
    )
    near = lax.all_to_all(slabs, NEAR, 0, 0, tiled=True)
    rest = (bc, dt, cum, skips)
    first, second, third = SPLIT
    own0, scale0 = intra(0, first, xc, z, *rest)
    near, own0 = lax.optimization_barrier((near, own0))
    copies = fold(near, blocks)
    far = lax.all_to_all(copies, FAR, 0, 0, tiled=True)
    z, copies = lax.optimization_barrier((z, copies))
    own1, scale1 = intra(first, second, xc, z, *rest)
    far, own1 = lax.optimization_barrier((far, own1))
    incoming = unfold(my_block, near, far)
    back = lax.all_to_all(incoming, NEAR, 0, 0, tiled=True)
    z, incoming = lax.optimization_barrier((z, incoming))
    own2, scale2 = intra(first + second, third, xc, z, *rest)
    owns, scales = (own0, own1, own2), (scale0, scale1, scale2)
    return finish(bc, back, owns, scales, norm_gain[None], w_out)


def solution(mesh):
    seq, head = mesh.devices.shape
    split = Mesh(mesh.devices.reshape(seq // 4, 2, 2, head), BOTH)
    return jax.shard_map(
        on_device,
        mesh=split,
        in_specs=(
            P(BOTH, None),
            P(),
            P(),
            P(None, "head"),
            P("head"),
            P(),
            P(),
            P("head"),
            P("head"),
            P("head"),
            P(),
            P(),
        ),
        out_specs=P(BOTH, None),
        check_vma=False,
    )
```

```python
import functools

import jax
import jax.numpy as jnp
from jax import lax
from jax.experimental import pallas as pl
from jax.experimental.pallas import tpu as pltpu
from jax.sharding import Mesh
from jax.sharding import PartitionSpec as P

HEADS = 32
HEAD_DIM = 64
STATE = 64
CONV = 4
DINNER = HEADS * HEAD_DIM
BC = 2 * STATE
SUB = 128
PAD = 16
EPSILON = 1e-05
FAR = "chips"
NEAR = ("row", "core", "head")
BOTH = (FAR, *NEAR)
WIDTH = 256
OWNED = 128
TOGETHER = 1
SPLIT = (3, 3, 2)
FINE = 256
SEND = 512
CHUNKS = 2
F32 = jnp.float32
BF16 = jnp.bfloat16
OWN = jnp.bfloat16
LIMIT = 60 * 1024 * 1024
LOG2E = 1.4426950408889634
FAR_AWAY = pl.BlockSpec(memory_space=pltpu.HBM)


def params(steps=1):
    return pltpu.CompilerParams(
        dimension_semantics=("arbitrary",) * steps, vmem_limit_bytes=LIMIT
    )


def silu(v):
    half = 0.5 * v
    return half + half * jnp.tanh(half)


def hi_lo(v, axis):
    hi = v.astype(BF16)
    lo = (v - hi.astype(F32)).astype(BF16)
    return jnp.concatenate([hi, lo], axis=axis)


def dot(a, b):
    return jnp.dot(a, b, preferred_element_type=F32)


def split3(v):
    hi = v.astype(BF16)
    rest = v - hi.astype(F32)
    mid = rest.astype(BF16)
    return [hi, mid, (rest - mid.astype(F32)).astype(BF16)]


def call(kernel, args, outs, scratch, name, far=(), far_out=(), scalars=()):
    specs = [pl.BlockSpec(memory_space=pltpu.SMEM)] * len(scalars)
    specs += [FAR_AWAY if i in far else pl.BlockSpec() for i in range(len(args))]
    return pl.pallas_call(
        kernel,
        in_specs=specs,
        out_specs=[FAR_AWAY if i in far_out else pl.BlockSpec() for i in range(len(outs))],
        out_shape=[jax.ShapeDtypeStruct(shape, dtype) for shape, dtype in outs],
        scratch_shapes=scratch,
        compiler_params=params(0),
        name=name,
    )(*scalars, *args)


def start(source, target, sem):
    copy = pltpu.make_async_copy(source, target, sem)
    copy.start()
    return copy


def on_chip(array):
    return pltpu.with_memory_space_constraint(array, pltpu.VMEM)


def place(r):
    return r // 8 + SUB // 8 * (r % 8)


def reorder(back=False):
    r = lax.broadcasted_iota(jnp.int32, (SUB, SUB), 1 if back else 0)
    c = lax.broadcasted_iota(jnp.int32, (SUB, SUB), 0 if back else 1)
    return (place(r) == c).astype(F32).astype(BF16)


def one_hot(first_channel, width):
    row = lax.broadcasted_iota(jnp.int32, (2 * HEADS, width), 0)
    chan = lax.broadcasted_iota(jnp.int32, (2 * HEADS, width), 1) + first_channel
    return ((row % HEADS) == (chan // HEAD_DIM)).astype(F32).astype(BF16)


def pack_kernel(w_ref, b_ref, dt_ref, a_ref, skip_ref, wbc_ref, bbc_ref, gain_ref,
                tok_ref, out_ref, tail_ref, gain_out):
    out_ref[...] = jnp.zeros_like(out_ref)
    here = dt_ref.shape[1]
    for k in range(out_ref.shape[0]):
        out_ref[k, 0:CONV] = w_ref[...]
        out_ref[k, CONV : CONV + 1] = b_ref[...]
        for row, ref in ((5, dt_ref), (6, a_ref), (7, skip_ref)):
            out_ref[k, row : row + 1, 0:here] = ref[...]
        for tap in range(CONV):
            row, cols = bc_slot(tap)
            out_ref[k, row : row + 1, cols] = wbc_ref[tap : tap + 1]
        row, cols = bc_slot(CONV)
        out_ref[k, row : row + 1, cols] = bbc_ref[...]
    tail_ref[...] = tok_ref[...]
    gain_out[...] = jnp.broadcast_to(gain_ref[...], gain_out.shape)


def bc_slot(k):
    at = 128 * (1 + k % 3)
    return 5 + k // 3, slice(at, at + BC)


def pack(small, tokens, copies):
    rows, depth = tokens.shape
    small = [a if a.ndim == 2 else a[None] for a in small]
    wide = small[0].shape[1]

    def whole(a):
        return pl.BlockSpec(a.shape, lambda g: (0, 0))

    return pl.pallas_call(
        pack_kernel,
        grid=(1,),
        in_specs=[whole(a) for a in small]
        + [pl.BlockSpec((8, depth), lambda g: (rows // 8 - 1, 0))],
        out_specs=[
            pl.BlockSpec((copies, 8, wide), lambda g: (0, 0, 0)),
            pl.BlockSpec((8, depth), lambda g: (0, 0)),
            pl.BlockSpec((8, DINNER), lambda g: (0, 0)),
        ],
        out_shape=[
            jax.ShapeDtypeStruct((copies, 8, wide), F32),
            jax.ShapeDtypeStruct((8, depth), BF16),
            jax.ShapeDtypeStruct((8, DINNER), F32),
        ],
        compiler_params=params(),
        name="pack",
    )(*small, tokens)


def half_lanes(w, which):
    parts = []
    for k in range(w.shape[1] // 128):
        at = k * 128 + which * HEAD_DIM
        parts.append(w[:, at : at + HEAD_DIM])
    return jnp.concatenate(parts, axis=1)


def convolve(x, weights, bias):
    first = lax.broadcasted_iota(jnp.int32, (8, 1), 0) == 0
    results = []
    for k in range((x.shape[0] - PAD) // SUB):
        at = PAD + k * SUB
        rows = x[at : at + SUB]
        edge = []
        for m in range(1, CONV):
            own = x[at + SUB - 8 * m : at + SUB - 8 * m + 8]
            last = PAD - m if k == 0 else at - 8 * m + 7
            edge.insert(0, jnp.where(first, x[last : last + 1], pltpu.roll(own, 1, 0)))
        summed = bias + weights[CONV - 1 : CONV] * rows
        for m in range(1, CONV):
            moved = jnp.concatenate(edge[CONV - 1 - m :] + [rows[: SUB - 8 * m]], axis=0)
            summed = summed + weights[CONV - 1 - m : CONV - m] * moved
        results.append(silu(summed))
    return results


def state_kernel(
    tok_hbm, halo_ref, w_hbm, wsmall_hbm, par,
    xc_hbm, mine_hbm, bc_hbm, dt_hbm, cum_hbm, skip_hbm, slab_ref,
    raw, tok, w_ref, wsmall, xc_ref, bc_ref, dt_ref, cum_ref, skip_ref,
    wgt, bt, in_sem, out_sem,
):
    rows = tok_hbm.shape[0]
    groups = DINNER // FINE
    half = DINNER
    fetch_tok = start(tok_hbm, raw, in_sem.at[0])
    fetch_small = start(wsmall_hbm, wsmall, in_sem.at[1])
    fetch_w = [
        start(w_hbm.at[:, i * half : (i + 1) * half], w_ref.at[i], in_sem.at[2 + i])
        for i in range(2)
    ]
    tok[0 : PAD - 8] = jnp.zeros((PAD - 8, tok.shape[1]), BF16)
    tok[PAD - 8 : PAD] = halo_ref[...]
    fetch_tok.wait()
    order = reorder()
    for k in range(rows // SUB):
        here = slice(k * SUB, (k + 1) * SUB)
        tok[PAD + k * SUB : PAD + (k + 1) * SUB] = dot(order, raw[here]).astype(BF16)
    fetch_small.wait()
    begin(tok, wsmall, par, bc_ref, dt_ref, cum_ref, wgt, bt)
    sends = [
        start(tok.at[PAD:], mine_hbm, out_sem.at[4]),
        start(bc_ref, bc_hbm, out_sem.at[0]),
        start(dt_ref, dt_hbm, out_sem.at[1]),
        start(cum_ref, cum_hbm, out_sem.at[2]),
    ]

    def project(g):
        at = 2 * g * FINE % half
        w = half_lanes(w_ref[2 * g * FINE // half, :, at : at + 2 * FINE], 1)
        return dot(tok[...], w).astype(BF16).astype(F32)

    wide = par.shape[2]
    for part in range(2):
        fetch_w[part].wait()
        mine_groups = range(part * groups // 2, (part + 1) * groups // 2)
        ahead = project(mine_groups[0])
        for g in mine_groups:
            x = ahead
            if g + 1 in mine_groups:
                ahead = project(g + 1)
            cols = slice(g * FINE, (g + 1) * FINE)
            spread = dot(wgt[...], one_hot(g * FINE, FINE))
            at = g * FINE % wide
            mine = par[g * FINE // wide, :, at : at + FINE]
            blocks = convolve(x, mine[0:CONV], mine[CONV : CONV + 1])
            xc = jnp.concatenate([block.astype(BF16) for block in blocks], axis=0)
            xc_ref[:, cols] = xc
            weighted = (xc.astype(F32) * spread[:rows]).astype(BF16)
            state = dot(bt[...], weighted)
            extra = spread[rows : rows + 8]
            skip_ref[:, cols] = extra
            for i in range(FINE // OWNED):
                own = slice(i * OWNED, (i + 1) * OWNED)
                owner = g * FINE // OWNED + i
                slab_ref[owner, 0:STATE] = state[:, own].astype(BF16)
                slab_ref[owner, STATE : STATE + 8] = extra[:, own].astype(BF16)
            if (g + 1) * FINE % SEND == 0:
                cols = slice((g + 1) * FINE - SEND, (g + 1) * FINE)
                sem = out_sem.at[5 + cols.start // SEND]
                sends.append(start(xc_ref.at[:, cols], xc_hbm.at[:, cols], sem))
    sends.append(start(skip_ref, skip_hbm, out_sem.at[3]))
    for copy in sends:
        copy.wait()


def begin(tok, wsmall_ref, par, bc_ref, dt_ref, cum_ref, wgt, bt):
    rows = dt_ref.shape[0]
    blocks = par.shape[0]
    each = HEADS // blocks
    lane = lax.broadcasted_iota(jnp.int32, (8, 128), 1)
    heads = jnp.zeros((8, 128), F32)
    for k in range(blocks):
        block = par[k, :, 0:128]
        moved = block if k == 0 else pltpu.roll(block, each * k, 1)
        heads = jnp.where(lane // each == k, moved, heads)
    heads = heads[:, :HEADS]
    small = lax.dot_general(
        tok[...], wsmall_ref[...], (((1,), (1,)), ((), ())),
        preferred_element_type=F32,
    )
    small = small.astype(BF16).astype(F32)
    raw = small[PAD:, BC:] + heads[5:6]
    step = jnp.maximum(raw, 0.0) + jnp.log1p(jnp.exp(-jnp.abs(raw)))
    decay = step * -jnp.exp(heads[6:7])
    r = lax.broadcasted_iota(jnp.int32, (SUB, SUB), 0)
    c = lax.broadcasted_iota(jnp.int32, (SUB, SUB), 1)
    ones = (place(r) >= place(c)).astype(F32).astype(BF16)
    before = jnp.zeros((1, HEADS), F32)
    parts = []
    for k in range(rows // SUB):
        three = jnp.concatenate(split3(decay[k * SUB : (k + 1) * SUB]), axis=1)
        sums = dot(ones, three)
        part = before + (
            sums[:, :HEADS] + sums[:, HEADS : 2 * HEADS] + sums[:, 2 * HEADS :]
        )
        before = part[SUB - 1 : SUB]
        parts.append(part)
    cum = jnp.concatenate(parts, axis=0)
    dt_ref[...] = step
    cum_ref[...] = cum
    wgt[0:rows] = hi_lo(step * jnp.exp(before - cum), 1)
    total = hi_lo(jnp.exp(before), 1)
    zero = jnp.zeros((1, HEADS), BF16)
    wgt[rows : rows + 8] = jnp.concatenate(
        [
            jnp.concatenate([total[:, :HEADS], zero], axis=1),
            jnp.concatenate([zero, total[:, HEADS:]], axis=1),
            hi_lo(heads[7:8], 1),
            jnp.zeros((5, 2 * HEADS), BF16),
        ],
        axis=0,
    )
    slots = [bc_slot(k) for k in range(CONV + 1)]
    taps = [par[0, row : row + 1, cols] for row, cols in slots]
    weights = jnp.concatenate(taps[:CONV], axis=0)
    conved = jnp.concatenate(convolve(small[:, :BC], weights, taps[CONV]), axis=0)
    bc_ref[...] = conved.astype(BF16)
    bt[...] = conved.T[:STATE].astype(BF16)


def local_state(tokens, halo, w_gate_x, w_small, packed):
    rows, depth = tokens.shape
    outs = [
        ((rows, DINNER), BF16),
        ((rows, depth), BF16),
        ((rows, BC), BF16),
        ((rows, HEADS), F32),
        ((rows, HEADS), F32),
        ((8, DINNER), F32),
    ]
    return call(
        state_kernel,
        [tokens, on_chip(halo), w_gate_x, w_small, on_chip(packed)],
        outs + [((DINNER // OWNED, STATE + 8, OWNED), BF16)],
        [
            pltpu.VMEM((rows, depth), BF16),
            pltpu.VMEM((PAD + rows, depth), BF16),
            pltpu.VMEM((2, depth, DINNER), BF16),
            pltpu.VMEM(w_small.shape, BF16),
            *(pltpu.VMEM(shape, dtype) for shape, dtype in outs[:1] + outs[2:]),
            pltpu.VMEM((rows + 8, 2 * HEADS), BF16),
            pltpu.VMEM((STATE, rows), BF16),
            pltpu.SemaphoreType.DMA((4,)),
            pltpu.SemaphoreType.DMA((5 + DINNER // SEND,)),
        ],
        "local_state",
        far=(0, 2, 3),
        far_out=range(6),
    )


def prepare(bc_ref, dt_ref, cum_ref, scores, left, rowlog, bt, wgt):
    rows = bc_ref.shape[0]
    heads = WIDTH // HEAD_DIM
    bt[...] = bc_ref[...].astype(F32).T[:STATE].astype(BF16)
    for k in range(rows // SUB):
        here = slice(k * SUB, (k + 1) * SUB)
        scores[here] = dot(bc_ref[here, STATE:], bt[:, here])
    cum = cum_ref[...]
    step = dt_ref[...]
    ones = jnp.ones((rows, HEADS), BF16)
    left[...] = jnp.concatenate(split3(cum * LOG2E) + [ones], axis=1)
    by_row = (jnp.log(jnp.maximum(step, 1e-37)) - cum) * LOG2E
    by_row = jnp.concatenate([p.astype(F32) for p in split3(by_row)] + [cum], axis=1).T
    for g in range(HEADS // heads):
        for p in range(3):
            first = p * HEADS + g * heads
            rowlog[g, p, 0:heads] = by_row[first : first + heads]
    starts, ends = [], []
    before = jnp.zeros((1, HEADS), F32)
    for k in range(rows // SUB):
        starts.append(jnp.broadcast_to(before, (SUB, HEADS)))
        before = cum[(k + 1) * SUB - 1 : (k + 1) * SUB]
        ends.append(jnp.broadcast_to(before, (SUB, HEADS)))
    starts = jnp.concatenate(starts, axis=0)
    ends = jnp.concatenate(ends, axis=0)
    wgt[0:rows] = hi_lo(step * jnp.exp(ends - cum), 1)
    wgt[rows : 2 * rows] = hi_lo(jnp.exp(cum - starts), 1)
    wgt[2 * rows : 3 * rows] = hi_lo(jnp.exp(cum), 1)


def intra_kernel(
    first_group, xc_ref, tok_ref, w_ref, bc_ref, dt_ref, cum_ref, skip_ref,
    own_ref, scale_ref, scores, left, rowlog, bt, wgt,
):
    rows = xc_ref.shape[0]
    blocks = rows // SUB
    heads = WIDTH // HEAD_DIM
    together = xc_ref.shape[1] // WIDTH

    @pl.when(pl.program_id(0) == 0)
    def _():
        prepare(bc_ref, dt_ref, cum_ref, scores, left, rowlog, bt, wgt)

    r = lax.broadcasted_iota(jnp.int32, (SUB, heads * SUB), 0)
    c = lax.broadcasted_iota(jnp.int32, (SUB, heads * SUB), 1)
    causal = place(r) >= place(c % SUB)
    low = lax.broadcasted_iota(jnp.int32, (1, 128), 1) < HEAD_DIM
    pr = lax.broadcasted_iota(jnp.int32, (3 * HEADS, heads * SUB), 0)
    pc = lax.broadcasted_iota(jnp.int32, (3 * HEADS, heads * SUB), 1)
    for i in range(together):
        g = first_group + pl.program_id(0) * together + i
        mine = slice(i * WIDTH, (i + 1) * WIDTH)
        spread = one_hot(g * WIDTH, WIDTH)
        pick = (pr % HEADS == g * heads + pc // SUB).astype(F32).astype(BF16)
        skip = skip_ref[2:3, mine]
        w = half_lanes(w_ref[:, 2 * i * WIDTH : 2 * (i + 1) * WIDTH], 0)
        z = dot(tok_ref[...], w).astype(BF16).astype(F32)
        state = jnp.zeros((STATE, WIDTH), F32)
        for k in range(blocks):
            here = slice(k * SUB, (k + 1) * SUB)
            xc = xc_ref[here, mine]
            late = jnp.concatenate(
                [
                    jnp.concatenate(
                        [rowlog[g, p, h : h + 1, here] for h in range(heads)], axis=1
                    )
                    for p in range(3)
                ]
                + [jnp.zeros((HEADS - 3, heads * SUB), F32)],
                axis=0,
            ).astype(BF16)
            gaps = dot(left[here], jnp.concatenate([pick, late], axis=0))
            decay = jnp.exp2(jnp.where(causal, gaps, -jnp.inf))
            score = scores[here]
            pieces = []
            for pair in range(heads // 2):
                both = [
                    (score * decay[:, h * SUB : (h + 1) * SUB]).astype(BF16)
                    for h in (2 * pair, 2 * pair + 1)
                ]
                x = xc[:, pair * 128 : pair * 128 + 128]
                none = jnp.zeros_like(x)
                right = jnp.concatenate(
                    [jnp.where(low, x, none), jnp.where(low, none, x)], axis=0
                )
                pieces.append(dot(jnp.concatenate(both, axis=1), right))
            y = jnp.concatenate(pieces, axis=1)
            xf = xc.astype(F32)
            grow = dot(wgt[rows + k * SUB : rows + (k + 1) * SUB], spread)
            if k > 0:
                y = y + grow * dot(bc_ref[here, STATE:], state.astype(BF16))
            if k + 1 < blocks:
                shrink = dot(wgt[here], spread)
                fresh = dot(bt[:, here], (xf * shrink).astype(BF16))
                state = state * grow[SUB - 1 : SUB] + fresh
            gate = silu(z[here])
            own_ref[here, mine] = ((y + skip * xf) * gate).astype(own_ref.dtype)
            full = dot(wgt[2 * rows + k * SUB : 2 * rows + (k + 1) * SUB], spread)
            scale_ref[here, mine] = (full * gate).astype(BF16)


def intra(first_group, groups, xc, tokens, w_gate_x, bc, dt, cum, skips):
    rows, depth = tokens.shape
    together = TOGETHER
    group = first_group // together
    wide = together * WIDTH

    def whole(a):
        return pl.BlockSpec(a.shape, lambda i: (0,) * a.ndim)

    return pl.pallas_call(
        functools.partial(intra_kernel, first_group),
        grid=(groups // together,),
        in_specs=[
            pl.BlockSpec((rows, wide), lambda i: (0, i + group)),
            whole(tokens),
            pl.BlockSpec((depth, 2 * wide), lambda i: (0, i + group)),
            whole(bc),
            whole(dt),
            whole(cum),
            pl.BlockSpec((8, wide), lambda i: (0, i + group)),
        ],
        out_specs=[
            pl.BlockSpec((rows, wide), lambda i: (0, i)),
            pl.BlockSpec((rows, wide), lambda i: (0, i)),
        ],
        out_shape=[
            jax.ShapeDtypeStruct((rows, groups * WIDTH), OWN),
            jax.ShapeDtypeStruct((rows, groups * WIDTH), BF16),
        ],
        scratch_shapes=[
            pltpu.VMEM((rows, SUB), F32),
            pltpu.VMEM((rows, 4 * HEADS), BF16),
            pltpu.VMEM((DINNER // WIDTH, 3, 8, rows), F32),
            pltpu.VMEM((STATE, rows), BF16),
            pltpu.VMEM((3 * rows, 2 * HEADS), BF16),
        ],
        compiler_params=params(),
        name="intra",
    )(xc, tokens, w_gate_x, bc, dt, cum, skips)


def through(state, slab):
    slab = slab.astype(F32)
    total = slab[STATE : STATE + 1] + slab[STATE + 1 : STATE + 2]
    return state * total + slab[0:STATE], total


def fold_kernel(in_ref, out_ref):
    state = jnp.zeros((STATE, OWNED), F32)
    whole = jnp.ones((1, OWNED), F32)
    for q in range(in_ref.shape[0]):
        state, total = through(state, in_ref[q])
        whole = whole * total
    hi = whole.astype(BF16).astype(F32)
    row = lax.broadcasted_iota(jnp.int32, (8, OWNED), 0)
    tail = jnp.where(row == 0, hi, jnp.where(row == 1, whole - hi, 0.0))
    state = state.astype(BF16)
    tail = tail.astype(BF16)
    for b in range(out_ref.shape[0]):
        out_ref[b, 0:STATE] = state
        out_ref[b, STATE:] = tail


def fold(near, blocks):
    out = ((blocks, *near.shape[1:]), BF16)
    return call(fold_kernel, [on_chip(near)], [out], [], "fold")[0]


def unfold_kernel(me_ref, near_ref, far_ref, out_ref):
    def earlier(b, state):
        return through(state, far_ref[b])[0]

    state = jnp.zeros((STATE, OWNED), F32)
    state = lax.fori_loop(0, me_ref[0], earlier, state)
    for q in range(near_ref.shape[0]):
        out_ref[q] = state.astype(BF16)
        state, _ = through(state, near_ref[q])


def unfold(me, near, far):
    count = near.shape[0]
    out = ((count, STATE, OWNED), BF16)
    operands = [on_chip(near), on_chip(far)]
    return call(unfold_kernel, operands, [out], [], "unfold", scalars=(me,))[0]


def finish_kernel(parts, bc_hbm, in_ref, gain_hbm, w_hbm, *refs):
    own_hbm, scale_hbm = refs[:parts], refs[parts : 2 * parts]
    out_hbm, bc_ref, gain_ref, w_ref, own_all, scale_all = refs[2 * parts : 2 * parts + 6]
    acc, out_ref, in_sem, w_sem = refs[2 * parts + 6 :]
    rows = bc_hbm.shape[0]
    span = DINNER // CHUNKS
    small = [
        start(bc_hbm, bc_ref, w_sem.at[CHUNKS + rows // SUB]),
        start(gain_hbm, gain_ref, w_sem.at[CHUNKS + rows // SUB + 1]),
    ]
    fetches, fetch_w = [], []
    for k in range(CHUNKS):
        fetches.append([])
        at = 0
        for p in range(parts):
            low, high = max(at, k * span), min(at + own_hbm[p].shape[1], (k + 1) * span)
            if low < high:
                there, here = slice(low - at, high - at), slice(low, high)
                pairs = ((own_hbm[p], own_all), (scale_hbm[p], scale_all))
                for i, (hbm, ref) in enumerate(pairs):
                    source, target = hbm.at[:, there], ref.at[:, here]
                    fetches[k].append(start(source, target, in_sem.at[k, p, i]))
            at += own_hbm[p].shape[1]
        part = slice(k * span, (k + 1) * span)
        fetch_w.append(start(w_hbm.at[part], w_ref.at[part], w_sem.at[k]))

    def gate(k, total):
        sides = []
        for g in range(k * span // WIDTH, (k + 1) * span // WIDTH):
            cols = slice(g * WIDTH, (g + 1) * WIDTH)
            slabs = [in_ref[2 * g], in_ref[2 * g + 1]]
            carried = dot(bc_ref[:, STATE:], jnp.concatenate(slabs, axis=1))
            scale = scale_all[:, cols].astype(F32)
            gated = own_all[:, cols].astype(F32) + scale * carried
            gated = gated.astype(BF16).astype(F32)
            square = gated * gated
            total = total + square[:, :128] + square[:, 128:]
            sides.append((gated * gain_ref[0:1, cols]).astype(BF16))
        return jnp.concatenate(sides, axis=1), total

    total = jnp.zeros((rows, 128), F32)
    for copy in small:
        copy.wait()
    for k in range(CHUNKS):
        for copy in fetches[k]:
            copy.wait()
        side, total = gate(k, total)
        fetch_w[k].wait()
        product = dot(side, w_ref[k * span : (k + 1) * span])
        if k > 0:
            product = acc[...] + product
        if k + 1 < CHUNKS:
            acc[...] = product
    mean = jnp.sum(total, axis=1, keepdims=True) * (1.0 / DINNER)
    product = (product * lax.rsqrt(mean + EPSILON)).astype(BF16)
    order = reorder(back=True)
    sends = []
    for k in range(rows // SUB):
        here = slice(k * SUB, (k + 1) * SUB)
        out_ref[here] = dot(order, product[here]).astype(BF16)
        sends.append(start(out_ref.at[here], out_hbm.at[here], w_sem.at[CHUNKS + k]))
    for copy in sends:
        copy.wait()


def finish(bc, incoming, owns, scales, gain, w_out):
    rows = bc.shape[0]
    columns = w_out.shape[1]
    parts = len(owns)
    return call(
        functools.partial(finish_kernel, parts),
        [bc, on_chip(incoming), gain, w_out, *owns, *scales],
        [((rows, columns), BF16)],
        [
            pltpu.VMEM(bc.shape, BF16),
            pltpu.VMEM(gain.shape, F32),
            pltpu.VMEM(w_out.shape, BF16),
            pltpu.VMEM((rows, DINNER), OWN),
            pltpu.VMEM((rows, DINNER), BF16),
            pltpu.VMEM((rows, columns), F32),
            pltpu.VMEM((rows, columns), BF16),
            pltpu.SemaphoreType.DMA((CHUNKS, parts, 2)),
            pltpu.SemaphoreType.DMA((CHUNKS + rows // SUB + 2,)),
        ],
        "finish",
        far=(0, *range(2, 4 + 2 * parts)),
        far_out=(0,),
    )[0]


def on_device(
    tokens, w_gate_x, w_bc_dt, conv_x_weight, conv_x_bias, conv_bc_weight,
    conv_bc_bias, dt_bias, a_log, skip_d, norm_gain, w_out,
):
    n = lax.axis_size("head")
    blocks = lax.axis_size(FAR)
    devices = blocks * lax.axis_size(NEAR)
    my_block = lax.axis_index(FAR)[None]
    small = [conv_x_weight, conv_x_bias, dt_bias, a_log, skip_d]
    small += [conv_bc_weight, conv_bc_bias, norm_gain]
    packed, tail, gain = pack(small, tokens, n)
    packed = lax.all_to_all(packed, "head", 0, 0, tiled=True)
    halo = lax.ppermute(tail, BOTH, [(i, i + 1) for i in range(devices - 1)])
    xc, mine, bc, dt, cum, skips, slabs = local_state(
        tokens, halo, w_gate_x, w_bc_dt.T, packed
    )
    near = lax.all_to_all(slabs, NEAR, 0, 0, tiled=True)
    rest = (bc, dt, cum, skips)
    first, second, third = SPLIT
    own0, scale0 = intra(0, first, xc, mine, w_gate_x, *rest)
    near, own0 = lax.optimization_barrier((near, own0))
    copies = fold(near, blocks)
    far = lax.all_to_all(copies, FAR, 0, 0, tiled=True)
    xc, copies = lax.optimization_barrier((xc, copies))
    own1, scale1 = intra(first, second, xc, mine, w_gate_x, *rest)
    far, own1 = lax.optimization_barrier((far, own1))
    incoming = unfold(my_block, near, far)
    back = lax.all_to_all(incoming, NEAR, 0, 0, tiled=True)
    xc, incoming = lax.optimization_barrier((xc, incoming))
    own2, scale2 = intra(first + second, third, xc, mine, w_gate_x, *rest)
    owns, scales = (own0, own1, own2), (scale0, scale1, scale2)
    return finish(bc, back, owns, scales, gain, w_out)


def solution(mesh):
    seq, head = mesh.devices.shape
    split = Mesh(mesh.devices.reshape(seq // 4, 2, 2, head), BOTH)
    return jax.shard_map(
        on_device,
        mesh=split,
        in_specs=(
            P(BOTH, None),
            P(),
            P(),
            P(None, "head"),
            P("head"),
            P(),
            P(),
            P("head"),
            P("head"),
            P("head"),
            P(),
            P(),
        ),
        out_specs=P(BOTH, None),
        check_vma=False,
    )
```

```python
import functools

import jax
import jax.numpy as jnp
from jax import lax
from jax.experimental import pallas as pl
from jax.experimental.pallas import tpu as pltpu
from jax.sharding import Mesh
from jax.sharding import PartitionSpec as P

HEADS = 32
HEAD_DIM = 64
STATE = 64
CONV = 4
DINNER = HEADS * HEAD_DIM
BC = 2 * STATE
SUB = 128
PAD = 16
EPSILON = 1e-05
FAR = "chips"
NEAR = ("row", "core", "head")
BOTH = (FAR, *NEAR)
WIDTH = 256
OWNED = 128
TOGETHER = 1
SPLIT = (3, 3, 2)
FINE = 256
SEND = 512
CHUNKS = 2
F32 = jnp.float32
BF16 = jnp.bfloat16
OWN = jnp.bfloat16
LIMIT = 60 * 1024 * 1024
LOG2E = 1.4426950408889634
FAR_AWAY = pl.BlockSpec(memory_space=pltpu.HBM)
HERE = pl.BlockSpec(memory_space=pltpu.VMEM)


def params(steps=1):
    return pltpu.CompilerParams(
        dimension_semantics=("arbitrary",) * steps, vmem_limit_bytes=LIMIT
    )


def silu(v):
    half = 0.5 * v
    return half + half * jnp.tanh(half)


def hi_lo(v, axis):
    hi = v.astype(BF16)
    lo = (v - hi.astype(F32)).astype(BF16)
    return jnp.concatenate([hi, lo], axis=axis)


def dot(a, b):
    return jnp.dot(a, b, preferred_element_type=F32)


def split3(v):
    hi = v.astype(BF16)
    rest = v - hi.astype(F32)
    mid = rest.astype(BF16)
    return [hi, mid, (rest - mid.astype(F32)).astype(BF16)]


def call(kernel, args, outs, scratch, name, far=(), far_out=(), near_out=(), scalars=()):
    specs = [pl.BlockSpec(memory_space=pltpu.SMEM)] * len(scalars)
    specs += [FAR_AWAY if i in far else pl.BlockSpec() for i in range(len(args))]
    return pl.pallas_call(
        kernel,
        in_specs=specs,
        out_specs=[
            FAR_AWAY if i in far_out else HERE if i in near_out else pl.BlockSpec()
            for i in range(len(outs))
        ],
        out_shape=[
            pltpu.VMEM(*out) if i in near_out else jax.ShapeDtypeStruct(*out)
            for i, out in enumerate(outs)
        ],
        scratch_shapes=scratch,
        compiler_params=params(0),
        name=name,
    )(*scalars, *args)


def start(source, target, sem):
    copy = pltpu.make_async_copy(source, target, sem)
    copy.start()
    return copy


def on_chip(array):
    return pltpu.with_memory_space_constraint(array, pltpu.VMEM)


def place(r):
    return r // 8 + SUB // 8 * (r % 8)


def reorder(back=False):
    r = lax.broadcasted_iota(jnp.int32, (SUB, SUB), 1 if back else 0)
    c = lax.broadcasted_iota(jnp.int32, (SUB, SUB), 0 if back else 1)
    return (place(r) == c).astype(F32).astype(BF16)


def one_hot(first_channel, width):
    row = lax.broadcasted_iota(jnp.int32, (2 * HEADS, width), 0)
    chan = lax.broadcasted_iota(jnp.int32, (2 * HEADS, width), 1) + first_channel
    return ((row % HEADS) == (chan // HEAD_DIM)).astype(F32).astype(BF16)


def pack_kernel(w_ref, b_ref, dt_ref, a_ref, skip_ref, wbc_ref, bbc_ref, gain_ref,
                tok_ref, out_ref, tail_ref, gain_out):
    out_ref[...] = jnp.zeros_like(out_ref)
    here = dt_ref.shape[1]
    for k in range(out_ref.shape[0]):
        out_ref[k, 0:CONV] = w_ref[...]
        out_ref[k, CONV : CONV + 1] = b_ref[...]
        for row, ref in ((5, dt_ref), (6, a_ref), (7, skip_ref)):
            out_ref[k, row : row + 1, 0:here] = ref[...]
        for tap in range(CONV):
            row, cols = bc_slot(tap)
            out_ref[k, row : row + 1, cols] = wbc_ref[tap : tap + 1]
        row, cols = bc_slot(CONV)
        out_ref[k, row : row + 1, cols] = bbc_ref[...]
    tail_ref[...] = tok_ref[...]
    gain_out[...] = jnp.broadcast_to(gain_ref[...], gain_out.shape)


def bc_slot(k):
    at = 128 * (1 + k % 3)
    return 5 + k // 3, slice(at, at + BC)


def pack(small, tokens, copies):
    rows, depth = tokens.shape
    small = [a if a.ndim == 2 else a[None] for a in small]
    wide = small[0].shape[1]

    def whole(a):
        return pl.BlockSpec(a.shape, lambda g: (0, 0))

    return pl.pallas_call(
        pack_kernel,
        grid=(1,),
        in_specs=[whole(a) for a in small]
        + [pl.BlockSpec((8, depth), lambda g: (rows // 8 - 1, 0))],
        out_specs=[
            pl.BlockSpec((copies, 8, wide), lambda g: (0, 0, 0)),
            pl.BlockSpec((8, depth), lambda g: (0, 0)),
            pl.BlockSpec((8, DINNER), lambda g: (0, 0)),
        ],
        out_shape=[
            jax.ShapeDtypeStruct((copies, 8, wide), F32),
            jax.ShapeDtypeStruct((8, depth), BF16),
            jax.ShapeDtypeStruct((8, DINNER), F32),
        ],
        compiler_params=params(),
        name="pack",
    )(*small, tokens)


def half_lanes(w, which):
    parts = []
    for k in range(w.shape[1] // 128):
        at = k * 128 + which * HEAD_DIM
        parts.append(w[:, at : at + HEAD_DIM])
    return jnp.concatenate(parts, axis=1)


def convolve(x, weights, bias):
    first = lax.broadcasted_iota(jnp.int32, (8, 1), 0) == 0
    results = []
    for k in range((x.shape[0] - PAD) // SUB):
        at = PAD + k * SUB
        rows = x[at : at + SUB]
        edge = []
        for m in range(1, CONV):
            own = x[at + SUB - 8 * m : at + SUB - 8 * m + 8]
            last = PAD - m if k == 0 else at - 8 * m + 7
            edge.insert(0, jnp.where(first, x[last : last + 1], pltpu.roll(own, 1, 0)))
        summed = bias + weights[CONV - 1 : CONV] * rows
        for m in range(1, CONV):
            moved = jnp.concatenate(edge[CONV - 1 - m :] + [rows[: SUB - 8 * m]], axis=0)
            summed = summed + weights[CONV - 1 - m : CONV - m] * moved
        results.append(silu(summed))
    return results


def state_kernel(
    tok_hbm, halo_ref, w_hbm, wsmall_hbm, par,
    xc_hbm, mine_hbm, bc_hbm, dt_hbm, cum_hbm, skip_hbm, slab_ref,
    raw, tok, w_ref, wsmall, xc_ref, bc_ref, dt_ref, cum_ref, skip_ref,
    wgt, bt, in_sem, out_sem,
):
    rows = tok_hbm.shape[0]
    groups = DINNER // FINE
    half = DINNER
    fetch_tok = start(tok_hbm, raw, in_sem.at[0])
    fetch_small = start(wsmall_hbm, wsmall, in_sem.at[1])
    fetch_w = [
        start(w_hbm.at[:, i * half : (i + 1) * half], w_ref.at[i], in_sem.at[2 + i])
        for i in range(2)
    ]
    tok[0 : PAD - 8] = jnp.zeros((PAD - 8, tok.shape[1]), BF16)
    tok[PAD - 8 : PAD] = halo_ref[...]
    fetch_tok.wait()
    order = reorder()
    for k in range(rows // SUB):
        here = slice(k * SUB, (k + 1) * SUB)
        tok[PAD + k * SUB : PAD + (k + 1) * SUB] = dot(order, raw[here]).astype(BF16)
    fetch_small.wait()
    begin(tok, wsmall, par, bc_ref, dt_ref, cum_ref, wgt, bt)
    sends = [
        start(tok.at[PAD:], mine_hbm, out_sem.at[4]),
        start(bc_ref, bc_hbm, out_sem.at[0]),
        start(dt_ref, dt_hbm, out_sem.at[1]),
        start(cum_ref, cum_hbm, out_sem.at[2]),
    ]

    def project(g):
        at = 2 * g * FINE % half
        w = half_lanes(w_ref[2 * g * FINE // half, :, at : at + 2 * FINE], 1)
        return dot(tok[...], w).astype(BF16).astype(F32)

    wide = par.shape[2]
    for part in range(2):
        fetch_w[part].wait()
        mine_groups = range(part * groups // 2, (part + 1) * groups // 2)
        ahead = project(mine_groups[0])
        for g in mine_groups:
            x = ahead
            if g + 1 in mine_groups:
                ahead = project(g + 1)
            cols = slice(g * FINE, (g + 1) * FINE)
            spread = dot(wgt[...], one_hot(g * FINE, FINE))
            at = g * FINE % wide
            mine = par[g * FINE // wide, :, at : at + FINE]
            blocks = convolve(x, mine[0:CONV], mine[CONV : CONV + 1])
            xc = jnp.concatenate([block.astype(BF16) for block in blocks], axis=0)
            xc_ref[:, cols] = xc
            weighted = (xc.astype(F32) * spread[:rows]).astype(BF16)
            state = dot(bt[...], weighted)
            extra = spread[rows : rows + 8]
            skip_ref[:, cols] = extra
            for i in range(FINE // OWNED):
                own = slice(i * OWNED, (i + 1) * OWNED)
                owner = g * FINE // OWNED + i
                slab_ref[owner, 0:STATE] = state[:, own].astype(BF16)
                slab_ref[owner, STATE : STATE + 8] = extra[:, own].astype(BF16)
            if (g + 1) * FINE % SEND == 0:
                cols = slice((g + 1) * FINE - SEND, (g + 1) * FINE)
                sem = out_sem.at[5 + cols.start // SEND]
                sends.append(start(xc_ref.at[:, cols], xc_hbm.at[:, cols], sem))
    sends.append(start(skip_ref, skip_hbm, out_sem.at[3]))
    for copy in sends:
        copy.wait()


def begin(tok, wsmall_ref, par, bc_ref, dt_ref, cum_ref, wgt, bt):
    rows = dt_ref.shape[0]
    blocks = par.shape[0]
    each = HEADS // blocks
    lane = lax.broadcasted_iota(jnp.int32, (8, 128), 1)
    heads = jnp.zeros((8, 128), F32)
    for k in range(blocks):
        block = par[k, :, 0:128]
        moved = block if k == 0 else pltpu.roll(block, each * k, 1)
        heads = jnp.where(lane // each == k, moved, heads)
    heads = heads[:, :HEADS]
    small = lax.dot_general(
        tok[...], wsmall_ref[...], (((1,), (1,)), ((), ())),
        preferred_element_type=F32,
    )
    small = small.astype(BF16).astype(F32)
    raw = small[PAD:, BC:] + heads[5:6]
    step = jnp.maximum(raw, 0.0) + jnp.log1p(jnp.exp(-jnp.abs(raw)))
    decay = step * -jnp.exp(heads[6:7])
    r = lax.broadcasted_iota(jnp.int32, (SUB, SUB), 0)
    c = lax.broadcasted_iota(jnp.int32, (SUB, SUB), 1)
    ones = (place(r) >= place(c)).astype(F32).astype(BF16)
    before = jnp.zeros((1, HEADS), F32)
    parts = []
    for k in range(rows // SUB):
        three = jnp.concatenate(split3(decay[k * SUB : (k + 1) * SUB]), axis=1)
        sums = dot(ones, three)
        part = before + (
            sums[:, :HEADS] + sums[:, HEADS : 2 * HEADS] + sums[:, 2 * HEADS :]
        )
        before = part[SUB - 1 : SUB]
        parts.append(part)
    cum = jnp.concatenate(parts, axis=0)
    dt_ref[...] = step
    cum_ref[...] = cum
    wgt[0:rows] = hi_lo(step * jnp.exp(before - cum), 1)
    total = hi_lo(jnp.exp(before), 1)
    zero = jnp.zeros((1, HEADS), BF16)
    wgt[rows : rows + 8] = jnp.concatenate(
        [
            jnp.concatenate([total[:, :HEADS], zero], axis=1),
            jnp.concatenate([zero, total[:, HEADS:]], axis=1),
            hi_lo(heads[7:8], 1),
            jnp.zeros((5, 2 * HEADS), BF16),
        ],
        axis=0,
    )
    slots = [bc_slot(k) for k in range(CONV + 1)]
    taps = [par[0, row : row + 1, cols] for row, cols in slots]
    weights = jnp.concatenate(taps[:CONV], axis=0)
    conved = jnp.concatenate(convolve(small[:, :BC], weights, taps[CONV]), axis=0)
    bc_ref[...] = conved.astype(BF16)
    bt[...] = conved.T[:STATE].astype(BF16)


def local_state(tokens, halo, w_gate_x, w_small, packed):
    rows, depth = tokens.shape
    outs = [
        ((rows, DINNER), BF16),
        ((rows, depth), BF16),
        ((rows, BC), BF16),
        ((rows, HEADS), F32),
        ((rows, HEADS), F32),
        ((8, DINNER), F32),
    ]
    return call(
        state_kernel,
        [tokens, on_chip(halo), w_gate_x, w_small, on_chip(packed)],
        outs + [((DINNER // OWNED, STATE + 8, OWNED), BF16)],
        [
            pltpu.VMEM((rows, depth), BF16),
            pltpu.VMEM((PAD + rows, depth), BF16),
            pltpu.VMEM((2, depth, DINNER), BF16),
            pltpu.VMEM(w_small.shape, BF16),
            *(pltpu.VMEM(shape, dtype) for shape, dtype in outs[:1] + outs[2:]),
            pltpu.VMEM((rows + 8, 2 * HEADS), BF16),
            pltpu.VMEM((STATE, rows), BF16),
            pltpu.SemaphoreType.DMA((4,)),
            pltpu.SemaphoreType.DMA((5 + DINNER // SEND,)),
        ],
        "local_state",
        far=(0, 2, 3),
        far_out=range(6),
        near_out=(6,),
    )


def prepare(bc_ref, dt_ref, cum_ref, scores, left, rowlog, bt, wgt):
    rows = bc_ref.shape[0]
    heads = WIDTH // HEAD_DIM
    bt[...] = bc_ref[...].astype(F32).T[:STATE].astype(BF16)
    for k in range(rows // SUB):
        here = slice(k * SUB, (k + 1) * SUB)
        scores[here] = dot(bc_ref[here, STATE:], bt[:, here])
    cum = cum_ref[...]
    step = dt_ref[...]
    ones = jnp.ones((rows, HEADS), BF16)
    starts, ends = [], []
    before = jnp.zeros((1, HEADS), F32)
    for k in range(rows // SUB):
        starts.append(jnp.broadcast_to(before, (SUB, HEADS)))
        before = cum[(k + 1) * SUB - 1 : (k + 1) * SUB]
        ends.append(jnp.broadcast_to(before, (SUB, HEADS)))
    starts = jnp.concatenate(starts, axis=0)
    ends = jnp.concatenate(ends, axis=0)
    passed = cum - starts
    left[...] = jnp.concatenate(split3(passed * LOG2E) + [ones], axis=1)
    by_row = (jnp.log(jnp.maximum(step, 1e-37)) - passed) * LOG2E
    by_row = jnp.concatenate([p.astype(F32) for p in split3(by_row)] + [cum], axis=1).T
    for g in range(HEADS // heads):
        for p in range(3):
            first = p * HEADS + g * heads
            rowlog[g, p, 0:heads] = by_row[first : first + heads]
    wgt[0:rows] = hi_lo(step * jnp.exp(ends - cum), 1)
    wgt[rows : 2 * rows] = hi_lo(jnp.exp(passed), 1)
    wgt[2 * rows : 3 * rows] = hi_lo(jnp.exp(cum), 1)


def intra_kernel(
    first_group, xc_ref, tok_ref, w_ref, bc_ref, dt_ref, cum_ref, skip_ref,
    own_ref, scale_ref, scores, left, rowlog, bt, wgt,
):
    rows = xc_ref.shape[0]
    blocks = rows // SUB
    heads = WIDTH // HEAD_DIM
    together = xc_ref.shape[1] // WIDTH

    @pl.when(pl.program_id(0) == 0)
    def _():
        prepare(bc_ref, dt_ref, cum_ref, scores, left, rowlog, bt, wgt)

    r = lax.broadcasted_iota(jnp.int32, (SUB, heads * SUB), 0)
    c = lax.broadcasted_iota(jnp.int32, (SUB, heads * SUB), 1)
    causal = place(r) >= place(c % SUB)
    low = lax.broadcasted_iota(jnp.int32, (1, 128), 1) < HEAD_DIM
    pr = lax.broadcasted_iota(jnp.int32, (3 * HEADS, heads * SUB), 0)
    pc = lax.broadcasted_iota(jnp.int32, (3 * HEADS, heads * SUB), 1)
    for i in range(together):
        g = first_group + pl.program_id(0) * together + i
        mine = slice(i * WIDTH, (i + 1) * WIDTH)
        expanded = dot(wgt[...], one_hot(g * WIDTH, WIDTH))
        pick = (pr % HEADS == g * heads + pc // SUB).astype(F32).astype(BF16)
        skip = skip_ref[2:3, mine]
        w = half_lanes(w_ref[:, 2 * i * WIDTH : 2 * (i + 1) * WIDTH], 0)
        z = dot(tok_ref[...], w).astype(BF16).astype(F32)
        state = jnp.zeros((STATE, WIDTH), F32)
        for k in range(blocks):
            here = slice(k * SUB, (k + 1) * SUB)
            xc = xc_ref[here, mine]
            late = jnp.concatenate(
                [
                    jnp.concatenate(
                        [rowlog[g, p, h : h + 1, here] for h in range(heads)], axis=1
                    )
                    for p in range(3)
                ]
                + [jnp.zeros((HEADS - 3, heads * SUB), F32)],
                axis=0,
            ).astype(BF16)
            gaps = dot(left[here], jnp.concatenate([pick, late], axis=0))
            decay = jnp.exp2(jnp.where(causal, gaps, -jnp.inf))
            score = scores[here]
            pieces = []
            for pair in range(heads // 2):
                both = [
                    (score * decay[:, h * SUB : (h + 1) * SUB]).astype(BF16)
                    for h in (2 * pair, 2 * pair + 1)
                ]
                x = xc[:, pair * 128 : pair * 128 + 128]
                none = jnp.zeros_like(x)
                right = jnp.concatenate(
                    [jnp.where(low, x, none), jnp.where(low, none, x)], axis=0
                )
                pieces.append(dot(jnp.concatenate(both, axis=1), right))
            y = jnp.concatenate(pieces, axis=1)
            xf = xc.astype(F32)
            grow = expanded[rows + k * SUB : rows + (k + 1) * SUB]
            if k > 0:
                y = y + grow * dot(bc_ref[here, STATE:], state.astype(BF16))
            if k + 1 < blocks:
                shrink = expanded[here]
                fresh = dot(bt[:, here], (xf * shrink).astype(BF16))
                state = state * grow[SUB - 1 : SUB] + fresh
            gate = silu(z[here])
            own_ref[here, mine] = ((y + skip * xf) * gate).astype(own_ref.dtype)
            full = expanded[2 * rows + k * SUB : 2 * rows + (k + 1) * SUB]
            scale_ref[here, mine] = (full * gate).astype(BF16)


def intra(first_group, groups, xc, tokens, w_gate_x, bc, dt, cum, skips):
    rows, depth = tokens.shape
    together = TOGETHER
    group = first_group // together
    wide = together * WIDTH

    def whole(a):
        return pl.BlockSpec(a.shape, lambda i: (0,) * a.ndim)

    return pl.pallas_call(
        functools.partial(intra_kernel, first_group),
        grid=(groups // together,),
        in_specs=[
            pl.BlockSpec((rows, wide), lambda i: (0, i + group)),
            whole(tokens),
            pl.BlockSpec((depth, 2 * wide), lambda i: (0, i + group)),
            whole(bc),
            whole(dt),
            whole(cum),
            pl.BlockSpec((8, wide), lambda i: (0, i + group)),
        ],
        out_specs=[
            pl.BlockSpec((rows, wide), lambda i: (0, i)),
            pl.BlockSpec((rows, wide), lambda i: (0, i)),
        ],
        out_shape=[
            jax.ShapeDtypeStruct((rows, groups * WIDTH), OWN),
            jax.ShapeDtypeStruct((rows, groups * WIDTH), BF16),
        ],
        scratch_shapes=[
            pltpu.VMEM((rows, SUB), F32),
            pltpu.VMEM((rows, 4 * HEADS), BF16),
            pltpu.VMEM((DINNER // WIDTH, 3, 8, rows), F32),
            pltpu.VMEM((STATE, rows), BF16),
            pltpu.VMEM((3 * rows, 2 * HEADS), BF16),
        ],
        compiler_params=params(),
        name="intra",
    )(xc, tokens, w_gate_x, bc, dt, cum, skips)


def through(state, slab):
    slab = slab.astype(F32)
    total = slab[STATE : STATE + 1] + slab[STATE + 1 : STATE + 2]
    return state * total + slab[0:STATE], total


def fold_kernel(in_ref, out_ref):
    state = jnp.zeros((STATE, OWNED), F32)
    whole = jnp.ones((1, OWNED), F32)
    for q in range(in_ref.shape[0]):
        state, total = through(state, in_ref[q])
        whole = whole * total
    hi = whole.astype(BF16).astype(F32)
    row = lax.broadcasted_iota(jnp.int32, (8, OWNED), 0)
    tail = jnp.where(row == 0, hi, jnp.where(row == 1, whole - hi, 0.0))
    state = state.astype(BF16)
    tail = tail.astype(BF16)
    for b in range(out_ref.shape[0]):
        out_ref[b, 0:STATE] = state
        out_ref[b, STATE:] = tail


def fold(near, blocks):
    out = ((blocks, *near.shape[1:]), BF16)
    return call(fold_kernel, [on_chip(near)], [out], [], "fold", near_out=(0,))[0]


def unfold_kernel(me_ref, near_ref, far_ref, out_ref):
    def earlier(b, state):
        return through(state, far_ref[b])[0]

    state = jnp.zeros((STATE, OWNED), F32)
    state = lax.fori_loop(0, me_ref[0], earlier, state)
    for q in range(near_ref.shape[0]):
        out_ref[q] = state.astype(BF16)
        state, _ = through(state, near_ref[q])


def unfold(me, near, far):
    count = near.shape[0]
    out = ((count, STATE, OWNED), BF16)
    operands = [on_chip(near), on_chip(far)]
    return call(
        unfold_kernel, operands, [out], [], "unfold", near_out=(0,), scalars=(me,)
    )[0]


def finish_kernel(parts, bc_hbm, in_ref, gain_hbm, w_hbm, *refs):
    own_hbm, scale_hbm = refs[:parts], refs[parts : 2 * parts]
    out_hbm, bc_ref, gain_ref, w_ref, own_all, scale_all = refs[2 * parts : 2 * parts + 6]
    acc, out_ref, in_sem, w_sem = refs[2 * parts + 6 :]
    rows = bc_hbm.shape[0]
    span = DINNER // CHUNKS
    small = [
        start(bc_hbm, bc_ref, w_sem.at[CHUNKS + rows // SUB]),
        start(gain_hbm, gain_ref, w_sem.at[CHUNKS + rows // SUB + 1]),
    ]
    fetches, fetch_w = [], []
    for k in range(CHUNKS):
        fetches.append([])
        at = 0
        for p in range(parts):
            low, high = max(at, k * span), min(at + own_hbm[p].shape[1], (k + 1) * span)
            if low < high:
                there, here = slice(low - at, high - at), slice(low, high)
                pairs = ((own_hbm[p], own_all), (scale_hbm[p], scale_all))
                for i, (hbm, ref) in enumerate(pairs):
                    source, target = hbm.at[:, there], ref.at[:, here]
                    fetches[k].append(start(source, target, in_sem.at[k, p, i]))
            at += own_hbm[p].shape[1]
        part = slice(k * span, (k + 1) * span)
        fetch_w.append(start(w_hbm.at[part], w_ref.at[part], w_sem.at[k]))

    def gate(k, total):
        sides = []
        for g in range(k * span // WIDTH, (k + 1) * span // WIDTH):
            cols = slice(g * WIDTH, (g + 1) * WIDTH)
            slabs = [in_ref[2 * g], in_ref[2 * g + 1]]
            carried = dot(bc_ref[:, STATE:], jnp.concatenate(slabs, axis=1))
            scale = scale_all[:, cols].astype(F32)
            gated = own_all[:, cols].astype(F32) + scale * carried
            gated = gated.astype(BF16).astype(F32)
            square = gated * gated
            total = total + square[:, :128] + square[:, 128:]
            sides.append((gated * gain_ref[0:1, cols]).astype(BF16))
        return jnp.concatenate(sides, axis=1), total

    total = jnp.zeros((rows, 128), F32)
    for copy in small:
        copy.wait()
    for k in range(CHUNKS):
        for copy in fetches[k]:
            copy.wait()
        side, total = gate(k, total)
        fetch_w[k].wait()
        product = dot(side, w_ref[k * span : (k + 1) * span])
        if k > 0:
            product = acc[...] + product
        if k + 1 < CHUNKS:
            acc[...] = product
    mean = jnp.sum(total, axis=1, keepdims=True) * (1.0 / DINNER)
    product = (product * lax.rsqrt(mean + EPSILON)).astype(BF16)
    order = reorder(back=True)
    sends = []
    for k in range(rows // SUB):
        here = slice(k * SUB, (k + 1) * SUB)
        out_ref[here] = dot(order, product[here]).astype(BF16)
        sends.append(start(out_ref.at[here], out_hbm.at[here], w_sem.at[CHUNKS + k]))
    for copy in sends:
        copy.wait()


def finish(bc, incoming, owns, scales, gain, w_out):
    rows = bc.shape[0]
    columns = w_out.shape[1]
    parts = len(owns)
    return call(
        functools.partial(finish_kernel, parts),
        [bc, on_chip(incoming), gain, w_out, *owns, *scales],
        [((rows, columns), BF16)],
        [
            pltpu.VMEM(bc.shape, BF16),
            pltpu.VMEM(gain.shape, F32),
            pltpu.VMEM(w_out.shape, BF16),
            pltpu.VMEM((rows, DINNER), OWN),
            pltpu.VMEM((rows, DINNER), BF16),
            pltpu.VMEM((rows, columns), F32),
            pltpu.VMEM((rows, columns), BF16),
            pltpu.SemaphoreType.DMA((CHUNKS, parts, 2)),
            pltpu.SemaphoreType.DMA((CHUNKS + rows // SUB + 2,)),
        ],
        "finish",
        far=(0, *range(2, 4 + 2 * parts)),
        far_out=(0,),
    )[0]


def on_device(
    tokens, w_gate_x, w_bc_dt, conv_x_weight, conv_x_bias, conv_bc_weight,
    conv_bc_bias, dt_bias, a_log, skip_d, norm_gain, w_out,
):
    n = lax.axis_size("head")
    blocks = lax.axis_size(FAR)
    devices = blocks * lax.axis_size(NEAR)
    my_block = lax.axis_index(FAR)[None]
    small = [conv_x_weight, conv_x_bias, dt_bias, a_log, skip_d]
    small += [conv_bc_weight, conv_bc_bias, norm_gain]
    packed, tail, gain = pack(small, tokens, n)
    packed = lax.all_to_all(packed, "head", 0, 0, tiled=True)
    halo = lax.ppermute(tail, BOTH, [(i, i + 1) for i in range(devices - 1)])
    xc, mine, bc, dt, cum, skips, slabs = local_state(
        tokens, halo, w_gate_x, w_bc_dt.T, packed
    )
    near = lax.all_to_all(slabs, NEAR, 0, 0, tiled=True)
    rest = (bc, dt, cum, skips)
    first, second, third = SPLIT
    own0, scale0 = intra(0, first, xc, mine, w_gate_x, *rest)
    near, own0 = lax.optimization_barrier((near, own0))
    copies = fold(near, blocks)
    far = lax.all_to_all(copies, FAR, 0, 0, tiled=True)
    xc, copies = lax.optimization_barrier((xc, copies))
    own1, scale1 = intra(first, second, xc, mine, w_gate_x, *rest)
    far, own1 = lax.optimization_barrier((far, own1))
    incoming = unfold(my_block, near, far)
    back = lax.all_to_all(incoming, NEAR, 0, 0, tiled=True)
    xc, incoming = lax.optimization_barrier((xc, incoming))
    own2, scale2 = intra(first + second, third, xc, mine, w_gate_x, *rest)
    owns, scales = (own0, own1, own2), (scale0, scale1, scale2)
    return finish(bc, back, owns, scales, gain, w_out)


def solution(mesh):
    seq, head = mesh.devices.shape
    split = Mesh(mesh.devices.reshape(seq // 4, 2, 2, head), BOTH)
    return jax.shard_map(
        on_device,
        mesh=split,
        in_specs=(
            P(BOTH, None),
            P(),
            P(),
            P(None, "head"),
            P("head"),
            P(),
            P(),
            P("head"),
            P("head"),
            P("head"),
            P(),
            P(),
        ),
        out_specs=P(BOTH, None),
        check_vma=False,
    )
```

```python
import functools

import jax
import jax.numpy as jnp
from jax import lax
from jax.experimental import pallas as pl
from jax.experimental.pallas import tpu as pltpu
from jax.sharding import Mesh
from jax.sharding import PartitionSpec as P

HEADS = 32
HEAD_DIM = 64
STATE = 64
CONV = 4
DINNER = HEADS * HEAD_DIM
BC = 2 * STATE
SUB = 128
PAD = 16
EPSILON = 1e-05
FAR = "chips"
NEAR = ("row", "core", "head")
BOTH = (FAR, *NEAR)
WIDTH = 256
OWNED = 128
TOGETHER = 1
SPLIT = (3, 3, 2)
FINE = 256
SEND = 512
CHUNKS = 2
F32 = jnp.float32
BF16 = jnp.bfloat16
OWN = jnp.bfloat16
LIMIT = 60 * 1024 * 1024
LOG2E = 1.4426950408889634
FAR_AWAY = pl.BlockSpec(memory_space=pltpu.HBM)
HERE = pl.BlockSpec(memory_space=pltpu.VMEM)


def params(steps=1):
    return pltpu.CompilerParams(
        dimension_semantics=("arbitrary",) * steps, vmem_limit_bytes=LIMIT
    )


def silu(v):
    half = 0.5 * v
    return half + half * jnp.tanh(half)


def hi_lo(v, axis):
    hi = v.astype(BF16)
    lo = (v - hi.astype(F32)).astype(BF16)
    return jnp.concatenate([hi, lo], axis=axis)


def dot(a, b):
    return jnp.dot(a, b, preferred_element_type=F32)


def split3(v):
    hi = v.astype(BF16)
    rest = v - hi.astype(F32)
    mid = rest.astype(BF16)
    return [hi, mid, (rest - mid.astype(F32)).astype(BF16)]


def call(kernel, args, outs, scratch, name, far=(), far_out=(), near_out=(), scalars=()):
    specs = [pl.BlockSpec(memory_space=pltpu.SMEM)] * len(scalars)
    specs += [FAR_AWAY if i in far else pl.BlockSpec() for i in range(len(args))]
    return pl.pallas_call(
        kernel,
        in_specs=specs,
        out_specs=[
            FAR_AWAY if i in far_out else HERE if i in near_out else pl.BlockSpec()
            for i in range(len(outs))
        ],
        out_shape=[
            pltpu.VMEM(*out) if i in near_out else jax.ShapeDtypeStruct(*out)
            for i, out in enumerate(outs)
        ],
        scratch_shapes=scratch,
        compiler_params=params(0),
        name=name,
    )(*scalars, *args)


def start(source, target, sem):
    copy = pltpu.make_async_copy(source, target, sem)
    copy.start()
    return copy


def on_chip(array):
    return pltpu.with_memory_space_constraint(array, pltpu.VMEM)


def place(r):
    return r // 8 + SUB // 8 * (r % 8)


def reorder(back=False):
    r = lax.broadcasted_iota(jnp.int32, (SUB, SUB), 1 if back else 0)
    c = lax.broadcasted_iota(jnp.int32, (SUB, SUB), 0 if back else 1)
    return (place(r) == c).astype(F32).astype(BF16)


def one_hot(first_channel, width):
    row = lax.broadcasted_iota(jnp.int32, (2 * HEADS, width), 0)
    chan = lax.broadcasted_iota(jnp.int32, (2 * HEADS, width), 1) + first_channel
    return ((row % HEADS) == (chan // HEAD_DIM)).astype(F32).astype(BF16)


def pack_kernel(w_ref, b_ref, dt_ref, a_ref, skip_ref, wbc_ref, bbc_ref, gain_ref,
                tok_ref, out_ref, tail_ref, gain_out):
    out_ref[...] = jnp.zeros_like(out_ref)
    here = dt_ref.shape[1]
    for k in range(out_ref.shape[0]):
        out_ref[k, 0:CONV] = w_ref[...]
        out_ref[k, CONV : CONV + 1] = b_ref[...]
        for row, ref in ((5, dt_ref), (6, a_ref), (7, skip_ref)):
            out_ref[k, row : row + 1, 0:here] = ref[...]
        for tap in range(CONV):
            row, cols = bc_slot(tap)
            out_ref[k, row : row + 1, cols] = wbc_ref[tap : tap + 1]
        row, cols = bc_slot(CONV)
        out_ref[k, row : row + 1, cols] = bbc_ref[...]
    tail_ref[...] = tok_ref[...]
    gain_out[...] = jnp.broadcast_to(gain_ref[...], gain_out.shape)


def bc_slot(k):
    at = 128 * (1 + k % 3)
    return 5 + k // 3, slice(at, at + BC)


def pack(small, tokens, copies):
    rows, depth = tokens.shape
    small = [a if a.ndim == 2 else a[None] for a in small]
    wide = small[0].shape[1]

    def whole(a):
        return pl.BlockSpec(a.shape, lambda g: (0, 0))

    return pl.pallas_call(
        pack_kernel,
        grid=(1,),
        in_specs=[whole(a) for a in small]
        + [pl.BlockSpec((8, depth), lambda g: (rows // 8 - 1, 0))],
        out_specs=[
            HERE,
            HERE,
            pl.BlockSpec((8, DINNER), lambda g: (0, 0)),
        ],
        out_shape=[
            pltpu.VMEM((copies, 8, wide), F32),
            pltpu.VMEM((8, depth), BF16),
            jax.ShapeDtypeStruct((8, DINNER), F32),
        ],
        compiler_params=params(),
        name="pack",
    )(*small, tokens)


def half_lanes(w, which):
    parts = []
    for k in range(w.shape[1] // 128):
        at = k * 128 + which * HEAD_DIM
        parts.append(w[:, at : at + HEAD_DIM])
    return jnp.concatenate(parts, axis=1)


def convolve(x, weights, bias):
    first = lax.broadcasted_iota(jnp.int32, (8, 1), 0) == 0
    results = []
    for k in range((x.shape[0] - PAD) // SUB):
        at = PAD + k * SUB
        rows = x[at : at + SUB]
        edge = []
        for m in range(1, CONV):
            own = x[at + SUB - 8 * m : at + SUB - 8 * m + 8]
            last = PAD - m if k == 0 else at - 8 * m + 7
            edge.insert(0, jnp.where(first, x[last : last + 1], pltpu.roll(own, 1, 0)))
        summed = bias + weights[CONV - 1 : CONV] * rows
        for m in range(1, CONV):
            moved = jnp.concatenate(edge[CONV - 1 - m :] + [rows[: SUB - 8 * m]], axis=0)
            summed = summed + weights[CONV - 1 - m : CONV - m] * moved
        results.append(silu(summed))
    return results


def state_kernel(
    tok_hbm, halo_ref, w_hbm, wsmall_hbm, par,
    xc_hbm, mine_hbm, bc_hbm, dt_hbm, cum_hbm, skip_hbm, slab_ref,
    raw, tok, w_ref, wsmall, xc_ref, bc_ref, dt_ref, cum_ref, skip_ref,
    wgt, bt, in_sem, out_sem,
):
    rows = tok_hbm.shape[0]
    groups = DINNER // FINE
    half = DINNER
    fetch_tok = start(tok_hbm, raw, in_sem.at[0])
    fetch_small = start(wsmall_hbm, wsmall, in_sem.at[1])
    fetch_w = [
        start(w_hbm.at[:, i * half : (i + 1) * half], w_ref.at[i], in_sem.at[2 + i])
        for i in range(2)
    ]
    tok[0 : PAD - 8] = jnp.zeros((PAD - 8, tok.shape[1]), BF16)
    tok[PAD - 8 : PAD] = halo_ref[...]
    fetch_tok.wait()
    order = reorder()
    for k in range(rows // SUB):
        here = slice(k * SUB, (k + 1) * SUB)
        tok[PAD + k * SUB : PAD + (k + 1) * SUB] = dot(order, raw[here]).astype(BF16)
    fetch_small.wait()
    begin(tok, wsmall, par, bc_ref, dt_ref, cum_ref, wgt, bt)
    sends = [
        start(tok.at[PAD:], mine_hbm, out_sem.at[4]),
        start(bc_ref, bc_hbm, out_sem.at[0]),
        start(dt_ref, dt_hbm, out_sem.at[1]),
        start(cum_ref, cum_hbm, out_sem.at[2]),
    ]

    def project(g):
        at = 2 * g * FINE % half
        w = half_lanes(w_ref[2 * g * FINE // half, :, at : at + 2 * FINE], 1)
        return dot(tok[...], w).astype(BF16).astype(F32)

    wide = par.shape[2]
    for part in range(2):
        fetch_w[part].wait()
        mine_groups = range(part * groups // 2, (part + 1) * groups // 2)
        ahead = project(mine_groups[0])
        for g in mine_groups:
            x = ahead
            if g + 1 in mine_groups:
                ahead = project(g + 1)
            cols = slice(g * FINE, (g + 1) * FINE)
            spread = dot(wgt[...], one_hot(g * FINE, FINE))
            at = g * FINE % wide
            mine = par[g * FINE // wide, :, at : at + FINE]
            blocks = convolve(x, mine[0:CONV], mine[CONV : CONV + 1])
            xc = jnp.concatenate([block.astype(BF16) for block in blocks], axis=0)
            xc_ref[:, cols] = xc
            weighted = (xc.astype(F32) * spread[:rows]).astype(BF16)
            state = dot(bt[...], weighted)
            extra = spread[rows : rows + 8]
            skip_ref[:, cols] = extra
            for i in range(FINE // OWNED):
                own = slice(i * OWNED, (i + 1) * OWNED)
                owner = g * FINE // OWNED + i
                slab_ref[owner, 0:STATE] = state[:, own].astype(BF16)
                slab_ref[owner, STATE : STATE + 8] = extra[:, own].astype(BF16)
            if (g + 1) * FINE % SEND == 0:
                cols = slice((g + 1) * FINE - SEND, (g + 1) * FINE)
                sem = out_sem.at[5 + cols.start // SEND]
                sends.append(start(xc_ref.at[:, cols], xc_hbm.at[:, cols], sem))
    sends.append(start(skip_ref, skip_hbm, out_sem.at[3]))
    for copy in sends:
        copy.wait()


def begin(tok, wsmall_ref, par, bc_ref, dt_ref, cum_ref, wgt, bt):
    rows = dt_ref.shape[0]
    blocks = par.shape[0]
    each = HEADS // blocks
    lane = lax.broadcasted_iota(jnp.int32, (8, 128), 1)
    heads = jnp.zeros((8, 128), F32)
    for k in range(blocks):
        block = par[k, :, 0:128]
        moved = block if k == 0 else pltpu.roll(block, each * k, 1)
        heads = jnp.where(lane // each == k, moved, heads)
    heads = heads[:, :HEADS]
    small = lax.dot_general(
        tok[...], wsmall_ref[...], (((1,), (1,)), ((), ())),
        preferred_element_type=F32,
    )
    small = small.astype(BF16).astype(F32)
    raw = small[PAD:, BC:] + heads[5:6]
    step = jnp.maximum(raw, 0.0) + jnp.log1p(jnp.exp(-jnp.abs(raw)))
    decay = step * -jnp.exp(heads[6:7])
    r = lax.broadcasted_iota(jnp.int32, (SUB, SUB), 0)
    c = lax.broadcasted_iota(jnp.int32, (SUB, SUB), 1)
    ones = (place(r) >= place(c)).astype(F32).astype(BF16)
    before = jnp.zeros((1, HEADS), F32)
    parts = []
    for k in range(rows // SUB):
        three = jnp.concatenate(split3(decay[k * SUB : (k + 1) * SUB]), axis=1)
        sums = dot(ones, three)
        part = before + (
            sums[:, :HEADS] + sums[:, HEADS : 2 * HEADS] + sums[:, 2 * HEADS :]
        )
        before = part[SUB - 1 : SUB]
        parts.append(part)
    cum = jnp.concatenate(parts, axis=0)
    dt_ref[...] = step
    cum_ref[...] = cum
    wgt[0:rows] = hi_lo(step * jnp.exp(before - cum), 1)
    total = hi_lo(jnp.exp(before), 1)
    zero = jnp.zeros((1, HEADS), BF16)
    wgt[rows : rows + 8] = jnp.concatenate(
        [
            jnp.concatenate([total[:, :HEADS], zero], axis=1),
            jnp.concatenate([zero, total[:, HEADS:]], axis=1),
            hi_lo(heads[7:8], 1),
            jnp.zeros((5, 2 * HEADS), BF16),
        ],
        axis=0,
    )
    slots = [bc_slot(k) for k in range(CONV + 1)]
    taps = [par[0, row : row + 1, cols] for row, cols in slots]
    weights = jnp.concatenate(taps[:CONV], axis=0)
    conved = jnp.concatenate(convolve(small[:, :BC], weights, taps[CONV]), axis=0)
    bc_ref[...] = conved.astype(BF16)
    bt[...] = conved.T[:STATE].astype(BF16)


def local_state(tokens, halo, w_gate_x, w_small, packed):
    rows, depth = tokens.shape
    outs = [
        ((rows, DINNER), BF16),
        ((rows, depth), BF16),
        ((rows, BC), BF16),
        ((rows, HEADS), F32),
        ((rows, HEADS), F32),
        ((8, DINNER), F32),
    ]
    return call(
        state_kernel,
        [tokens, on_chip(halo), w_gate_x, w_small, on_chip(packed)],
        outs + [((DINNER // OWNED, STATE + 8, OWNED), BF16)],
        [
            pltpu.VMEM((rows, depth), BF16),
            pltpu.VMEM((PAD + rows, depth), BF16),
            pltpu.VMEM((2, depth, DINNER), BF16),
            pltpu.VMEM(w_small.shape, BF16),
            *(pltpu.VMEM(shape, dtype) for shape, dtype in outs[:1] + outs[2:]),
            pltpu.VMEM((rows + 8, 2 * HEADS), BF16),
            pltpu.VMEM((STATE, rows), BF16),
            pltpu.SemaphoreType.DMA((4,)),
            pltpu.SemaphoreType.DMA((5 + DINNER // SEND,)),
        ],
        "local_state",
        far=(0, 2, 3),
        far_out=range(6),
        near_out=(6,),
    )


def prepare(bc_ref, dt_ref, cum_ref, scores, left, rowlog, bt, wgt):
    rows = bc_ref.shape[0]
    heads = WIDTH // HEAD_DIM
    bt[...] = bc_ref[...].astype(F32).T[:STATE].astype(BF16)
    for k in range(rows // SUB):
        here = slice(k * SUB, (k + 1) * SUB)
        scores[here] = dot(bc_ref[here, STATE:], bt[:, here])
    cum = cum_ref[...]
    step = dt_ref[...]
    ones = jnp.ones((rows, HEADS), BF16)
    starts, ends = [], []
    before = jnp.zeros((1, HEADS), F32)
    for k in range(rows // SUB):
        starts.append(jnp.broadcast_to(before, (SUB, HEADS)))
        before = cum[(k + 1) * SUB - 1 : (k + 1) * SUB]
        ends.append(jnp.broadcast_to(before, (SUB, HEADS)))
    starts = jnp.concatenate(starts, axis=0)
    ends = jnp.concatenate(ends, axis=0)
    passed = cum - starts
    left[...] = jnp.concatenate(split3(passed * LOG2E) + [ones], axis=1)
    by_row = (jnp.log(jnp.maximum(step, 1e-37)) - passed) * LOG2E
    by_row = jnp.concatenate([p.astype(F32) for p in split3(by_row)] + [cum], axis=1).T
    for g in range(HEADS // heads):
        for p in range(3):
            first = p * HEADS + g * heads
            rowlog[g, p, 0:heads] = by_row[first : first + heads]
    wgt[0:rows] = hi_lo(step * jnp.exp(ends - cum), 1)
    wgt[rows : 2 * rows] = hi_lo(jnp.exp(passed), 1)
    wgt[2 * rows : 3 * rows] = hi_lo(jnp.exp(cum), 1)


def intra_kernel(
    first_group, xc_ref, tok_ref, w_ref, bc_ref, dt_ref, cum_ref, skip_ref,
    own_ref, scale_ref, scores, left, rowlog, bt, wgt,
):
    rows = xc_ref.shape[0]
    blocks = rows // SUB
    heads = WIDTH // HEAD_DIM
    together = xc_ref.shape[1] // WIDTH

    @pl.when(pl.program_id(0) == 0)
    def _():
        prepare(bc_ref, dt_ref, cum_ref, scores, left, rowlog, bt, wgt)

    r = lax.broadcasted_iota(jnp.int32, (SUB, heads * SUB), 0)
    c = lax.broadcasted_iota(jnp.int32, (SUB, heads * SUB), 1)
    causal = place(r) >= place(c % SUB)
    low = lax.broadcasted_iota(jnp.int32, (1, 128), 1) < HEAD_DIM
    pr = lax.broadcasted_iota(jnp.int32, (3 * HEADS, heads * SUB), 0)
    pc = lax.broadcasted_iota(jnp.int32, (3 * HEADS, heads * SUB), 1)
    for i in range(together):
        g = first_group + pl.program_id(0) * together + i
        mine = slice(i * WIDTH, (i + 1) * WIDTH)
        expanded = dot(wgt[...], one_hot(g * WIDTH, WIDTH))
        pick = (pr % HEADS == g * heads + pc // SUB).astype(F32).astype(BF16)
        skip = skip_ref[2:3, mine]
        w = half_lanes(w_ref[:, 2 * i * WIDTH : 2 * (i + 1) * WIDTH], 0)
        z = dot(tok_ref[...], w).astype(BF16).astype(F32)
        state = jnp.zeros((STATE, WIDTH), F32)
        for k in range(blocks):
            here = slice(k * SUB, (k + 1) * SUB)
            xc = xc_ref[here, mine]
            late = jnp.concatenate(
                [
                    jnp.concatenate(
                        [rowlog[g, p, h : h + 1, here] for h in range(heads)], axis=1
                    )
                    for p in range(3)
                ]
                + [jnp.zeros((HEADS - 3, heads * SUB), F32)],
                axis=0,
            ).astype(BF16)
            gaps = dot(left[here], jnp.concatenate([pick, late], axis=0))
            decay = jnp.exp2(jnp.where(causal, gaps, -jnp.inf))
            score = scores[here]
            pieces = []
            for pair in range(heads // 2):
                both = [
                    (score * decay[:, h * SUB : (h + 1) * SUB]).astype(BF16)
                    for h in (2 * pair, 2 * pair + 1)
                ]
                x = xc[:, pair * 128 : pair * 128 + 128]
                none = jnp.zeros_like(x)
                right = jnp.concatenate(
                    [jnp.where(low, x, none), jnp.where(low, none, x)], axis=0
                )
                pieces.append(dot(jnp.concatenate(both, axis=1), right))
            y = jnp.concatenate(pieces, axis=1)
            xf = xc.astype(F32)
            grow = expanded[rows + k * SUB : rows + (k + 1) * SUB]
            if k > 0:
                y = y + grow * dot(bc_ref[here, STATE:], state.astype(BF16))
            if k + 1 < blocks:
                shrink = expanded[here]
                fresh = dot(bt[:, here], (xf * shrink).astype(BF16))
                state = state * grow[SUB - 1 : SUB] + fresh
            gate = silu(z[here])
            own_ref[here, mine] = ((y + skip * xf) * gate).astype(own_ref.dtype)
            full = expanded[2 * rows + k * SUB : 2 * rows + (k + 1) * SUB]
            scale_ref[here, mine] = (full * gate).astype(BF16)


def intra(first_group, groups, xc, tokens, w_gate_x, bc, dt, cum, skips):
    rows, depth = tokens.shape
    together = TOGETHER
    group = first_group // together
    wide = together * WIDTH

    def whole(a):
        return pl.BlockSpec(a.shape, lambda i: (0,) * a.ndim)

    return pl.pallas_call(
        functools.partial(intra_kernel, first_group),
        grid=(groups // together,),
        in_specs=[
            pl.BlockSpec((rows, wide), lambda i: (0, i + group)),
            whole(tokens),
            pl.BlockSpec((depth, 2 * wide), lambda i: (0, i + group)),
            whole(bc),
            whole(dt),
            whole(cum),
            pl.BlockSpec((8, wide), lambda i: (0, i + group)),
        ],
        out_specs=[
            pl.BlockSpec((rows, wide), lambda i: (0, i)),
            pl.BlockSpec((rows, wide), lambda i: (0, i)),
        ],
        out_shape=[
            jax.ShapeDtypeStruct((rows, groups * WIDTH), OWN),
            jax.ShapeDtypeStruct((rows, groups * WIDTH), BF16),
        ],
        scratch_shapes=[
            pltpu.VMEM((rows, SUB), F32),
            pltpu.VMEM((rows, 4 * HEADS), BF16),
            pltpu.VMEM((DINNER // WIDTH, 3, 8, rows), F32),
            pltpu.VMEM((STATE, rows), BF16),
            pltpu.VMEM((3 * rows, 2 * HEADS), BF16),
        ],
        compiler_params=params(),
        name="intra",
    )(xc, tokens, w_gate_x, bc, dt, cum, skips)


def through(state, slab):
    slab = slab.astype(F32)
    total = slab[STATE : STATE + 1] + slab[STATE + 1 : STATE + 2]
    return state * total + slab[0:STATE], total


def fold_kernel(in_ref, out_ref):
    state = jnp.zeros((STATE, OWNED), F32)
    whole = jnp.ones((1, OWNED), F32)
    for q in range(in_ref.shape[0]):
        state, total = through(state, in_ref[q])
        whole = whole * total
    hi = whole.astype(BF16).astype(F32)
    row = lax.broadcasted_iota(jnp.int32, (8, OWNED), 0)
    tail = jnp.where(row == 0, hi, jnp.where(row == 1, whole - hi, 0.0))
    state = state.astype(BF16)
    tail = tail.astype(BF16)
    for b in range(out_ref.shape[0]):
        out_ref[b, 0:STATE] = state
        out_ref[b, STATE:] = tail


def fold(near, blocks):
    out = ((blocks, *near.shape[1:]), BF16)
    return call(fold_kernel, [on_chip(near)], [out], [], "fold", near_out=(0,))[0]


def unfold_kernel(me_ref, near_ref, far_ref, out_ref):
    def earlier(b, state):
        return through(state, far_ref[b])[0]

    state = jnp.zeros((STATE, OWNED), F32)
    state = lax.fori_loop(0, me_ref[0], earlier, state)
    for q in range(near_ref.shape[0]):
        out_ref[q] = state.astype(BF16)
        state, _ = through(state, near_ref[q])


def unfold(me, near, far):
    count = near.shape[0]
    out = ((count, STATE, OWNED), BF16)
    operands = [on_chip(near), on_chip(far)]
    return call(
        unfold_kernel, operands, [out], [], "unfold", near_out=(0,), scalars=(me,)
    )[0]


def finish_kernel(parts, bc_hbm, in_ref, gain_hbm, w_hbm, *refs):
    own_hbm, scale_hbm = refs[:parts], refs[parts : 2 * parts]
    out_hbm, bc_ref, gain_ref, w_ref, own_all, scale_all = refs[2 * parts : 2 * parts + 6]
    acc, out_ref, in_sem, w_sem = refs[2 * parts + 6 :]
    rows = bc_hbm.shape[0]
    span = DINNER // CHUNKS
    small = [
        start(bc_hbm, bc_ref, w_sem.at[CHUNKS + rows // SUB]),
        start(gain_hbm, gain_ref, w_sem.at[CHUNKS + rows // SUB + 1]),
    ]
    fetches, fetch_w = [], []
    for k in range(CHUNKS):
        fetches.append([])
        at = 0
        for p in range(parts):
            low, high = max(at, k * span), min(at + own_hbm[p].shape[1], (k + 1) * span)
            if low < high:
                there, here = slice(low - at, high - at), slice(low, high)
                pairs = ((own_hbm[p], own_all), (scale_hbm[p], scale_all))
                for i, (hbm, ref) in enumerate(pairs):
                    source, target = hbm.at[:, there], ref.at[:, here]
                    fetches[k].append(start(source, target, in_sem.at[k, p, i]))
            at += own_hbm[p].shape[1]
        part = slice(k * span, (k + 1) * span)
        fetch_w.append(start(w_hbm.at[part], w_ref.at[part], w_sem.at[k]))

    def gate(k, total):
        sides = []
        for g in range(k * span // WIDTH, (k + 1) * span // WIDTH):
            cols = slice(g * WIDTH, (g + 1) * WIDTH)
            slabs = [in_ref[2 * g], in_ref[2 * g + 1]]
            carried = dot(bc_ref[:, STATE:], jnp.concatenate(slabs, axis=1))
            scale = scale_all[:, cols].astype(F32)
            gated = own_all[:, cols].astype(F32) + scale * carried
            gated = gated.astype(BF16).astype(F32)
            square = gated * gated
            total = total + square[:, :128] + square[:, 128:]
            sides.append((gated * gain_ref[0:1, cols]).astype(BF16))
        return jnp.concatenate(sides, axis=1), total

    total = jnp.zeros((rows, 128), F32)
    for copy in small:
        copy.wait()
    for k in range(CHUNKS):
        for copy in fetches[k]:
            copy.wait()
        side, total = gate(k, total)
        fetch_w[k].wait()
        product = dot(side, w_ref[k * span : (k + 1) * span])
        if k > 0:
            product = acc[...] + product
        if k + 1 < CHUNKS:
            acc[...] = product
    mean = jnp.sum(total, axis=1, keepdims=True) * (1.0 / DINNER)
    product = (product * lax.rsqrt(mean + EPSILON)).astype(BF16)
    order = reorder(back=True)
    sends = []
    for k in range(rows // SUB):
        here = slice(k * SUB, (k + 1) * SUB)
        out_ref[here] = dot(order, product[here]).astype(BF16)
        sends.append(start(out_ref.at[here], out_hbm.at[here], w_sem.at[CHUNKS + k]))
    for copy in sends:
        copy.wait()


def finish(bc, incoming, owns, scales, gain, w_out):
    rows = bc.shape[0]
    columns = w_out.shape[1]
    parts = len(owns)
    return call(
        functools.partial(finish_kernel, parts),
        [bc, on_chip(incoming), gain, w_out, *owns, *scales],
        [((rows, columns), BF16)],
        [
            pltpu.VMEM(bc.shape, BF16),
            pltpu.VMEM(gain.shape, F32),
            pltpu.VMEM(w_out.shape, BF16),
            pltpu.VMEM((rows, DINNER), OWN),
            pltpu.VMEM((rows, DINNER), BF16),
            pltpu.VMEM((rows, columns), F32),
            pltpu.VMEM((rows, columns), BF16),
            pltpu.SemaphoreType.DMA((CHUNKS, parts, 2)),
            pltpu.SemaphoreType.DMA((CHUNKS + rows // SUB + 2,)),
        ],
        "finish",
        far=(0, *range(2, 4 + 2 * parts)),
        far_out=(0,),
    )[0]


def on_device(
    tokens, w_gate_x, w_bc_dt, conv_x_weight, conv_x_bias, conv_bc_weight,
    conv_bc_bias, dt_bias, a_log, skip_d, norm_gain, w_out,
):
    n = lax.axis_size("head")
    blocks = lax.axis_size(FAR)
    devices = blocks * lax.axis_size(NEAR)
    my_block = lax.axis_index(FAR)[None]
    small = [conv_x_weight, conv_x_bias, dt_bias, a_log, skip_d]
    small += [conv_bc_weight, conv_bc_bias, norm_gain]
    packed, tail, gain = pack(small, tokens, n)
    packed = lax.all_to_all(packed, "head", 0, 0, tiled=True)
    halo = lax.ppermute(tail, BOTH, [(i, i + 1) for i in range(devices - 1)])
    xc, mine, bc, dt, cum, skips, slabs = local_state(
        tokens, halo, w_gate_x, w_bc_dt.T, packed
    )
    near = lax.all_to_all(slabs, NEAR, 0, 0, tiled=True)
    rest = (bc, dt, cum, skips)
    first, second, third = SPLIT
    own0, scale0 = intra(0, first, xc, mine, w_gate_x, *rest)
    near, own0 = lax.optimization_barrier((near, own0))
    copies = fold(near, blocks)
    far = lax.all_to_all(copies, FAR, 0, 0, tiled=True)
    xc, copies = lax.optimization_barrier((xc, copies))
    own1, scale1 = intra(first, second, xc, mine, w_gate_x, *rest)
    far, own1 = lax.optimization_barrier((far, own1))
    incoming = unfold(my_block, near, far)
    back = lax.all_to_all(incoming, NEAR, 0, 0, tiled=True)
    xc, incoming = lax.optimization_barrier((xc, incoming))
    own2, scale2 = intra(first + second, third, xc, mine, w_gate_x, *rest)
    owns, scales = (own0, own1, own2), (scale0, scale1, scale2)
    return finish(bc, back, owns, scales, gain, w_out)


def solution(mesh):
    seq, head = mesh.devices.shape
    split = Mesh(mesh.devices.reshape(seq // 4, 2, 2, head), BOTH)
    return jax.shard_map(
        on_device,
        mesh=split,
        in_specs=(
            P(BOTH, None),
            P(),
            P(),
            P(None, "head"),
            P("head"),
            P(),
            P(),
            P("head"),
            P("head"),
            P("head"),
            P(),
            P(),
        ),
        out_specs=P(BOTH, None),
        check_vma=False,
    )
```

```python
import functools

import jax
import jax.numpy as jnp
from jax import lax
from jax.experimental import pallas as pl
from jax.experimental.pallas import tpu as pltpu
from jax.sharding import Mesh
from jax.sharding import PartitionSpec as P

HEADS = 32
HEAD_DIM = 64
STATE = 64
CONV = 4
DINNER = HEADS * HEAD_DIM
BC = 2 * STATE
SUB = 128
PAD = 16
EPSILON = 1e-05
FAR = "chips"
NEAR = ("row", "core", "head")
BOTH = (FAR, *NEAR)
WIDTH = 256
OWNED = 128
TOGETHER = 1
SPLIT = (2, 3, 3)
FINE = 512
SEND = 512
CHUNKS = 2
F32 = jnp.float32
BF16 = jnp.bfloat16
OWN = jnp.bfloat16
LIMIT = 60 * 1024 * 1024
LOG2E = 1.4426950408889634
FAR_AWAY = pl.BlockSpec(memory_space=pltpu.HBM)
HERE = pl.BlockSpec(memory_space=pltpu.VMEM)


def params(steps=1):
    return pltpu.CompilerParams(
        dimension_semantics=("arbitrary",) * steps, vmem_limit_bytes=LIMIT
    )


def silu(v):
    half = 0.5 * v
    return half + half * jnp.tanh(half)


def hi_lo(v, axis):
    hi = v.astype(BF16)
    lo = (v - hi.astype(F32)).astype(BF16)
    return jnp.concatenate([hi, lo], axis=axis)


def dot(a, b):
    return jnp.dot(a, b, preferred_element_type=F32)


def split3(v):
    hi = v.astype(BF16)
    rest = v - hi.astype(F32)
    mid = rest.astype(BF16)
    return [hi, mid, (rest - mid.astype(F32)).astype(BF16)]


def call(kernel, args, outs, scratch, name, far=(), far_out=(), near_out=(), scalars=()):
    specs = [pl.BlockSpec(memory_space=pltpu.SMEM)] * len(scalars)
    specs += [FAR_AWAY if i in far else pl.BlockSpec() for i in range(len(args))]
    return pl.pallas_call(
        kernel,
        in_specs=specs,
        out_specs=[
            FAR_AWAY if i in far_out else HERE if i in near_out else pl.BlockSpec()
            for i in range(len(outs))
        ],
        out_shape=[
            pltpu.VMEM(*out) if i in near_out else jax.ShapeDtypeStruct(*out)
            for i, out in enumerate(outs)
        ],
        scratch_shapes=scratch,
        compiler_params=params(0),
        name=name,
    )(*scalars, *args)


def start(source, target, sem):
    copy = pltpu.make_async_copy(source, target, sem)
    copy.start()
    return copy


def on_chip(array):
    return pltpu.with_memory_space_constraint(array, pltpu.VMEM)


def place(r):
    return r // 8 + SUB // 8 * (r % 8)


def reorder(back=False):
    r = lax.broadcasted_iota(jnp.int32, (SUB, SUB), 1 if back else 0)
    c = lax.broadcasted_iota(jnp.int32, (SUB, SUB), 0 if back else 1)
    return (place(r) == c).astype(F32).astype(BF16)


def one_hot(first_channel, width):
    row = lax.broadcasted_iota(jnp.int32, (2 * HEADS, width), 0)
    chan = lax.broadcasted_iota(jnp.int32, (2 * HEADS, width), 1) + first_channel
    return ((row % HEADS) == (chan // HEAD_DIM)).astype(F32).astype(BF16)


def pack_kernel(w_ref, b_ref, dt_ref, a_ref, skip_ref, wbc_ref, bbc_ref, gain_ref,
                tok_ref, out_ref, tail_ref, gain_out):
    out_ref[...] = jnp.zeros_like(out_ref)
    here = dt_ref.shape[1]
    for k in range(out_ref.shape[0]):
        out_ref[k, 0:CONV] = w_ref[...]
        out_ref[k, CONV : CONV + 1] = b_ref[...]
        for row, ref in ((5, dt_ref), (6, a_ref), (7, skip_ref)):
            out_ref[k, row : row + 1, 0:here] = ref[...]
        for tap in range(CONV):
            row, cols = bc_slot(tap)
            out_ref[k, row : row + 1, cols] = wbc_ref[tap : tap + 1]
        row, cols = bc_slot(CONV)
        out_ref[k, row : row + 1, cols] = bbc_ref[...]
    tail_ref[...] = tok_ref[...]
    gain_out[...] = jnp.broadcast_to(gain_ref[...], gain_out.shape)


def bc_slot(k):
    at = 128 * (1 + k % 3)
    return 5 + k // 3, slice(at, at + BC)


def pack(small, tokens, copies):
    rows, depth = tokens.shape
    small = [a if a.ndim == 2 else a[None] for a in small]
    wide = small[0].shape[1]

    def whole(a):
        return pl.BlockSpec(a.shape, lambda g: (0, 0))

    return pl.pallas_call(
        pack_kernel,
        grid=(1,),
        in_specs=[whole(a) for a in small]
        + [pl.BlockSpec((8, depth), lambda g: (rows // 8 - 1, 0))],
        out_specs=[
            HERE,
            HERE,
            pl.BlockSpec((8, DINNER), lambda g: (0, 0)),
        ],
        out_shape=[
            pltpu.VMEM((copies, 8, wide), F32),
            pltpu.VMEM((8, depth), BF16),
            jax.ShapeDtypeStruct((8, DINNER), F32),
        ],
        compiler_params=params(),
        name="pack",
    )(*small, tokens)


def half_lanes(w, which):
    parts = []
    for k in range(w.shape[1] // 128):
        at = k * 128 + which * HEAD_DIM
        parts.append(w[:, at : at + HEAD_DIM])
    return jnp.concatenate(parts, axis=1)


def convolve(x, weights, bias):
    first = lax.broadcasted_iota(jnp.int32, (8, 1), 0) == 0
    results = []
    for k in range((x.shape[0] - PAD) // SUB):
        at = PAD + k * SUB
        rows = x[at : at + SUB]
        edge = []
        for m in range(1, CONV):
            own = x[at + SUB - 8 * m : at + SUB - 8 * m + 8]
            last = PAD - m if k == 0 else at - 8 * m + 7
            edge.insert(0, jnp.where(first, x[last : last + 1], pltpu.roll(own, 1, 0)))
        summed = bias + weights[CONV - 1 : CONV] * rows
        for m in range(1, CONV):
            moved = jnp.concatenate(edge[CONV - 1 - m :] + [rows[: SUB - 8 * m]], axis=0)
            summed = summed + weights[CONV - 1 - m : CONV - m] * moved
        results.append(silu(summed))
    return results


def state_kernel(
    tok_hbm, halo_ref, w_hbm, wsmall_hbm, par,
    xc_hbm, mine_hbm, bc_hbm, dt_hbm, cum_hbm, skip_hbm, slab_ref,
    raw, tok, w_ref, wsmall, xc_ref, bc_ref, dt_ref, cum_ref, skip_ref,
    wgt, bt, in_sem, out_sem,
):
    rows = tok_hbm.shape[0]
    groups = DINNER // FINE
    half = DINNER
    fetch_tok = start(tok_hbm, raw, in_sem.at[0])
    fetch_small = start(wsmall_hbm, wsmall, in_sem.at[1])
    fetch_w = [
        start(w_hbm.at[:, i * half : (i + 1) * half], w_ref.at[i], in_sem.at[2 + i])
        for i in range(2)
    ]
    tok[0 : PAD - 8] = jnp.zeros((PAD - 8, tok.shape[1]), BF16)
    tok[PAD - 8 : PAD] = halo_ref[...]
    fetch_tok.wait()
    order = reorder()
    for k in range(rows // SUB):
        here = slice(k * SUB, (k + 1) * SUB)
        tok[PAD + k * SUB : PAD + (k + 1) * SUB] = dot(order, raw[here]).astype(BF16)
    fetch_small.wait()
    begin(tok, wsmall, par, bc_ref, dt_ref, cum_ref, wgt, bt)
    sends = [
        start(tok.at[PAD:], mine_hbm, out_sem.at[4]),
        start(bc_ref, bc_hbm, out_sem.at[0]),
        start(dt_ref, dt_hbm, out_sem.at[1]),
        start(cum_ref, cum_hbm, out_sem.at[2]),
    ]

    def project(g):
        at = 2 * g * FINE % half
        w = half_lanes(w_ref[2 * g * FINE // half, :, at : at + 2 * FINE], 1)
        return dot(tok[...], w).astype(BF16).astype(F32)

    wide = par.shape[2]
    for part in range(2):
        fetch_w[part].wait()
        mine_groups = range(part * groups // 2, (part + 1) * groups // 2)
        ahead = project(mine_groups[0])
        for g in mine_groups:
            x = ahead
            if g + 1 in mine_groups:
                ahead = project(g + 1)
            cols = slice(g * FINE, (g + 1) * FINE)
            spread = dot(wgt[...], one_hot(g * FINE, FINE))
            at = g * FINE % wide
            mine = par[g * FINE // wide, :, at : at + FINE]
            blocks = convolve(x, mine[0:CONV], mine[CONV : CONV + 1])
            xc = jnp.concatenate([block.astype(BF16) for block in blocks], axis=0)
            xc_ref[:, cols] = xc
            weighted = (xc.astype(F32) * spread[:rows]).astype(BF16)
            state = dot(bt[...], weighted)
            extra = spread[rows : rows + 8]
            skip_ref[:, cols] = extra
            for i in range(FINE // OWNED):
                own = slice(i * OWNED, (i + 1) * OWNED)
                owner = g * FINE // OWNED + i
                slab_ref[owner, 0:STATE] = state[:, own].astype(BF16)
                slab_ref[owner, STATE : STATE + 8] = extra[:, own].astype(BF16)
            if (g + 1) * FINE % SEND == 0:
                cols = slice((g + 1) * FINE - SEND, (g + 1) * FINE)
                sem = out_sem.at[5 + cols.start // SEND]
                sends.append(start(xc_ref.at[:, cols], xc_hbm.at[:, cols], sem))
    sends.append(start(skip_ref, skip_hbm, out_sem.at[3]))
    for copy in sends:
        copy.wait()


def begin(tok, wsmall_ref, par, bc_ref, dt_ref, cum_ref, wgt, bt):
    rows = dt_ref.shape[0]
    blocks = par.shape[0]
    each = HEADS // blocks
    lane = lax.broadcasted_iota(jnp.int32, (8, 128), 1)
    heads = jnp.zeros((8, 128), F32)
    for k in range(blocks):
        block = par[k, :, 0:128]
        moved = block if k == 0 else pltpu.roll(block, each * k, 1)
        heads = jnp.where(lane // each == k, moved, heads)
    heads = heads[:, :HEADS]
    small = lax.dot_general(
        tok[...], wsmall_ref[...], (((1,), (1,)), ((), ())),
        preferred_element_type=F32,
    )
    small = small.astype(BF16).astype(F32)
    raw = small[PAD:, BC:] + heads[5:6]
    step = jnp.maximum(raw, 0.0) + jnp.log1p(jnp.exp(-jnp.abs(raw)))
    decay = step * -jnp.exp(heads[6:7])
    r = lax.broadcasted_iota(jnp.int32, (SUB, SUB), 0)
    c = lax.broadcasted_iota(jnp.int32, (SUB, SUB), 1)
    ones = (place(r) >= place(c)).astype(F32).astype(BF16)
    before = jnp.zeros((1, HEADS), F32)
    parts = []
    for k in range(rows // SUB):
        three = jnp.concatenate(split3(decay[k * SUB : (k + 1) * SUB]), axis=1)
        sums = dot(ones, three)
        part = before + (
            sums[:, :HEADS] + sums[:, HEADS : 2 * HEADS] + sums[:, 2 * HEADS :]
        )
        before = part[SUB - 1 : SUB]
        parts.append(part)
    cum = jnp.concatenate(parts, axis=0)
    dt_ref[...] = step
    cum_ref[...] = cum
    wgt[0:rows] = hi_lo(step * jnp.exp(before - cum), 1)
    total = hi_lo(jnp.exp(before), 1)
    zero = jnp.zeros((1, HEADS), BF16)
    wgt[rows : rows + 8] = jnp.concatenate(
        [
            jnp.concatenate([total[:, :HEADS], zero], axis=1),
            jnp.concatenate([zero, total[:, HEADS:]], axis=1),
            hi_lo(heads[7:8], 1),
            jnp.zeros((5, 2 * HEADS), BF16),
        ],
        axis=0,
    )
    slots = [bc_slot(k) for k in range(CONV + 1)]
    taps = [par[0, row : row + 1, cols] for row, cols in slots]
    weights = jnp.concatenate(taps[:CONV], axis=0)
    conved = jnp.concatenate(convolve(small[:, :BC], weights, taps[CONV]), axis=0)
    bc_ref[...] = conved.astype(BF16)
    bt[...] = conved.T[:STATE].astype(BF16)


def local_state(tokens, halo, w_gate_x, w_small, packed):
    rows, depth = tokens.shape
    outs = [
        ((rows, DINNER), BF16),
        ((rows, depth), BF16),
        ((rows, BC), BF16),
        ((rows, HEADS), F32),
        ((rows, HEADS), F32),
        ((8, DINNER), F32),
    ]
    return call(
        state_kernel,
        [tokens, on_chip(halo), w_gate_x, w_small, on_chip(packed)],
        outs + [((DINNER // OWNED, STATE + 8, OWNED), BF16)],
        [
            pltpu.VMEM((rows, depth), BF16),
            pltpu.VMEM((PAD + rows, depth), BF16),
            pltpu.VMEM((2, depth, DINNER), BF16),
            pltpu.VMEM(w_small.shape, BF16),
            *(pltpu.VMEM(shape, dtype) for shape, dtype in outs[:1] + outs[2:]),
            pltpu.VMEM((rows + 8, 2 * HEADS), BF16),
            pltpu.VMEM((STATE, rows), BF16),
            pltpu.SemaphoreType.DMA((4,)),
            pltpu.SemaphoreType.DMA((5 + DINNER // SEND,)),
        ],
        "local_state",
        far=(0, 2, 3),
        far_out=range(6),
        near_out=(6,),
    )


def prepare(bc_ref, dt_ref, cum_ref, scores, left, rowlog, bt, wgt):
    rows = bc_ref.shape[0]
    heads = WIDTH // HEAD_DIM
    bt[...] = bc_ref[...].astype(F32).T[:STATE].astype(BF16)
    for k in range(rows // SUB):
        here = slice(k * SUB, (k + 1) * SUB)
        scores[here] = dot(bc_ref[here, STATE:], bt[:, here])
    cum = cum_ref[...]
    step = dt_ref[...]
    ones = jnp.ones((rows, HEADS), BF16)
    starts, ends = [], []
    before = jnp.zeros((1, HEADS), F32)
    for k in range(rows // SUB):
        starts.append(jnp.broadcast_to(before, (SUB, HEADS)))
        before = cum[(k + 1) * SUB - 1 : (k + 1) * SUB]
        ends.append(jnp.broadcast_to(before, (SUB, HEADS)))
    starts = jnp.concatenate(starts, axis=0)
    ends = jnp.concatenate(ends, axis=0)
    passed = cum - starts
    left[...] = jnp.concatenate(split3(passed * LOG2E) + [ones], axis=1)
    by_row = (jnp.log(jnp.maximum(step, 1e-37)) - passed) * LOG2E
    by_row = jnp.concatenate([p.astype(F32) for p in split3(by_row)] + [cum], axis=1).T
    for g in range(HEADS // heads):
        for p in range(3):
            first = p * HEADS + g * heads
            rowlog[g, p, 0:heads] = by_row[first : first + heads]
    wgt[0:rows] = hi_lo(step * jnp.exp(ends - cum), 1)
    wgt[rows : 2 * rows] = hi_lo(jnp.exp(passed), 1)
    wgt[2 * rows : 3 * rows] = hi_lo(jnp.exp(cum), 1)


def intra_kernel(
    first_group, xc_ref, tok_ref, w_ref, bc_ref, dt_ref, cum_ref, skip_ref,
    own_ref, scale_ref, scores, left, rowlog, bt, wgt,
):
    rows = xc_ref.shape[0]
    blocks = rows // SUB
    heads = WIDTH // HEAD_DIM
    together = xc_ref.shape[1] // WIDTH

    @pl.when(pl.program_id(0) == 0)
    def _():
        prepare(bc_ref, dt_ref, cum_ref, scores, left, rowlog, bt, wgt)

    r = lax.broadcasted_iota(jnp.int32, (SUB, heads * SUB), 0)
    c = lax.broadcasted_iota(jnp.int32, (SUB, heads * SUB), 1)
    causal = place(r) >= place(c % SUB)
    low = lax.broadcasted_iota(jnp.int32, (1, 128), 1) < HEAD_DIM
    pr = lax.broadcasted_iota(jnp.int32, (3 * HEADS, heads * SUB), 0)
    pc = lax.broadcasted_iota(jnp.int32, (3 * HEADS, heads * SUB), 1)
    for i in range(together):
        g = first_group + pl.program_id(0) * together + i
        mine = slice(i * WIDTH, (i + 1) * WIDTH)
        expanded = dot(wgt[...], one_hot(g * WIDTH, WIDTH))
        pick = (pr % HEADS == g * heads + pc // SUB).astype(F32).astype(BF16)
        skip = skip_ref[2:3, mine]
        w = half_lanes(w_ref[:, 2 * i * WIDTH : 2 * (i + 1) * WIDTH], 0)
        z = dot(tok_ref[...], w).astype(BF16).astype(F32)
        state = jnp.zeros((STATE, WIDTH), F32)
        for k in range(blocks):
            here = slice(k * SUB, (k + 1) * SUB)
            xc = xc_ref[here, mine]
            late = jnp.concatenate(
                [
                    jnp.concatenate(
                        [rowlog[g, p, h : h + 1, here] for h in range(heads)], axis=1
                    )
                    for p in range(3)
                ]
                + [jnp.zeros((HEADS - 3, heads * SUB), F32)],
                axis=0,
            ).astype(BF16)
            gaps = dot(left[here], jnp.concatenate([pick, late], axis=0))
            decay = jnp.exp2(jnp.where(causal, gaps, -jnp.inf))
            score = scores[here]
            pieces = []
            for pair in range(heads // 2):
                both = [
                    (score * decay[:, h * SUB : (h + 1) * SUB]).astype(BF16)
                    for h in (2 * pair, 2 * pair + 1)
                ]
                x = xc[:, pair * 128 : pair * 128 + 128]
                none = jnp.zeros_like(x)
                right = jnp.concatenate(
                    [jnp.where(low, x, none), jnp.where(low, none, x)], axis=0
                )
                pieces.append(dot(jnp.concatenate(both, axis=1), right))
            y = jnp.concatenate(pieces, axis=1)
            xf = xc.astype(F32)
            grow = expanded[rows + k * SUB : rows + (k + 1) * SUB]
            if k > 0:
                y = y + grow * dot(bc_ref[here, STATE:], state.astype(BF16))
            if k + 1 < blocks:
                shrink = expanded[here]
                fresh = dot(bt[:, here], (xf * shrink).astype(BF16))
                state = state * grow[SUB - 1 : SUB] + fresh
            gate = silu(z[here])
            own_ref[here, mine] = ((y + skip * xf) * gate).astype(own_ref.dtype)
            full = expanded[2 * rows + k * SUB : 2 * rows + (k + 1) * SUB]
            scale_ref[here, mine] = (full * gate).astype(BF16)


def intra(first_group, groups, xc, tokens, w_gate_x, bc, dt, cum, skips):
    rows, depth = tokens.shape
    together = TOGETHER
    group = first_group // together
    wide = together * WIDTH

    def whole(a):
        return pl.BlockSpec(a.shape, lambda i: (0,) * a.ndim)

    return pl.pallas_call(
        functools.partial(intra_kernel, first_group),
        grid=(groups // together,),
        in_specs=[
            pl.BlockSpec((rows, wide), lambda i: (0, i + group)),
            whole(tokens),
            pl.BlockSpec((depth, 2 * wide), lambda i: (0, i + group)),
            whole(bc),
            whole(dt),
            whole(cum),
            pl.BlockSpec((8, wide), lambda i: (0, i + group)),
        ],
        out_specs=[
            pl.BlockSpec((rows, wide), lambda i: (0, i)),
            pl.BlockSpec((rows, wide), lambda i: (0, i)),
        ],
        out_shape=[
            jax.ShapeDtypeStruct((rows, groups * WIDTH), OWN),
            jax.ShapeDtypeStruct((rows, groups * WIDTH), BF16),
        ],
        scratch_shapes=[
            pltpu.VMEM((rows, SUB), F32),
            pltpu.VMEM((rows, 4 * HEADS), BF16),
            pltpu.VMEM((DINNER // WIDTH, 3, 8, rows), F32),
            pltpu.VMEM((STATE, rows), BF16),
            pltpu.VMEM((3 * rows, 2 * HEADS), BF16),
        ],
        compiler_params=params(),
        name="intra",
    )(xc, tokens, w_gate_x, bc, dt, cum, skips)


def through(state, slab):
    slab = slab.astype(F32)
    total = slab[STATE : STATE + 1] + slab[STATE + 1 : STATE + 2]
    return state * total + slab[0:STATE], total


def fold_kernel(in_ref, out_ref):
    state = jnp.zeros((STATE, OWNED), F32)
    whole = jnp.ones((1, OWNED), F32)
    for q in range(in_ref.shape[0]):
        state, total = through(state, in_ref[q])
        whole = whole * total
    hi = whole.astype(BF16).astype(F32)
    row = lax.broadcasted_iota(jnp.int32, (8, OWNED), 0)
    tail = jnp.where(row == 0, hi, jnp.where(row == 1, whole - hi, 0.0))
    state = state.astype(BF16)
    tail = tail.astype(BF16)
    for b in range(out_ref.shape[0]):
        out_ref[b, 0:STATE] = state
        out_ref[b, STATE:] = tail


def fold(near, blocks):
    out = ((blocks, *near.shape[1:]), BF16)
    return call(fold_kernel, [on_chip(near)], [out], [], "fold", near_out=(0,))[0]


def unfold_kernel(me_ref, near_ref, far_ref, out_ref):
    def earlier(b, state):
        return through(state, far_ref[b])[0]

    state = jnp.zeros((STATE, OWNED), F32)
    state = lax.fori_loop(0, me_ref[0], earlier, state)
    for q in range(near_ref.shape[0]):
        out_ref[q] = state.astype(BF16)
        state, _ = through(state, near_ref[q])


def unfold(me, near, far):
    count = near.shape[0]
    out = ((count, STATE, OWNED), BF16)
    operands = [on_chip(near), on_chip(far)]
    return call(
        unfold_kernel, operands, [out], [], "unfold", near_out=(0,), scalars=(me,)
    )[0]


def finish_kernel(parts, bc_hbm, in_ref, gain_hbm, w_hbm, *refs):
    own_hbm, scale_hbm = refs[:parts], refs[parts : 2 * parts]
    out_hbm, bc_ref, gain_ref, w_ref, own_all, scale_all = refs[2 * parts : 2 * parts + 6]
    acc, out_ref, in_sem, w_sem = refs[2 * parts + 6 :]
    rows = bc_hbm.shape[0]
    span = DINNER // CHUNKS
    small = [
        start(bc_hbm, bc_ref, w_sem.at[CHUNKS + rows // SUB]),
        start(gain_hbm, gain_ref, w_sem.at[CHUNKS + rows // SUB + 1]),
    ]
    fetches, fetch_w = [], []
    for k in range(CHUNKS):
        fetches.append([])
        at = 0
        for p in range(parts):
            low, high = max(at, k * span), min(at + own_hbm[p].shape[1], (k + 1) * span)
            if low < high:
                there, here = slice(low - at, high - at), slice(low, high)
                pairs = ((own_hbm[p], own_all), (scale_hbm[p], scale_all))
                for i, (hbm, ref) in enumerate(pairs):
                    source, target = hbm.at[:, there], ref.at[:, here]
                    fetches[k].append(start(source, target, in_sem.at[k, p, i]))
            at += own_hbm[p].shape[1]
        part = slice(k * span, (k + 1) * span)
        fetch_w.append(start(w_hbm.at[part], w_ref.at[part], w_sem.at[k]))

    def gate(k, total):
        sides = []
        for g in range(k * span // WIDTH, (k + 1) * span // WIDTH):
            cols = slice(g * WIDTH, (g + 1) * WIDTH)
            slabs = [in_ref[2 * g], in_ref[2 * g + 1]]
            carried = dot(bc_ref[:, STATE:], jnp.concatenate(slabs, axis=1))
            scale = scale_all[:, cols].astype(F32)
            gated = own_all[:, cols].astype(F32) + scale * carried
            gated = gated.astype(BF16).astype(F32)
            square = gated * gated
            total = total + square[:, :128] + square[:, 128:]
            sides.append((gated * gain_ref[0:1, cols]).astype(BF16))
        return jnp.concatenate(sides, axis=1), total

    total = jnp.zeros((rows, 128), F32)
    for copy in small:
        copy.wait()
    for k in range(CHUNKS):
        for copy in fetches[k]:
            copy.wait()
        side, total = gate(k, total)
        fetch_w[k].wait()
        product = dot(side, w_ref[k * span : (k + 1) * span])
        if k > 0:
            product = acc[...] + product
        if k + 1 < CHUNKS:
            acc[...] = product
    mean = jnp.sum(total, axis=1, keepdims=True) * (1.0 / DINNER)
    product = (product * lax.rsqrt(mean + EPSILON)).astype(BF16)
    order = reorder(back=True)
    sends = []
    for k in range(rows // SUB):
        here = slice(k * SUB, (k + 1) * SUB)
        out_ref[here] = dot(order, product[here]).astype(BF16)
        sends.append(start(out_ref.at[here], out_hbm.at[here], w_sem.at[CHUNKS + k]))
    for copy in sends:
        copy.wait()


def finish(bc, incoming, owns, scales, gain, w_out):
    rows = bc.shape[0]
    columns = w_out.shape[1]
    parts = len(owns)
    return call(
        functools.partial(finish_kernel, parts),
        [bc, on_chip(incoming), gain, w_out, *owns, *scales],
        [((rows, columns), BF16)],
        [
            pltpu.VMEM(bc.shape, BF16),
            pltpu.VMEM(gain.shape, F32),
            pltpu.VMEM(w_out.shape, BF16),
            pltpu.VMEM((rows, DINNER), OWN),
            pltpu.VMEM((rows, DINNER), BF16),
            pltpu.VMEM((rows, columns), F32),
            pltpu.VMEM((rows, columns), BF16),
            pltpu.SemaphoreType.DMA((CHUNKS, parts, 2)),
            pltpu.SemaphoreType.DMA((CHUNKS + rows // SUB + 2,)),
        ],
        "finish",
        far=(0, *range(2, 4 + 2 * parts)),
        far_out=(0,),
    )[0]


def on_device(
    tokens, w_gate_x, w_bc_dt, conv_x_weight, conv_x_bias, conv_bc_weight,
    conv_bc_bias, dt_bias, a_log, skip_d, norm_gain, w_out,
):
    n = lax.axis_size("head")
    blocks = lax.axis_size(FAR)
    devices = blocks * lax.axis_size(NEAR)
    my_block = lax.axis_index(FAR)[None]
    small = [conv_x_weight, conv_x_bias, dt_bias, a_log, skip_d]
    small += [conv_bc_weight, conv_bc_bias, norm_gain]
    packed, tail, gain = pack(small, tokens, n)
    packed = lax.all_to_all(packed, "head", 0, 0, tiled=True)
    halo = lax.ppermute(tail, BOTH, [(i, i + 1) for i in range(devices - 1)])
    xc, mine, bc, dt, cum, skips, slabs = local_state(
        tokens, halo, w_gate_x, w_bc_dt.T, packed
    )
    near = lax.all_to_all(slabs, NEAR, 0, 0, tiled=True)
    rest = (bc, dt, cum, skips)
    first, second, third = SPLIT
    own0, scale0 = intra(0, first, xc, mine, w_gate_x, *rest)
    near, own0 = lax.optimization_barrier((near, own0))
    copies = fold(near, blocks)
    far = lax.all_to_all(copies, FAR, 0, 0, tiled=True)
    xc, copies = lax.optimization_barrier((xc, copies))
    own1, scale1 = intra(first, second, xc, mine, w_gate_x, *rest)
    far, own1 = lax.optimization_barrier((far, own1))
    incoming = unfold(my_block, near, far)
    back = lax.all_to_all(incoming, NEAR, 0, 0, tiled=True)
    xc, incoming = lax.optimization_barrier((xc, incoming))
    own2, scale2 = intra(first + second, third, xc, mine, w_gate_x, *rest)
    owns, scales = (own0, own1, own2), (scale0, scale1, scale2)
    return finish(bc, back, owns, scales, gain, w_out)


def solution(mesh):
    seq, head = mesh.devices.shape
    split = Mesh(mesh.devices.reshape(seq // 4, 2, 2, head), BOTH)
    return jax.shard_map(
        on_device,
        mesh=split,
        in_specs=(
            P(BOTH, None),
            P(),
            P(),
            P(None, "head"),
            P("head"),
            P(),
            P(),
            P("head"),
            P("head"),
            P("head"),
            P(),
            P(),
        ),
        out_specs=P(BOTH, None),
        check_vma=False,
    )
```

```python
import functools

import jax
import jax.numpy as jnp
from jax import lax
from jax.experimental import pallas as pl
from jax.experimental.pallas import tpu as pltpu
from jax.sharding import Mesh
from jax.sharding import PartitionSpec as P

HEADS = 32
HEAD_DIM = 64
STATE = 64
CONV = 4
DINNER = HEADS * HEAD_DIM
BC = 2 * STATE
SUB = 128
PAD = 16
EPSILON = 1e-05
FAR = "chips"
NEAR = ("row", "core", "head")
BOTH = (FAR, *NEAR)
WIDTH = 256
OWNED = 128
TOGETHER = 1
SPLIT = (2, 3, 3)
FINE = 512
SEND = 512
CHUNKS = 2
F32 = jnp.float32
BF16 = jnp.bfloat16
OWN = jnp.bfloat16
LIMIT = 60 * 1024 * 1024
LOG2E = 1.4426950408889634
FAR_AWAY = pl.BlockSpec(memory_space=pltpu.HBM)
HERE = pl.BlockSpec(memory_space=pltpu.VMEM)


def params(steps=1):
    return pltpu.CompilerParams(
        dimension_semantics=("arbitrary",) * steps, vmem_limit_bytes=LIMIT
    )


def silu(v):
    half = 0.5 * v
    return half + half * jnp.tanh(half)


def hi_lo(v, axis):
    hi = v.astype(BF16)
    lo = (v - hi.astype(F32)).astype(BF16)
    return jnp.concatenate([hi, lo], axis=axis)


def dot(a, b):
    return jnp.dot(a, b, preferred_element_type=F32)


def split3(v):
    hi = v.astype(BF16)
    rest = v - hi.astype(F32)
    mid = rest.astype(BF16)
    return [hi, mid, (rest - mid.astype(F32)).astype(BF16)]


def call(kernel, args, outs, scratch, name, far=(), far_out=(), near_out=(), scalars=()):
    specs = [pl.BlockSpec(memory_space=pltpu.SMEM)] * len(scalars)
    specs += [FAR_AWAY if i in far else pl.BlockSpec() for i in range(len(args))]
    return pl.pallas_call(
        kernel,
        in_specs=specs,
        out_specs=[
            FAR_AWAY if i in far_out else HERE if i in near_out else pl.BlockSpec()
            for i in range(len(outs))
        ],
        out_shape=[
            pltpu.VMEM(*out) if i in near_out else jax.ShapeDtypeStruct(*out)
            for i, out in enumerate(outs)
        ],
        scratch_shapes=scratch,
        compiler_params=params(0),
        name=name,
    )(*scalars, *args)


def start(source, target, sem):
    copy = pltpu.make_async_copy(source, target, sem)
    copy.start()
    return copy


def on_chip(array):
    return pltpu.with_memory_space_constraint(array, pltpu.VMEM)


def place(r):
    return r // 8 + SUB // 8 * (r % 8)


def reorder(back=False):
    r = lax.broadcasted_iota(jnp.int32, (SUB, SUB), 1 if back else 0)
    c = lax.broadcasted_iota(jnp.int32, (SUB, SUB), 0 if back else 1)
    return (place(r) == c).astype(F32).astype(BF16)


def one_hot(first_channel, width):
    row = lax.broadcasted_iota(jnp.int32, (2 * HEADS, width), 0)
    chan = lax.broadcasted_iota(jnp.int32, (2 * HEADS, width), 1) + first_channel
    return ((row % HEADS) == (chan // HEAD_DIM)).astype(F32).astype(BF16)


def pack_kernel(w_ref, b_ref, dt_ref, a_ref, skip_ref, wbc_ref, bbc_ref, gain_ref,
                tok_ref, out_ref, tail_ref, gain_out):
    out_ref[...] = jnp.zeros_like(out_ref)
    here = dt_ref.shape[1]
    for k in range(out_ref.shape[0]):
        out_ref[k, 0:CONV] = w_ref[...]
        out_ref[k, CONV : CONV + 1] = b_ref[...]
        for row, ref in ((5, dt_ref), (6, a_ref), (7, skip_ref)):
            out_ref[k, row : row + 1, 0:here] = ref[...]
        for tap in range(CONV):
            row, cols = bc_slot(tap)
            out_ref[k, row : row + 1, cols] = wbc_ref[tap : tap + 1]
        row, cols = bc_slot(CONV)
        out_ref[k, row : row + 1, cols] = bbc_ref[...]
    tail_ref[...] = tok_ref[...]
    gain_out[...] = jnp.broadcast_to(gain_ref[...], gain_out.shape)


def bc_slot(k):
    at = 128 * (1 + k % 3)
    return 5 + k // 3, slice(at, at + BC)


def pack(small, tokens, copies):
    rows, depth = tokens.shape
    small = [a if a.ndim == 2 else a[None] for a in small]
    wide = small[0].shape[1]

    def whole(a):
        return pl.BlockSpec(a.shape, lambda g: (0, 0))

    return pl.pallas_call(
        pack_kernel,
        grid=(1,),
        in_specs=[whole(a) for a in small]
        + [pl.BlockSpec((8, depth), lambda g: (rows // 8 - 1, 0))],
        out_specs=[
            HERE,
            HERE,
            pl.BlockSpec((8, DINNER), lambda g: (0, 0)),
        ],
        out_shape=[
            pltpu.VMEM((copies, 8, wide), F32),
            pltpu.VMEM((8, depth), BF16),
            jax.ShapeDtypeStruct((8, DINNER), F32),
        ],
        compiler_params=params(),
        name="pack",
    )(*small, tokens)


def half_lanes(w, which):
    parts = []
    for k in range(w.shape[1] // 128):
        at = k * 128 + which * HEAD_DIM
        parts.append(w[:, at : at + HEAD_DIM])
    return jnp.concatenate(parts, axis=1)


def convolve(x, weights, bias):
    first = lax.broadcasted_iota(jnp.int32, (8, 1), 0) == 0
    results = []
    for k in range((x.shape[0] - PAD) // SUB):
        at = PAD + k * SUB
        rows = x[at : at + SUB]
        edge = []
        for m in range(1, CONV):
            own = x[at + SUB - 8 * m : at + SUB - 8 * m + 8]
            last = PAD - m if k == 0 else at - 8 * m + 7
            edge.insert(0, jnp.where(first, x[last : last + 1], pltpu.roll(own, 1, 0)))
        summed = bias + weights[CONV - 1 : CONV] * rows
        for m in range(1, CONV):
            moved = jnp.concatenate(edge[CONV - 1 - m :] + [rows[: SUB - 8 * m]], axis=0)
            summed = summed + weights[CONV - 1 - m : CONV - m] * moved
        results.append(silu(summed))
    return results


def state_kernel(
    tok_hbm, halo_ref, w_hbm, wsmall_hbm, par,
    xc_hbm, mine_hbm, bc_hbm, dt_hbm, cum_hbm, skip_hbm, slab_ref,
    raw, tok, w_ref, wsmall, xc_ref, bc_ref, dt_ref, cum_ref, skip_ref,
    wgt, bt, in_sem, out_sem,
):
    rows = tok_hbm.shape[0]
    groups = DINNER // FINE
    half = DINNER
    fetch_tok = start(tok_hbm, raw, in_sem.at[0])
    fetch_small = start(wsmall_hbm, wsmall, in_sem.at[1])
    fetch_w = [
        start(w_hbm.at[:, i * half : (i + 1) * half], w_ref.at[i], in_sem.at[2 + i])
        for i in range(2)
    ]
    tok[0 : PAD - 8] = jnp.zeros((PAD - 8, tok.shape[1]), BF16)
    tok[PAD - 8 : PAD] = halo_ref[...]
    fetch_tok.wait()
    order = reorder()
    for k in range(rows // SUB):
        here = slice(k * SUB, (k + 1) * SUB)
        tok[PAD + k * SUB : PAD + (k + 1) * SUB] = dot(order, raw[here]).astype(BF16)
    fetch_small.wait()
    begin(tok, wsmall, par, bc_ref, dt_ref, cum_ref, wgt, bt)
    sends = [
        start(tok.at[PAD:], mine_hbm, out_sem.at[4]),
        start(bc_ref, bc_hbm, out_sem.at[0]),
        start(dt_ref, dt_hbm, out_sem.at[1]),
        start(cum_ref, cum_hbm, out_sem.at[2]),
    ]

    def project(g):
        at = 2 * g * FINE % half
        w = half_lanes(w_ref[2 * g * FINE // half, :, at : at + 2 * FINE], 1)
        return dot(tok[...], w).astype(BF16).astype(F32)

    wide = par.shape[2]
    for part in range(2):
        fetch_w[part].wait()
        mine_groups = range(part * groups // 2, (part + 1) * groups // 2)
        ahead = project(mine_groups[0])
        for g in mine_groups:
            x = ahead
            if g + 1 in mine_groups:
                ahead = project(g + 1)
            cols = slice(g * FINE, (g + 1) * FINE)
            spread = dot(wgt[...], one_hot(g * FINE, FINE))
            at = g * FINE % wide
            mine = par[g * FINE // wide, :, at : at + FINE]
            blocks = convolve(x, mine[0:CONV], mine[CONV : CONV + 1])
            xc = jnp.concatenate([block.astype(BF16) for block in blocks], axis=0)
            xc_ref[:, cols] = xc
            weighted = (xc.astype(F32) * spread[:rows]).astype(BF16)
            state = dot(bt[...], weighted)
            extra = spread[rows : rows + 8]
            skip_ref[:, cols] = extra
            for i in range(FINE // OWNED):
                own = slice(i * OWNED, (i + 1) * OWNED)
                owner = g * FINE // OWNED + i
                slab_ref[owner, 0:STATE] = state[:, own].astype(BF16)
                slab_ref[owner, STATE : STATE + 8] = extra[:, own].astype(BF16)
            if (g + 1) * FINE % SEND == 0:
                cols = slice((g + 1) * FINE - SEND, (g + 1) * FINE)
                sem = out_sem.at[5 + cols.start // SEND]
                sends.append(start(xc_ref.at[:, cols], xc_hbm.at[:, cols], sem))
    sends.append(start(skip_ref, skip_hbm, out_sem.at[3]))
    for copy in sends:
        copy.wait()


def begin(tok, wsmall_ref, par, bc_ref, dt_ref, cum_ref, wgt, bt):
    rows = dt_ref.shape[0]
    blocks = par.shape[0]
    each = HEADS // blocks
    lane = lax.broadcasted_iota(jnp.int32, (8, 128), 1)
    heads = jnp.zeros((8, 128), F32)
    for k in range(blocks):
        block = par[k, :, 0:128]
        moved = block if k == 0 else pltpu.roll(block, each * k, 1)
        heads = jnp.where(lane // each == k, moved, heads)
    heads = heads[:, :HEADS]
    small = lax.dot_general(
        tok[...], wsmall_ref[...], (((1,), (1,)), ((), ())),
        preferred_element_type=F32,
    )
    small = small.astype(BF16).astype(F32)
    raw = small[PAD:, BC:] + heads[5:6]
    step = jnp.maximum(raw, 0.0) + jnp.log1p(jnp.exp(-jnp.abs(raw)))
    decay = step * -jnp.exp(heads[6:7])
    r = lax.broadcasted_iota(jnp.int32, (SUB, SUB), 0)
    c = lax.broadcasted_iota(jnp.int32, (SUB, SUB), 1)
    ones = (place(r) >= place(c)).astype(F32).astype(BF16)
    before = jnp.zeros((1, HEADS), F32)
    parts = []
    for k in range(rows // SUB):
        three = jnp.concatenate(split3(decay[k * SUB : (k + 1) * SUB]), axis=1)
        sums = dot(ones, three)
        part = before + (
            sums[:, :HEADS] + sums[:, HEADS : 2 * HEADS] + sums[:, 2 * HEADS :]
        )
        before = part[SUB - 1 : SUB]
        parts.append(part)
    cum = jnp.concatenate(parts, axis=0)
    dt_ref[...] = step
    cum_ref[...] = cum
    wgt[0:rows] = hi_lo(step * jnp.exp(before - cum), 1)
    total = hi_lo(jnp.exp(before), 1)
    zero = jnp.zeros((1, HEADS), BF16)
    wgt[rows : rows + 8] = jnp.concatenate(
        [
            jnp.concatenate([total[:, :HEADS], zero], axis=1),
            jnp.concatenate([zero, total[:, HEADS:]], axis=1),
            hi_lo(heads[7:8], 1),
            jnp.zeros((5, 2 * HEADS), BF16),
        ],
        axis=0,
    )
    slots = [bc_slot(k) for k in range(CONV + 1)]
    taps = [par[0, row : row + 1, cols] for row, cols in slots]
    weights = jnp.concatenate(taps[:CONV], axis=0)
    conved = jnp.concatenate(convolve(small[:, :BC], weights, taps[CONV]), axis=0)
    bc_ref[...] = conved.astype(BF16)
    bt[...] = conved.T[:STATE].astype(BF16)


def local_state(tokens, halo, w_gate_x, w_small, packed):
    rows, depth = tokens.shape
    outs = [
        ((rows, DINNER), BF16),
        ((rows, depth), BF16),
        ((rows, BC), BF16),
        ((rows, HEADS), F32),
        ((rows, HEADS), F32),
        ((8, DINNER), F32),
    ]
    return call(
        state_kernel,
        [tokens, on_chip(halo), w_gate_x, w_small, on_chip(packed)],
        outs + [((DINNER // OWNED, STATE + 8, OWNED), BF16)],
        [
            pltpu.VMEM((rows, depth), BF16),
            pltpu.VMEM((PAD + rows, depth), BF16),
            pltpu.VMEM((2, depth, DINNER), BF16),
            pltpu.VMEM(w_small.shape, BF16),
            *(pltpu.VMEM(shape, dtype) for shape, dtype in outs[:1] + outs[2:]),
            pltpu.VMEM((rows + 8, 2 * HEADS), BF16),
            pltpu.VMEM((STATE, rows), BF16),
            pltpu.SemaphoreType.DMA((4,)),
            pltpu.SemaphoreType.DMA((5 + DINNER // SEND,)),
        ],
        "local_state",
        far=(0, 2, 3),
        far_out=range(6),
        near_out=(6,),
    )


def prepare(bc_ref, dt_ref, cum_ref, scores, left, rowlog, bt, wgt):
    rows = bc_ref.shape[0]
    heads = WIDTH // HEAD_DIM
    bt[...] = bc_ref[...].astype(F32).T[:STATE].astype(BF16)
    for k in range(rows // SUB):
        here = slice(k * SUB, (k + 1) * SUB)
        scores[here] = dot(bc_ref[here, STATE:], bt[:, here])
    cum = cum_ref[...]
    step = dt_ref[...]
    ones = jnp.ones((rows, HEADS), BF16)
    starts, ends = [], []
    before = jnp.zeros((1, HEADS), F32)
    for k in range(rows // SUB):
        starts.append(jnp.broadcast_to(before, (SUB, HEADS)))
        before = cum[(k + 1) * SUB - 1 : (k + 1) * SUB]
        ends.append(jnp.broadcast_to(before, (SUB, HEADS)))
    starts = jnp.concatenate(starts, axis=0)
    ends = jnp.concatenate(ends, axis=0)
    passed = cum - starts
    left[...] = jnp.concatenate(split3(passed * LOG2E) + [ones], axis=1)
    by_row = (jnp.log(jnp.maximum(step, 1e-37)) - passed) * LOG2E
    by_row = jnp.concatenate([p.astype(F32) for p in split3(by_row)] + [cum], axis=1).T
    for g in range(HEADS // heads):
        for p in range(3):
            first = p * HEADS + g * heads
            rowlog[g, p, 0:heads] = by_row[first : first + heads]
    wgt[0:rows] = hi_lo(step * jnp.exp(ends - cum), 1)
    wgt[rows : 2 * rows] = hi_lo(jnp.exp(passed), 1)
    wgt[2 * rows : 3 * rows] = hi_lo(jnp.exp(cum), 1)


def intra_kernel(
    first_group, xc_ref, tok_ref, w_ref, bc_ref, dt_ref, cum_ref, skip_ref,
    own_ref, scale_ref, scores, left, rowlog, bt, wgt,
):
    rows = xc_ref.shape[0]
    blocks = rows // SUB
    heads = WIDTH // HEAD_DIM
    together = xc_ref.shape[1] // WIDTH

    @pl.when(pl.program_id(0) == 0)
    def _():
        prepare(bc_ref, dt_ref, cum_ref, scores, left, rowlog, bt, wgt)

    r = lax.broadcasted_iota(jnp.int32, (SUB, heads * SUB), 0)
    c = lax.broadcasted_iota(jnp.int32, (SUB, heads * SUB), 1)
    causal = place(r) >= place(c % SUB)
    low = lax.broadcasted_iota(jnp.int32, (1, 128), 1) < HEAD_DIM
    pr = lax.broadcasted_iota(jnp.int32, (3 * HEADS, heads * SUB), 0)
    pc = lax.broadcasted_iota(jnp.int32, (3 * HEADS, heads * SUB), 1)
    for i in range(together):
        g = first_group + pl.program_id(0) * together + i
        mine = slice(i * WIDTH, (i + 1) * WIDTH)
        expanded = dot(wgt[...], one_hot(g * WIDTH, WIDTH))
        pick = (pr % HEADS == g * heads + pc // SUB).astype(F32).astype(BF16)
        skip = skip_ref[2:3, mine]
        w = half_lanes(w_ref[:, 2 * i * WIDTH : 2 * (i + 1) * WIDTH], 0)
        z = dot(tok_ref[...], w).astype(BF16).astype(F32)
        state = jnp.zeros((STATE, WIDTH), F32)
        for k in range(blocks):
            here = slice(k * SUB, (k + 1) * SUB)
            xc = xc_ref[here, mine]
            late = jnp.concatenate(
                [
                    jnp.concatenate(
                        [rowlog[g, p, h : h + 1, here] for h in range(heads)], axis=1
                    )
                    for p in range(3)
                ]
                + [jnp.zeros((HEADS - 3, heads * SUB), F32)],
                axis=0,
            ).astype(BF16)
            gaps = dot(left[here], jnp.concatenate([pick, late], axis=0))
            decay = jnp.exp2(jnp.where(causal, gaps, -jnp.inf))
            score = scores[here]
            pieces = []
            for pair in range(heads // 2):
                both = [
                    (score * decay[:, h * SUB : (h + 1) * SUB]).astype(BF16)
                    for h in (2 * pair, 2 * pair + 1)
                ]
                x = xc[:, pair * 128 : pair * 128 + 128]
                none = jnp.zeros_like(x)
                right = jnp.concatenate(
                    [jnp.where(low, x, none), jnp.where(low, none, x)], axis=0
                )
                pieces.append(dot(jnp.concatenate(both, axis=1), right))
            y = jnp.concatenate(pieces, axis=1)
            xf = xc.astype(F32)
            grow = expanded[rows + k * SUB : rows + (k + 1) * SUB]
            if k > 0:
                y = y + grow * dot(bc_ref[here, STATE:], state.astype(BF16))
            if k + 1 < blocks:
                shrink = expanded[here]
                fresh = dot(bt[:, here], (xf * shrink).astype(BF16))
                state = state * grow[SUB - 1 : SUB] + fresh
            gate = silu(z[here])
            own_ref[here, mine] = ((y + skip * xf) * gate).astype(own_ref.dtype)
            full = expanded[2 * rows + k * SUB : 2 * rows + (k + 1) * SUB]
            scale_ref[here, mine] = (full * gate).astype(BF16)


def intra(first_group, groups, xc, tokens, w_gate_x, bc, dt, cum, skips):
    rows, depth = tokens.shape
    together = TOGETHER
    group = first_group // together
    wide = together * WIDTH

    def whole(a):
        return pl.BlockSpec(a.shape, lambda i: (0,) * a.ndim)

    return pl.pallas_call(
        functools.partial(intra_kernel, first_group),
        grid=(groups // together,),
        in_specs=[
            pl.BlockSpec((rows, wide), lambda i: (0, i + group)),
            whole(tokens),
            pl.BlockSpec((depth, 2 * wide), lambda i: (0, i + group)),
            whole(bc),
            whole(dt),
            whole(cum),
            pl.BlockSpec((8, wide), lambda i: (0, i + group)),
        ],
        out_specs=[
            pl.BlockSpec((rows, wide), lambda i: (0, i)),
            pl.BlockSpec((rows, wide), lambda i: (0, i)),
        ],
        out_shape=[
            jax.ShapeDtypeStruct((rows, groups * WIDTH), OWN),
            jax.ShapeDtypeStruct((rows, groups * WIDTH), BF16),
        ],
        scratch_shapes=[
            pltpu.VMEM((rows, SUB), F32),
            pltpu.VMEM((rows, 4 * HEADS), BF16),
            pltpu.VMEM((DINNER // WIDTH, 3, 8, rows), F32),
            pltpu.VMEM((STATE, rows), BF16),
            pltpu.VMEM((3 * rows, 2 * HEADS), BF16),
        ],
        compiler_params=params(),
        name="intra",
    )(xc, tokens, w_gate_x, bc, dt, cum, skips)


def through(state, slab):
    slab = slab.astype(F32)
    total = slab[STATE : STATE + 1] + slab[STATE + 1 : STATE + 2]
    return state * total + slab[0:STATE], total


def fold_kernel(in_ref, out_ref):
    state = jnp.zeros((STATE, OWNED), F32)
    whole = jnp.ones((1, OWNED), F32)
    for q in range(in_ref.shape[0]):
        state, total = through(state, in_ref[q])
        whole = whole * total
    hi = whole.astype(BF16).astype(F32)
    row = lax.broadcasted_iota(jnp.int32, (8, OWNED), 0)
    tail = jnp.where(row == 0, hi, jnp.where(row == 1, whole - hi, 0.0))
    state = state.astype(BF16)
    tail = tail.astype(BF16)
    for b in range(out_ref.shape[0]):
        out_ref[b, 0:STATE] = state
        out_ref[b, STATE:] = tail


def fold(near, blocks):
    out = ((blocks, *near.shape[1:]), BF16)
    return call(fold_kernel, [on_chip(near)], [out], [], "fold", near_out=(0,))[0]


def unfold_kernel(me_ref, near_ref, far_ref, out_ref):
    def earlier(b, state):
        return through(state, far_ref[b])[0]

    state = jnp.zeros((STATE, OWNED), F32)
    state = lax.fori_loop(0, me_ref[0], earlier, state)
    for q in range(near_ref.shape[0]):
        out_ref[q] = state.astype(BF16)
        state, _ = through(state, near_ref[q])


def unfold(me, near, far):
    count = near.shape[0]
    out = ((count, STATE, OWNED), BF16)
    operands = [on_chip(near), on_chip(far)]
    return call(
        unfold_kernel, operands, [out], [], "unfold", near_out=(0,), scalars=(me,)
    )[0]


def finish_kernel(parts, bc_hbm, in_ref, gain_hbm, w_hbm, *refs):
    own_hbm, scale_hbm = refs[:parts], refs[parts : 2 * parts]
    out_hbm, bc_ref, gain_ref, w_ref, own_all, scale_all = refs[2 * parts : 2 * parts + 6]
    acc, out_ref, in_sem, w_sem = refs[2 * parts + 6 :]
    rows = bc_hbm.shape[0]
    span = DINNER // CHUNKS
    small = [
        start(bc_hbm, bc_ref, w_sem.at[CHUNKS + rows // SUB]),
        start(gain_hbm, gain_ref, w_sem.at[CHUNKS + rows // SUB + 1]),
    ]
    fetches, fetch_w = [], []
    for k in range(CHUNKS):
        fetches.append([])
        at = 0
        for p in range(parts):
            low, high = max(at, k * span), min(at + own_hbm[p].shape[1], (k + 1) * span)
            if low < high:
                there, here = slice(low - at, high - at), slice(low, high)
                pairs = ((own_hbm[p], own_all), (scale_hbm[p], scale_all))
                for i, (hbm, ref) in enumerate(pairs):
                    source, target = hbm.at[:, there], ref.at[:, here]
                    fetches[k].append(start(source, target, in_sem.at[k, p, i]))
            at += own_hbm[p].shape[1]
        part = slice(k * span, (k + 1) * span)
        fetch_w.append(start(w_hbm.at[part], w_ref.at[part], w_sem.at[k]))

    def gate(k, total):
        sides = []
        for g in range(k * span // WIDTH, (k + 1) * span // WIDTH):
            cols = slice(g * WIDTH, (g + 1) * WIDTH)
            slabs = [in_ref[2 * g], in_ref[2 * g + 1]]
            carried = dot(bc_ref[:, STATE:], jnp.concatenate(slabs, axis=1))
            scale = scale_all[:, cols].astype(F32)
            gated = own_all[:, cols].astype(F32) + scale * carried
            gated = gated.astype(BF16).astype(F32)
            square = gated * gated
            total = total + square[:, :128] + square[:, 128:]
            sides.append((gated * gain_ref[0:1, cols]).astype(BF16))
        return jnp.concatenate(sides, axis=1), total

    total = jnp.zeros((rows, 128), F32)
    for copy in small:
        copy.wait()
    for copy in fetches[0]:
        copy.wait()
    side, total = gate(0, total)
    for copy in fetches[1] + fetch_w[:1]:
        copy.wait()
    acc[...] = dot(side, w_ref[:span])
    side, total = gate(1, total)
    fetch_w[1].wait()
    product = acc[...] + dot(side, w_ref[span:])
    mean = jnp.sum(total, axis=1, keepdims=True) * (1.0 / DINNER)
    product = (product * lax.rsqrt(mean + EPSILON)).astype(BF16)
    order = reorder(back=True)
    sends = []
    for k in range(rows // SUB):
        here = slice(k * SUB, (k + 1) * SUB)
        out_ref[here] = dot(order, product[here]).astype(BF16)
        sends.append(start(out_ref.at[here], out_hbm.at[here], w_sem.at[CHUNKS + k]))
    for copy in sends:
        copy.wait()


def finish(bc, incoming, owns, scales, gain, w_out):
    rows = bc.shape[0]
    columns = w_out.shape[1]
    parts = len(owns)
    return call(
        functools.partial(finish_kernel, parts),
        [bc, on_chip(incoming), gain, w_out, *owns, *scales],
        [((rows, columns), BF16)],
        [
            pltpu.VMEM(bc.shape, BF16),
            pltpu.VMEM(gain.shape, F32),
            pltpu.VMEM(w_out.shape, BF16),
            pltpu.VMEM((rows, DINNER), OWN),
            pltpu.VMEM((rows, DINNER), BF16),
            pltpu.VMEM((rows, columns), F32),
            pltpu.VMEM((rows, columns), BF16),
            pltpu.SemaphoreType.DMA((CHUNKS, parts, 2)),
            pltpu.SemaphoreType.DMA((CHUNKS + rows // SUB + 2,)),
        ],
        "finish",
        far=(0, *range(2, 4 + 2 * parts)),
        far_out=(0,),
    )[0]


def on_device(
    tokens, w_gate_x, w_bc_dt, conv_x_weight, conv_x_bias, conv_bc_weight,
    conv_bc_bias, dt_bias, a_log, skip_d, norm_gain, w_out,
):
    n = lax.axis_size("head")
    blocks = lax.axis_size(FAR)
    devices = blocks * lax.axis_size(NEAR)
    my_block = lax.axis_index(FAR)[None]
    small = [conv_x_weight, conv_x_bias, dt_bias, a_log, skip_d]
    small += [conv_bc_weight, conv_bc_bias, norm_gain]
    packed, tail, gain = pack(small, tokens, n)
    packed = lax.all_to_all(packed, "head", 0, 0, tiled=True)
    halo = lax.ppermute(tail, BOTH, [(i, i + 1) for i in range(devices - 1)])
    xc, mine, bc, dt, cum, skips, slabs = local_state(
        tokens, halo, w_gate_x, w_bc_dt.T, packed
    )
    near = lax.all_to_all(slabs, NEAR, 0, 0, tiled=True)
    rest = (bc, dt, cum, skips)
    first, second, third = SPLIT
    own0, scale0 = intra(0, first, xc, mine, w_gate_x, *rest)
    near, own0 = lax.optimization_barrier((near, own0))
    copies = fold(near, blocks)
    far = lax.all_to_all(copies, FAR, 0, 0, tiled=True)
    xc, copies = lax.optimization_barrier((xc, copies))
    own1, scale1 = intra(first, second, xc, mine, w_gate_x, *rest)
    far, own1 = lax.optimization_barrier((far, own1))
    incoming = unfold(my_block, near, far)
    back = lax.all_to_all(incoming, NEAR, 0, 0, tiled=True)
    xc, incoming = lax.optimization_barrier((xc, incoming))
    own2, scale2 = intra(first + second, third, xc, mine, w_gate_x, *rest)
    owns, scales = (own0, own1, own2), (scale0, scale1, scale2)
    return finish(bc, back, owns, scales, gain, w_out)


def solution(mesh):
    seq, head = mesh.devices.shape
    split = Mesh(mesh.devices.reshape(seq // 4, 2, 2, head), BOTH)
    return jax.shard_map(
        on_device,
        mesh=split,
        in_specs=(
            P(BOTH, None),
            P(),
            P(),
            P(None, "head"),
            P("head"),
            P(),
            P(),
            P("head"),
            P("head"),
            P("head"),
            P(),
            P(),
        ),
        out_specs=P(BOTH, None),
        check_vma=False,
    )
```
